32 devices in a mesh: dp: 8 (over y, x, core), seq: 4 (over z).
Axes of the slice: x: 2, y: 2, z: 4, core: 2. Of those that a mesh axis runs over, the one named last changes fastest.
Arguments:
- tokens: bfloat16 [16, 1024, 768], P('dp', 'seq'), may hold values from -6 to 6
- chars: bfloat16 [16, 1024, 4, 768], P('dp', 'seq'), may hold values from -6 to 6
- char_counts: int32 [16, 1024], P('dp', 'seq'), may hold values from 1 to 4
- lengths: int32 [16], replicated, may hold values from 128 to 1024, as said below
- perm: int32 [2, 8], replicated, may hold values from 0 to 7, as said below
- token_out_cotangent: bfloat16 [16, 1024, 768], P('dp', 'seq'), may hold values from -6 to 6
- char_out_cotangent: bfloat16 [16, 1024, 768], P('dp', 'seq'), may hold values from -6 to 6
- w_qkv: float32 [768, 2304], P('dp'), may hold values from -0.21875 to 0.21875
- b_qv: float32 [1536], P('dp'), may hold values from -1.75 to 1.75
- w_out: float32 [768, 768], P('dp'), may hold values from -0.875 to 0.875
- w_in: float32 [768, 3072], P('dp'), may hold values from -0.21875 to 0.21875
- b_in: float32 [3072], P('dp'), may hold values from -1.75 to 1.75
- w_back: float32 [3072, 768], P('dp'), may hold values from -0.109375 to 0.109375
- gru_x: float32 [768, 2304], P('dp'), may hold values from -0.21875 to 0.21875
- gru_h: float32 [384, 2304], P('dp'), may hold values from -0.3125 to 0.3125
- gru_bias: float32 [2304, 2], P('dp'), may hold values from -1.75 to 1.75
- blend_w: float32 [768, 1536], P('dp'), may hold values from -0.21875 to 0.21875
- conv_w: float32 [4608, 1536], P('dp'), may hold values from -0.09375 to 0.09375
- conv_b: float32 [1536], P('dp'), may hold values from -1.75 to 1.75
- norm_gain: float32 [768, 4], P('dp'), may hold values from 0.1 to 1.9
- norm_bias: float32 [768, 4], P('dp'), may hold values from -1.75 to 1.75
- row_bias: float32 [768, 4], P('dp'), may hold values from -1.75 to 1.75
Outputs:
- token_out: bfloat16 [16, 1024, 768], P('dp', 'seq')
- char_out: bfloat16 [16, 1024, 768], P('dp', 'seq')
- tokens_grad: bfloat16 [16, 1024, 768], P('dp', 'seq')
- chars_grad: bfloat16 [16, 1024, 4, 768], P('dp', 'seq')
- w_qkv_grad: float32 [768, 2304], P('dp')
- b_qv_grad: float32 [1536], P('dp')
- w_out_grad: float32 [768, 768], P('dp')
- w_in_grad: float32 [768, 3072], P('dp')
- b_in_grad: float32 [3072], P('dp')
- w_back_grad: float32 [3072, 768], P('dp')
- gru_x_grad: float32 [768, 2304], P('dp')
- gru_h_grad: float32 [384, 2304], P('dp')
- gru_bias_grad: float32 [2304, 2], P('dp')
- blend_w_grad: float32 [768, 1536], P('dp')
- conv_w_grad: float32 [4608, 1536], P('dp')
- conv_b_grad: float32 [1536], P('dp')
- norm_gain_grad: float32 [768, 4], P('dp')
- norm_bias_grad: float32 [768, 4], P('dp')
- row_bias_grad: float32 [768, 4], P('dp')
The draws below stay inside these ranges and needn't reach their ends.
Inputs may be any that keep to these rules, and one draw needn't show every extreme that they name: Positions j < lengths[s] of sequence s are valid keys; the first sequence is full and the second has exactly 128 valid positions. perm[m, g] is g xor perm[m, 0] (bitwise) for every group g; perm[m, 0] is never 0, and differs from one micro-batch to another. `char_counts`: characters of each token; its other rows of chars are unused.
All inputs are finite; a program needn't handle non-finite values.
Results may differ from the reference program's by a relative error of at most 0.019.
The reference program's roundings to bfloat16 on the way count: a program that leaves them out, or rounds other values in their place, can miss the bound.
Values may be sent and summed in bfloat16 or wider, within the bound.
A program may use at most 384 MiB of HBM per device.

```python
import jax
import jax.numpy as jnp
from jax import lax

D = 768
HEADS = 12
HEAD = 64
FF = 3072
H = 384
NCHAR = 4
MB = 2
L = 1024
GROUPS = 8
SEQS = 16


def draw_lengths(key, part):
    drawn = jax.random.randint(key, (SEQS,), L // 8, L + 1, dtype=jnp.int32)
    return drawn.at[0].set(L).at[1].set(L // 8)


def draw_perm(key, part):
    choices_all = jnp.arange(1, GROUPS, dtype=jnp.int32)
    shuffled = jax.random.permutation(jax.random.fold_in(key, 7), choices_all)
    masks = shuffled[:MB].astype(jnp.int32)
    group_ids = jnp.arange(GROUPS, dtype=jnp.int32)
    return jnp.bitwise_xor(group_ids[None, :], masks[:, None]).astype(jnp.int32)


def set_ends(values, own_key, smallest, largest):
    shape = values.shape
    place = [jax.random.randint(jax.random.fold_in(own_key, axis), (), 0, shape[axis]) for axis in range(len(shape))]
    values = values.at[tuple(place)].set(smallest)
    longest = shape.index(max(shape))
    place[longest] = (place[longest] + 1) % shape[longest]
    return values.at[tuple(place)].set(largest)


def block_levels(key, extent, cuts, smallest, largest):
    level = 1.0
    for axis_at, shards_of in cuts:
        heights = jax.random.uniform(jax.random.fold_in(jax.random.fold_in(key, 6), axis_at), (shards_of,), jnp.float32, smallest / len(cuts), largest / len(cuts))
        level = level * jnp.repeat(jnp.exp(heights), extent[axis_at] // shards_of).reshape((-1,) + (1,) * (len(extent) - 1 - axis_at))
    return level


def centred(own_key, dims, deviation, limit, shards=(), kind=jnp.bfloat16):
    loudness = block_levels(own_key, dims, shards, -0.22, 0.18) if shards else 1.0
    result = jax.random.normal(own_key, dims, jnp.float32) * deviation * loudness
    return jnp.minimum(jnp.maximum(result, -limit), limit).astype(kind)


def setup_inputs(seed: int = 0) -> dict:
    streams_of = jax.random.split(jax.random.key(seed), 23)
    tokens = centred(streams_of[0], (SEQS, L, D), 1.0, 6.0, ((0, 8), (1, 4)))
    chars = centred(streams_of[1], (SEQS, L, NCHAR, D), 1.0, 6.0, ((0, 8), (1, 4)))
    char_counts = set_ends(jax.random.randint(streams_of[2], (SEQS, L), 1, NCHAR + 1), jax.random.fold_in(streams_of[2], 1), 1, NCHAR).astype(jnp.int32)
    lengths = draw_lengths(jax.random.fold_in(streams_of[22], 71), 0)
    perm = draw_perm(jax.random.fold_in(streams_of[22], 71), 0)
    token_out_cotangent = centred(streams_of[5], (SEQS, L, D), 1.0, 6.0, ((0, 8), (1, 4)))
    char_out_cotangent = centred(streams_of[6], (SEQS, L, D), 1.0, 6.0, ((0, 8), (1, 4)))
    w_qkv = centred(streams_of[7], (D, 3 * D), D ** -0.5, 0.21875, ((0, 8),), jnp.float32)
    b_qv = centred(streams_of[8], (2 * D,), 0.3, 1.75, ((0, 8),), jnp.float32)
    w_out = centred(streams_of[9], (D, D), (D // 16) ** -0.5, 0.875, ((0, 8),), jnp.float32)
    w_in = centred(streams_of[10], (D, FF), D ** -0.5, 0.21875, ((0, 8),), jnp.float32)
    b_in = centred(streams_of[11], (FF,), 0.3, 1.75, ((0, 8),), jnp.float32)
    w_back = centred(streams_of[12], (FF, D), FF ** -0.5, 0.109375, ((0, 8),), jnp.float32)
    gru_x = centred(streams_of[13], (D, 6 * H), D ** -0.5, 0.21875, ((0, 8),), jnp.float32)
    gru_h = centred(streams_of[14], (H, 6 * H), H ** -0.5, 0.3125, ((0, 8),), jnp.float32)
    gru_bias = centred(streams_of[15], (6 * H, 2), 0.3, 1.75, ((0, 8),), jnp.float32)
    blend_w = centred(streams_of[16], (D, 2 * D), D ** -0.5, 0.21875, ((0, 8),), jnp.float32)
    conv_w = centred(streams_of[17], (6 * D, 2 * D), (6 * D) ** -0.5, 0.09375, ((0, 8),), jnp.float32)
    conv_b = centred(streams_of[18], (2 * D,), 0.3, 1.75, ((0, 8),), jnp.float32)
    norm_gain = jnp.clip(1.0 + 0.18 * jax.random.normal(streams_of[19], (D, 4), jnp.float32), 0.1, 1.9)
    norm_bias = centred(streams_of[20], (D, 4), 0.3, 1.75, ((0, 8),), jnp.float32)
    row_bias = centred(streams_of[21], (D, 4), 0.3, 1.75, ((0, 8),), jnp.float32)
    return {"tokens": tokens, "chars": chars, "char_counts": char_counts, "lengths": lengths, "perm": perm, "token_out_cotangent": token_out_cotangent, "char_out_cotangent": char_out_cotangent, "w_qkv": w_qkv, "b_qv": b_qv, "w_out": w_out, "w_in": w_in, "b_in": b_in, "w_back": w_back, "gru_x": gru_x, "gru_h": gru_h, "gru_bias": gru_bias, "blend_w": blend_w, "conv_w": conv_w, "conv_b": conv_b, "norm_gain": norm_gain, "norm_bias": norm_bias, "row_bias": row_bias}


@jax.custom_vjp
def low(v):
    return lax.optimization_barrier(v.astype(jnp.bfloat16)).astype(jnp.float32)

@jax.custom_vjp
def low_back(v):
    return v

def low_keep(v):
    return (low(v), None)

def low_pass(kept, grad):
    return (grad,)

def back_keep(v):
    return (v, None)

def back_low(kept, grad):
    return (low(grad),)
low.defvjp(low_keep, low_pass)
low_back.defvjp(back_keep, back_low)

def both_ways(values):
    return low_back(low(values))

def product(left, right):
    return jnp.dot(left, right, precision=lax.Precision.HIGHEST)

def norm_rows(values, gain, shift):
    center = values - lax.optimization_barrier(jnp.mean(values, axis=-1, keepdims=True))
    spread = lax.optimization_barrier(jnp.mean(center * center, axis=-1, keepdims=True))
    return center * lax.rsqrt(spread + 1e-06) * gain + shift

def gelu_exact(values):
    return jax.nn.gelu(values, approximate=False)

def gru_cell(live, gates, recur, state):
    width = state.shape[-1]
    reset = jax.nn.sigmoid(gates[:, :width] + recur[:, :width])
    update = jax.nn.sigmoid(gates[:, width:2 * width] + recur[:, width:2 * width])
    fresh = jnp.tanh(gates[:, 2 * width:] + reset * recur[:, 2 * width:])
    return jnp.where(live, (1.0 - update) * fresh + update * state, state)

def layer(masters, tokens_row, chars_row, counts_row, length_row):
    w_qkv, b_qv, w_out, w_in, b_in, w_back, gru_x, gru_h, gru_bias, blend_w, conv_w, conv_b, norm_gain, norm_bias, row_bias = [low(piece) for piece in masters]
    positions, width = tokens_row.shape
    three = 3 * H
    project = product(tokens_row, w_qkv) + jnp.concatenate([b_qv[:width], jnp.zeros((width,), jnp.float32), b_qv[width:]])
    query = both_ways(project[:, :width])
    keys = both_ways(project[:, width:2 * width])
    values = both_ways(project[:, 2 * width:])
    raw = jnp.einsum('qhd,khd->hqk', query.reshape(positions, HEADS, HEAD), keys.reshape(positions, HEADS, HEAD), precision=lax.Precision.HIGHEST)
    valid = jnp.arange(positions, dtype=jnp.int32) < length_row
    scores = low_back(jnp.where(valid[None, None, :], raw * HEAD ** (-0.5), -1e+30))
    top = lax.optimization_barrier(jnp.max(scores, axis=-1, keepdims=True))
    raised = jnp.exp(scores - top)
    probs = raised / lax.optimization_barrier(jnp.sum(raised, axis=-1, keepdims=True))
    context = both_ways(jnp.einsum('hqk,khd->qhd', low(probs), values.reshape(positions, HEADS, HEAD), precision=lax.Precision.HIGHEST).reshape(positions, width))
    summed_first = tokens_row + low_back(product(context, w_out) + row_bias[:, 0])
    hidden1 = norm_rows(summed_first, norm_gain[:, 0], norm_bias[:, 0])
    inner = low_back(product(low(hidden1), w_in) + b_in)
    activated = low(gelu_exact(inner))
    summed_second = hidden1 + low_back(product(activated, w_back) + row_bias[:, 1])
    hidden2 = norm_rows(summed_second, norm_gain[:, 1], norm_bias[:, 1])
    gates = low_back(product(chars_row.reshape(positions * NCHAR, width), gru_x) + gru_bias[:, 0]).reshape(positions, NCHAR, 2 * three)
    ahead = jnp.zeros((positions, H), jnp.float32)
    for position in range(NCHAR):
        live = (position < counts_row)[:, None]
        recur = low_back(product(low(ahead), gru_h[:, :three]) + gru_bias[:three, 1])
        ahead = gru_cell(live, gates[:, position, :three], recur, ahead)
    behind = jnp.zeros((positions, H), jnp.float32)
    for position in reversed(range(NCHAR)):
        live = (position < counts_row)[:, None]
        recur = low_back(product(low(behind), gru_h[:, three:]) + gru_bias[three:, 1])
        behind = gru_cell(live, gates[:, position, three:], recur, behind)
    char_state = jnp.concatenate([ahead, behind], axis=-1)
    token_side = product(low(hidden2), blend_w[:, :width]) + row_bias[:, 2]
    char_side = product(low(char_state), blend_w[:, width:]) + row_bias[:, 3]
    joined = both_ways(jnp.concatenate([token_side, char_side], axis=-1))
    padded = jnp.pad(joined, ((1, 1), (0, 0)))
    stacked = jnp.concatenate([padded[:-2], padded[1:-1], padded[2:]], axis=-1)
    mixed = low_back(product(stacked, conv_w) + conv_b)
    lifted = gelu_exact(mixed)
    token_out = norm_rows(hidden2 + lifted[:, :width], norm_gain[:, 2], norm_bias[:, 2])
    char_out = norm_rows(char_state + lifted[:, width:], norm_gain[:, 3], norm_bias[:, 3])
    return (token_out, char_out)

def reference(tokens, chars, char_counts, lengths, perm, token_out_cotangent, char_out_cotangent, w_qkv, b_qv, w_out, w_in, b_in, w_back, gru_x, gru_h, gru_bias, blend_w, conv_w, conv_b, norm_gain, norm_bias, row_bias):
    masters = (w_qkv, b_qv, w_out, w_in, b_in, w_back, gru_x, gru_h, gru_bias, blend_w, conv_w, conv_b, norm_gain, norm_bias, row_bias)
    group_ids = jnp.arange(GROUPS, dtype=jnp.int32)
    micro_ids = jnp.arange(MB, dtype=jnp.int32)
    matches = (perm[:, :, None] == group_ids[None, None, :]).astype(jnp.int32)
    inverse = lax.optimization_barrier(jnp.sum(group_ids[None, :, None] * matches, axis=1)).astype(jnp.int32)
    source_rows = (inverse.T * MB + micro_ids[None, :]).reshape(-1).astype(jnp.int32)
    placed_rows = (perm.T * MB + micro_ids[None, :]).reshape(-1).astype(jnp.int32)
    tokens_placed = jnp.take(tokens, source_rows, axis=0)
    chars_placed = jnp.take(chars, source_rows, axis=0)
    counts_placed = jnp.take(char_counts, source_rows, axis=0)
    lengths_placed = jnp.take(lengths, source_rows, axis=0)

    def one_sequence(totals, item):
        tokens_row, chars_row, counts_row, length_row, token_cot, char_cot = item

        def forward(params, tokens_value, chars_value):
            return layer(params, tokens_value, chars_value, counts_row, length_row)
        outputs, pullback = jax.vjp(forward, masters, tokens_row.astype(jnp.float32), chars_row.astype(jnp.float32))
        param_grads, tokens_back, chars_back = pullback((token_cot.astype(jnp.float32), char_cot.astype(jnp.float32)))
        totals = jax.tree.map(jnp.add, totals, param_grads)
        return (totals, (outputs[0].astype(jnp.bfloat16), outputs[1].astype(jnp.bfloat16), tokens_back.astype(jnp.bfloat16), chars_back.astype(jnp.bfloat16)))
    start = jax.tree.map(jnp.zeros_like, masters)
    totals, rows_out = lax.scan(one_sequence, start, (tokens_placed, chars_placed, counts_placed, lengths_placed, token_out_cotangent, char_out_cotangent))
    tokens_grad = jnp.take(rows_out[2], placed_rows, axis=0)
    chars_grad = jnp.take(rows_out[3], placed_rows, axis=0)
    return (rows_out[0], rows_out[1], tokens_grad, chars_grad, totals[0], totals[1], totals[2], totals[3], totals[4], totals[5], totals[6], totals[7], totals[8], totals[9], totals[10], totals[11], totals[12], totals[13], totals[14])
```

```python
from functools import partial

import jax
import jax.numpy as jnp
from jax import lax
from jax.experimental import pallas as pl
from jax.experimental.pallas import tpu as pltpu
from jax.sharding import PartitionSpec as P

HEAD = 64
H = 384
NCHAR = 4
WIDE = 768
BF = jnp.bfloat16
F32 = jnp.float32


def dot_plain(left, right):
    return jnp.dot(left, right, preferred_element_type=F32)


def dot_left(left, right):
    return lax.dot_general(left, right, (((0,), (0,)), ((), ())), preferred_element_type=F32)


def dot_right(left, right):
    return lax.dot_general(left, right, (((1,), (1,)), ((), ())), preferred_element_type=F32)


def column_sum(values):
    return jnp.sum(values.astype(F32), axis=0)


def norm_rows(values, gain, shift):
    center = values - jnp.mean(values, axis=-1, keepdims=True)
    spread = jnp.mean(center * center, axis=-1, keepdims=True)
    rstd = lax.rsqrt(spread + 1e-06)
    return center * rstd * gain + shift


def norm_back(values, gain, grad):
    center = values - jnp.mean(values, axis=-1, keepdims=True)
    spread = jnp.mean(center * center, axis=-1, keepdims=True)
    rstd = lax.rsqrt(spread + 1e-06)
    hat = center * rstd
    lead = grad * gain
    back = rstd * (
        lead
        - jnp.mean(lead, axis=-1, keepdims=True)
        - hat * jnp.mean(lead * hat, axis=-1, keepdims=True)
    )
    return back, jnp.sum(grad * hat, axis=0), jnp.sum(grad, axis=0)


def gelu_exact(values):
    return jax.nn.gelu(values, approximate=False)


def gelu_slope(values):
    cdf = 0.5 * (1.0 + lax.erf(values * (0.5**0.5)))
    pdf = jnp.exp(-0.5 * values * values) * 0.3989422804014327
    return cdf + values * pdf


def gru_cell(live, gates, recur, state):
    width = state.shape[-1]
    reset = jax.nn.sigmoid(gates[:, :width] + recur[:, :width])
    update = jax.nn.sigmoid(gates[:, width : 2 * width] + recur[:, width : 2 * width])
    fresh = jnp.tanh(gates[:, 2 * width :] + reset * recur[:, 2 * width :])
    return jnp.where(live, (1.0 - update) * fresh + update * state, state)


def attention_forward_kernel(per, len_ref, qkv_ref, out_ref):
    block = pl.program_id(1)
    length = len_ref[pl.program_id(0)]
    span = per * HEAD
    total = qkv_ref.shape[0] * qkv_ref.shape[2]
    rows = qkv_ref.shape[2]
    q_all = qkv_ref[block, 0, :, :span]
    k_all = qkv_ref[:, 0, :, span : 2 * span].reshape(total, span)
    v_all = qkv_ref[:, 0, :, 2 * span :].reshape(total, span)
    valid = lax.broadcasted_iota(jnp.int32, (rows, total), 1) < length
    pieces = []
    for j in range(per):
        part = slice(j * HEAD, (j + 1) * HEAD)
        scores = dot_right(q_all[:, part], k_all[:, part]) * HEAD ** (-0.5)
        scores = jnp.where(valid, scores, -1e30)
        raised = jnp.exp(scores - jnp.max(scores, axis=-1, keepdims=True))
        probs = (raised / jnp.sum(raised, axis=-1, keepdims=True)).astype(BF)
        pieces.append(dot_plain(probs, v_all[:, part]))
    out_ref[0, 0] = jnp.concatenate(pieces, axis=-1).astype(BF)


def attention_forward(qkv, lengths, per):
    seqs, rows = qkv.shape[1], qkv.shape[2]
    parts = qkv.shape[0]
    span = per * HEAD
    return pl.pallas_call(
        partial(attention_forward_kernel, per),
        grid_spec=pltpu.PrefetchScalarGridSpec(
            num_scalar_prefetch=1,
            grid=(seqs, parts),
            in_specs=[pl.BlockSpec((parts, 1, rows, 3 * span), lambda m, b, n: (0, m, 0, 0))],
            out_specs=pl.BlockSpec((1, 1, rows, span), lambda m, b, n: (b, m, 0, 0)),
        ),
        out_shape=jax.ShapeDtypeStruct((parts, seqs, rows, span), BF),
        name="attend_forward",
    )(lengths, qkv)


def attention_backward_kernel(per, len_ref, qkv_ref, grad_ref, out_ref, key_acc, value_acc):
    block = pl.program_id(1)
    length = len_ref[pl.program_id(0)]
    span = per * HEAD
    parts, rows = qkv_ref.shape[0], qkv_ref.shape[2]
    total = parts * rows
    scale = HEAD ** (-0.5)

    @pl.when(block == 0)
    def _():
        key_acc[...] = jnp.zeros_like(key_acc)
        value_acc[...] = jnp.zeros_like(value_acc)

    q_all = qkv_ref[block, 0, :, :span]
    g_all = grad_ref[block, 0]
    k_all = qkv_ref[:, 0, :, span : 2 * span].reshape(total, span)
    v_all = qkv_ref[:, 0, :, 2 * span :].reshape(total, span)
    valid = lax.broadcasted_iota(jnp.int32, (total, rows), 0) < length
    q_pieces, k_pieces, v_pieces = [], [], []
    for j in range(per):
        part = slice(j * HEAD, (j + 1) * HEAD)
        q, g, k, v = q_all[:, part], g_all[:, part], k_all[:, part], v_all[:, part]
        scores = jnp.where(valid, dot_right(k, q) * scale, -1e30)
        raised = jnp.exp(scores - jnp.max(scores, axis=0, keepdims=True))
        probs = raised / jnp.sum(raised, axis=0, keepdims=True)
        d_probs = dot_right(v, g)
        delta = jnp.sum(d_probs * probs, axis=0, keepdims=True)
        d_scores = (probs * (d_probs - delta)).astype(BF)
        q_pieces.append(dot_left(d_scores, k) * scale)
        k_pieces.append(dot_plain(d_scores, q) * scale)
        v_pieces.append(dot_plain(probs.astype(BF), g))
    out_ref[block, 0, :, :span] = jnp.concatenate(q_pieces, axis=-1).astype(BF)
    key_acc[...] += jnp.concatenate(k_pieces, axis=-1)
    value_acc[...] += jnp.concatenate(v_pieces, axis=-1)

    @pl.when(block == parts - 1)
    def _():
        out_ref[:, 0, :, span : 2 * span] = key_acc[...].astype(BF).reshape(parts, rows, span)
        out_ref[:, 0, :, 2 * span :] = value_acc[...].astype(BF).reshape(parts, rows, span)


def attention_backward(qkv, grads, lengths, per):
    parts, seqs, rows, _ = qkv.shape
    span = per * HEAD
    return pl.pallas_call(
        partial(attention_backward_kernel, per),
        grid_spec=pltpu.PrefetchScalarGridSpec(
            num_scalar_prefetch=1,
            grid=(seqs, parts),
            in_specs=[
                pl.BlockSpec((parts, 1, rows, 3 * span), lambda m, b, n: (0, m, 0, 0)),
                pl.BlockSpec((parts, 1, rows, span), lambda m, b, n: (0, m, 0, 0)),
            ],
            out_specs=pl.BlockSpec((parts, 1, rows, 3 * span), lambda m, b, n: (0, m, 0, 0)),
            scratch_shapes=[
                pltpu.VMEM((parts * rows, span), F32),
                pltpu.VMEM((parts * rows, span), F32),
            ],
        ),
        out_shape=jax.ShapeDtypeStruct(qkv.shape, BF),
        name="attend_backward",
    )(lengths, qkv, grads)


def exchange(blocks):
    return lax.all_to_all(blocks, "seq", split_axis=0, concat_axis=0)


def relocate(masks, value):
    levels = lax.axis_size("dp").bit_length() - 1
    for bit in range(levels):
        apart = 1 << bit
        pairs = [(source, source ^ apart) for source in range(lax.axis_size("dp"))]
        other = lax.ppermute(value, "dp", pairs)
        moving = (jnp.bitwise_and(masks, apart) != 0)[:, None, None]
        value = jnp.where(moving, other, value)
    return value


def edges(block):
    count = lax.axis_size("seq")
    forward = [(i, i + 1) for i in range(count - 1)]
    backward = [(target, source) for source, target in forward]
    low = lax.ppermute(block[:, -1:], "seq", forward)
    high = lax.ppermute(block[:, :1], "seq", backward)
    return low, high


def shifted(block, low, high):
    before = jnp.concatenate([low, block[:, :-1]], axis=1)
    after = jnp.concatenate([block[:, 1:], high], axis=1)
    flat = (-1, block.shape[-1])
    return before.reshape(flat), block.reshape(flat), after.reshape(flat)


def heads_first(weight, parts):
    rows = weight.shape[0]
    split = weight.reshape(rows, 3, parts, WIDE // parts)
    return split.transpose(0, 2, 1, 3).reshape(rows, 3 * WIDE)


def heads_last(weight, parts):
    rows = weight.shape[0]
    split = weight.reshape(rows, parts, 3, WIDE // parts)
    return split.transpose(0, 2, 1, 3).reshape(rows, 3 * WIDE)


def gather_weights(big, small):
    copies = [piece.astype(BF) for piece in big]
    sizes = [piece.size for piece in small]
    flat = jnp.concatenate([piece.reshape(-1) for piece in small]).astype(BF)
    columns = copies[0].shape[1]
    high = -(-flat.size // columns)
    high = -(-high // 8) * 8
    flat = jnp.pad(flat, (0, high * columns - flat.size)).reshape(high, columns)
    rows = copies[-1].shape[0]
    copies[-1] = jnp.concatenate([copies[-1], flat], axis=0)
    full = [lax.all_gather(piece, "dp", axis=0) for piece in copies]
    last = full[-1]
    full[-1] = last[:, :rows]
    full = [piece.reshape(-1, piece.shape[-1]) for piece in full]
    table = last[:, rows:].reshape(last.shape[0], -1)
    vectors = []
    start = 0
    for piece, size in zip(small, sizes):
        part = table[:, start : start + size]
        vectors.append(part.reshape((-1,) + piece.shape[1:]).astype(F32))
        start += size
    return full, vectors


def reduce_grads(big, small):
    groups = lax.axis_size("dp")
    blocks = []
    for grad in big:
        rows, columns = grad.shape
        for start in range(0, columns, WIDE):
            blocks.append(grad[:, start : start + WIDE].reshape(groups, rows // groups, WIDE))
    flat = jnp.concatenate([piece.reshape(groups, -1) for piece in small], axis=1)
    high = -(-flat.shape[1] // WIDE)
    high = -(-high // 16) * 16
    flat = jnp.pad(flat, ((0, 0), (0, high * WIDE - flat.shape[1])))
    blocks.append(flat.reshape(groups, high, WIDE))
    packed = jnp.concatenate([piece.astype(BF) for piece in blocks], axis=1)
    mine = lax.psum_scatter(packed, "dp", scatter_dimension=0, tiled=False)
    mine = lax.psum(mine, "seq").astype(F32)
    outs = []
    at = 0
    for grad in big:
        rows, columns = grad.shape[0] // groups, grad.shape[1]
        parts = []
        for _ in range(columns // WIDE):
            parts.append(mine[at : at + rows])
            at += rows
        outs.append(parts[0] if len(parts) == 1 else jnp.concatenate(parts, axis=1))
    tail = mine[at:].reshape(-1)
    start = 0
    for piece in small:
        size = piece.size // groups
        shape = (piece.shape[0] // groups,) + piece.shape[1:]
        outs.append(tail[start : start + size].reshape(shape))
        start += size
    return outs


def body(
    tokens,
    chars,
    char_counts,
    lengths,
    perm,
    token_cot,
    char_cot,
    w_qkv,
    b_qv,
    w_out,
    w_in,
    b_in,
    w_back,
    gru_x,
    gru_h,
    gru_bias,
    blend_w,
    conv_w,
    conv_b,
    norm_gain,
    norm_bias,
    row_bias,
):
    parts = lax.axis_size("seq")
    seqs, local, width = tokens.shape
    rows = seqs * local
    per = width // HEAD // parts
    three = 3 * H
    masks = perm[:, 0]
    place = lax.axis_index("dp")
    own_lengths = lax.dynamic_slice(lengths, (place * seqs,), (seqs,))
    cots = relocate(masks, jnp.concatenate([token_cot, char_cot], axis=-1))

    big = (heads_first(w_qkv, parts), gru_x, w_out, w_in, w_back, blend_w, conv_w, gru_h)
    small = (b_qv, b_in, gru_bias, conv_b, norm_gain, norm_bias, row_bias)
    full, vectors = gather_weights(big, small)
    w_qkv, gru_x, w_out, w_in, w_back, blend_w, conv_w, gru_h = full
    b_qv, b_in, gru_bias, conv_b, norm_gain, norm_bias, row_bias = vectors

    flat_tokens = tokens.reshape(rows, width)
    bias = jnp.concatenate([b_qv[:width], jnp.zeros((width,), F32), b_qv[width:]])
    bias = heads_first(bias[None], parts)[0]
    project = (dot_plain(flat_tokens, w_qkv) + bias).astype(BF)
    span = 3 * per * HEAD
    qkv = project.reshape(seqs, local, parts, span).transpose(2, 0, 1, 3)
    qkv = exchange(qkv)
    context = exchange(attention_forward(qkv, own_lengths, per))
    context = context.transpose(1, 2, 0, 3).reshape(rows, width)

    counts = char_counts.reshape(rows, 1)
    flat_chars = chars.transpose(2, 0, 1, 3).reshape(NCHAR * rows, width)
    gates = (dot_plain(flat_chars, gru_x) + gru_bias[:, 0]).reshape(NCHAR, rows, 2 * three)
    sides = []
    for side in range(2):
        columns = slice(side * three, (side + 1) * three)
        state = jnp.zeros((rows, H), F32)
        steps = []
        for order in range(NCHAR):
            position = order if side == 0 else NCHAR - 1 - order
            live = position < counts
            low = state.astype(BF)
            recur = dot_plain(low, gru_h[:, columns]) + gru_bias[columns, 1]
            steps.append((position, live, low, recur, state))
            state = gru_cell(live, gates[position, :, columns], recur, state)
        sides.append((state, steps))
    char_state = jnp.concatenate([sides[0][0], sides[1][0]], axis=-1)

    summed_first = flat_tokens.astype(F32) + dot_plain(context, w_out) + row_bias[:, 0]
    hidden1 = norm_rows(summed_first, norm_gain[:, 0], norm_bias[:, 0])
    hidden1_low = hidden1.astype(BF)
    inner = dot_plain(hidden1_low, w_in) + b_in
    activated = gelu_exact(inner).astype(BF)
    summed_second = hidden1 + dot_plain(activated, w_back) + row_bias[:, 1]
    hidden2 = norm_rows(summed_second, norm_gain[:, 1], norm_bias[:, 1])
    hidden2_low = hidden2.astype(BF)
    char_low = char_state.astype(BF)
    token_side = dot_plain(hidden2_low, blend_w[:, :width]) + row_bias[:, 2]
    char_side = dot_plain(char_low, blend_w[:, width:]) + row_bias[:, 3]
    joined = jnp.concatenate([token_side, char_side], axis=-1).astype(BF)
    joined = joined.reshape(seqs, local, 2 * width)
    taps = shifted(joined, *edges(joined))
    stacked = jnp.concatenate(taps, axis=-1)
    mixed = dot_plain(stacked, conv_w) + conv_b
    lifted = gelu_exact(mixed)
    token_pre = hidden2 + lifted[:, :width]
    char_pre = char_state + lifted[:, width:]
    token_out = norm_rows(token_pre, norm_gain[:, 2], norm_bias[:, 2]).astype(BF)
    char_out = norm_rows(char_pre, norm_gain[:, 3], norm_bias[:, 3]).astype(BF)
    outs = jnp.concatenate([token_out, char_out], axis=-1).reshape(seqs, local, 2 * width)
    outs = relocate(masks, outs)

    flat_cots = cots.reshape(rows, 2 * width).astype(F32)
    d_token_pre, gain_token, shift_token = norm_back(
        token_pre, norm_gain[:, 2], flat_cots[:, :width]
    )
    d_char_pre, gain_char, shift_char = norm_back(char_pre, norm_gain[:, 3], flat_cots[:, width:])
    d_mixed = jnp.concatenate([d_token_pre, d_char_pre], axis=-1) * gelu_slope(mixed)
    d_mixed = d_mixed.astype(BF)
    grad_conv = dot_left(stacked, d_mixed)
    beside = d_mixed.reshape(seqs, local, 2 * width)
    before, same, after = shifted(beside, *edges(beside))
    taps_w = conv_w.reshape(3, 2 * width, 2 * width)
    d_joined = dot_right(after, taps_w[0]) + dot_right(same, taps_w[1])
    d_joined = (d_joined + dot_right(before, taps_w[2])).astype(BF)
    d_token_side = d_joined[:, :width]
    d_char_side = d_joined[:, width:]
    grad_blend = jnp.concatenate(
        [dot_left(hidden2_low, d_token_side), dot_left(char_low, d_char_side)], axis=-1
    )
    d_hidden2 = d_token_pre + dot_right(d_token_side, blend_w[:, :width])
    d_char_state = d_char_pre + dot_right(d_char_side, blend_w[:, width:])

    d_second, gain_second, shift_second = norm_back(summed_second, norm_gain[:, 1], d_hidden2)
    d_branch = d_second.astype(BF)
    grad_back = dot_left(activated, d_branch)
    d_inner = (dot_right(d_branch, w_back) * gelu_slope(inner)).astype(BF)
    grad_in = dot_left(hidden1_low, d_inner)
    d_hidden1 = d_second + dot_right(d_inner, w_in)
    d_first, gain_first, shift_first = norm_back(summed_first, norm_gain[:, 0], d_hidden1)
    d_attend = d_first.astype(BF)
    grad_out = dot_left(context, d_attend)
    d_context = dot_right(d_attend, w_out).astype(BF)
    d_context = d_context.reshape(seqs, local, parts, per * HEAD).transpose(2, 0, 1, 3)
    d_project = exchange(attention_backward(qkv, exchange(d_context), own_lengths, per))
    d_project = d_project.transpose(1, 2, 0, 3).reshape(rows, 3 * width)

    d_gates = [[None, None] for _ in range(NCHAR)]
    grad_side, bias_side = [], []
    for side in range(2):
        columns = slice(side * three, (side + 1) * three)
        d_state = d_char_state[:, side * H : (side + 1) * H]
        lows, recurs = [], []
        for position, live, low, recur, state in reversed(sides[side][1]):
            _, pull = jax.vjp(
                partial(gru_cell, live), gates[position, :, columns], recur, state
            )
            d_gate, d_recur, d_keep = pull(d_state)
            d_recur = d_recur.astype(BF)
            lows.append(low)
            recurs.append(d_recur)
            d_state = d_keep + dot_right(d_recur, gru_h[:, columns])
            d_gates[position][side] = d_gate.astype(BF)
        lows, recurs = jnp.concatenate(lows, axis=0), jnp.concatenate(recurs, axis=0)
        grad_side.append(dot_left(lows, recurs))
        bias_side.append(column_sum(recurs))
    d_gates = jnp.concatenate([jnp.concatenate(pair, axis=-1) for pair in d_gates], axis=0)
    grad_gru_x = dot_left(flat_chars, d_gates)
    chars_back = dot_right(d_gates, gru_x).astype(BF)
    chars_back = chars_back.reshape(NCHAR, seqs, local, width).transpose(1, 2, 0, 3)
    grad_gru_h = jnp.concatenate(grad_side, axis=-1)
    grad_gru_bias = jnp.stack([column_sum(d_gates), jnp.concatenate(bias_side)], axis=-1)

    grad_qkv = dot_left(flat_tokens, d_project)
    sums = heads_last(column_sum(d_project)[None], parts)[0]
    grad_b_qv = jnp.concatenate([sums[:width], sums[2 * width :]])
    tokens_back = (d_first + dot_right(d_project, w_qkv)).astype(BF)
    grad_gain = jnp.stack([gain_first, gain_second, gain_token, gain_char], axis=-1)
    grad_shift = jnp.stack([shift_first, shift_second, shift_token, shift_char], axis=-1)
    grad_rows = jnp.stack(
        [
            column_sum(d_attend),
            column_sum(d_branch),
            column_sum(d_token_side),
            column_sum(d_char_side),
        ],
        axis=-1,
    )
    big = (grad_qkv, grad_gru_x, grad_out, grad_in, grad_back, grad_blend, grad_conv, grad_gru_h)
    small = (
        grad_b_qv,
        column_sum(d_inner),
        grad_gru_bias,
        column_sum(d_mixed),
        grad_gain,
        grad_shift,
        grad_rows,
    )
    summed = reduce_grads(big, small)
    g_qkv, g_gru_x, g_out, g_in, g_back, g_blend, g_conv, g_gru_h = summed[:8]
    g_b_qv, g_b_in, g_gru_bias, g_conv_b, g_gain, g_shift, g_rows = summed[8:]
    return (
        outs[..., :width],
        outs[..., width:],
        tokens_back.reshape(seqs, local, width),
        chars_back,
        heads_last(g_qkv, parts),
        g_b_qv,
        g_out,
        g_in,
        g_b_in,
        g_back,
        g_gru_x,
        g_gru_h,
        g_gru_bias,
        g_blend,
        g_conv,
        g_conv_b,
        g_gain,
        g_shift,
        g_rows,
    )


def solution(mesh):
    rows, vector, seq = P("dp", None), P("dp"), P("dp", "seq", None)
    weights = (
        rows,
        vector,
        rows,
        rows,
        vector,
        rows,
        rows,
        rows,
        rows,
        rows,
        rows,
        vector,
        rows,
        rows,
        rows,
    )
    return jax.shard_map(
        body,
        mesh=mesh,
        in_specs=(seq, P("dp", "seq", None, None), P("dp", "seq"), P(), P(), seq, seq) + weights,
        out_specs=(seq, seq, seq, P("dp", "seq", None, None)) + weights,
        check_vma=False,
    )
```

```python
from functools import partial

import jax
import jax.numpy as jnp
from jax import lax
from jax.experimental import pallas as pl
from jax.experimental.pallas import tpu as pltpu
from jax.sharding import PartitionSpec as P

HEAD = 64
H = 384
NCHAR = 4
WIDE = 768
BF = jnp.bfloat16
F32 = jnp.float32


def dot_plain(left, right):
    return jnp.dot(left, right, preferred_element_type=F32)


def dot_left(left, right):
    return lax.dot_general(left, right, (((0,), (0,)), ((), ())), preferred_element_type=F32)


def dot_right(left, right):
    return lax.dot_general(left, right, (((1,), (1,)), ((), ())), preferred_element_type=F32)


def column_sum(values):
    return jnp.sum(values.astype(F32), axis=0)


def norm_rows(values, gain, shift):
    center = values - jnp.mean(values, axis=-1, keepdims=True)
    spread = jnp.mean(center * center, axis=-1, keepdims=True)
    rstd = lax.rsqrt(spread + 1e-06)
    return center * rstd * gain + shift


def norm_back(values, gain, grad):
    center = values - jnp.mean(values, axis=-1, keepdims=True)
    spread = jnp.mean(center * center, axis=-1, keepdims=True)
    rstd = lax.rsqrt(spread + 1e-06)
    hat = center * rstd
    lead = grad * gain
    back = rstd * (
        lead
        - jnp.mean(lead, axis=-1, keepdims=True)
        - hat * jnp.mean(lead * hat, axis=-1, keepdims=True)
    )
    return back, jnp.sum(grad * hat, axis=0), jnp.sum(grad, axis=0)


def gelu_exact(values):
    return jax.nn.gelu(values, approximate=False)


def gelu_slope(values):
    cdf = 0.5 * (1.0 + lax.erf(values * (0.5**0.5)))
    pdf = jnp.exp(-0.5 * values * values) * 0.3989422804014327
    return cdf + values * pdf


def gru_cell(live, gates, recur, state):
    width = state.shape[-1]
    reset = jax.nn.sigmoid(gates[:, :width] + recur[:, :width])
    update = jax.nn.sigmoid(gates[:, width : 2 * width] + recur[:, width : 2 * width])
    fresh = jnp.tanh(gates[:, 2 * width :] + reset * recur[:, 2 * width :])
    return jnp.where(live, (1.0 - update) * fresh + update * state, state)


def attention_forward_kernel(per, len_ref, qkv_ref, out_ref):
    block = pl.program_id(1)
    length = len_ref[pl.program_id(0)]
    span = per * HEAD
    total = qkv_ref.shape[0] * qkv_ref.shape[2]
    rows = qkv_ref.shape[2]
    q_all = qkv_ref[block, 0, :, :span]
    k_all = qkv_ref[:, 0, :, span : 2 * span].reshape(total, span)
    v_all = qkv_ref[:, 0, :, 2 * span :].reshape(total, span)
    valid = lax.broadcasted_iota(jnp.int32, (rows, total), 1) < length
    pieces = []
    for j in range(per):
        part = slice(j * HEAD, (j + 1) * HEAD)
        scores = dot_right(q_all[:, part], k_all[:, part]) * HEAD ** (-0.5)
        scores = jnp.where(valid, scores, -1e30)
        raised = jnp.exp(scores - jnp.max(scores, axis=-1, keepdims=True))
        probs = (raised / jnp.sum(raised, axis=-1, keepdims=True)).astype(BF)
        pieces.append(dot_plain(probs, v_all[:, part]))
    out_ref[0, 0] = jnp.concatenate(pieces, axis=-1).astype(BF)


def attention_forward(qkv, lengths, per):
    seqs, rows = qkv.shape[1], qkv.shape[2]
    parts = qkv.shape[0]
    span = per * HEAD
    return pl.pallas_call(
        partial(attention_forward_kernel, per),
        grid_spec=pltpu.PrefetchScalarGridSpec(
            num_scalar_prefetch=1,
            grid=(seqs, parts),
            in_specs=[pl.BlockSpec((parts, 1, rows, 3 * span), lambda m, b, n: (0, m, 0, 0))],
            out_specs=pl.BlockSpec((1, 1, rows, span), lambda m, b, n: (b, m, 0, 0)),
        ),
        out_shape=jax.ShapeDtypeStruct((parts, seqs, rows, span), BF),
        name="attend_forward",
    )(lengths, qkv)


def attention_backward_kernel(per, len_ref, qkv_ref, grad_ref, out_ref, key_acc, value_acc):
    block = pl.program_id(1)
    length = len_ref[pl.program_id(0)]
    span = per * HEAD
    parts, rows = qkv_ref.shape[0], qkv_ref.shape[2]
    total = parts * rows
    scale = HEAD ** (-0.5)

    @pl.when(block == 0)
    def _():
        key_acc[...] = jnp.zeros_like(key_acc)
        value_acc[...] = jnp.zeros_like(value_acc)

    q_all = qkv_ref[block, 0, :, :span]
    g_all = grad_ref[block, 0]
    k_all = qkv_ref[:, 0, :, span : 2 * span].reshape(total, span)
    v_all = qkv_ref[:, 0, :, 2 * span :].reshape(total, span)
    valid = lax.broadcasted_iota(jnp.int32, (total, rows), 0) < length
    q_pieces, k_pieces, v_pieces = [], [], []
    for j in range(per):
        part = slice(j * HEAD, (j + 1) * HEAD)
        q, g, k, v = q_all[:, part], g_all[:, part], k_all[:, part], v_all[:, part]
        scores = jnp.where(valid, dot_right(k, q) * scale, -1e30)
        raised = jnp.exp(scores - jnp.max(scores, axis=0, keepdims=True))
        probs = raised / jnp.sum(raised, axis=0, keepdims=True)
        d_probs = dot_right(v, g)
        delta = jnp.sum(d_probs * probs, axis=0, keepdims=True)
        d_scores = (probs * (d_probs - delta)).astype(BF)
        q_pieces.append(dot_left(d_scores, k) * scale)
        k_pieces.append(dot_plain(d_scores, q) * scale)
        v_pieces.append(dot_plain(probs.astype(BF), g))
    out_ref[block, 0, :, :span] = jnp.concatenate(q_pieces, axis=-1).astype(BF)
    key_acc[...] += jnp.concatenate(k_pieces, axis=-1)
    value_acc[...] += jnp.concatenate(v_pieces, axis=-1)

    @pl.when(block == parts - 1)
    def _():
        out_ref[:, 0, :, span : 2 * span] = key_acc[...].astype(BF).reshape(parts, rows, span)
        out_ref[:, 0, :, 2 * span :] = value_acc[...].astype(BF).reshape(parts, rows, span)


def attention_backward(qkv, grads, lengths, per):
    parts, seqs, rows, _ = qkv.shape
    span = per * HEAD
    return pl.pallas_call(
        partial(attention_backward_kernel, per),
        grid_spec=pltpu.PrefetchScalarGridSpec(
            num_scalar_prefetch=1,
            grid=(seqs, parts),
            in_specs=[
                pl.BlockSpec((parts, 1, rows, 3 * span), lambda m, b, n: (0, m, 0, 0)),
                pl.BlockSpec((parts, 1, rows, span), lambda m, b, n: (0, m, 0, 0)),
            ],
            out_specs=pl.BlockSpec((parts, 1, rows, 3 * span), lambda m, b, n: (0, m, 0, 0)),
            scratch_shapes=[
                pltpu.VMEM((parts * rows, span), F32),
                pltpu.VMEM((parts * rows, span), F32),
            ],
        ),
        out_shape=jax.ShapeDtypeStruct(qkv.shape, BF),
        name="attend_backward",
    )(lengths, qkv, grads)


def exchange(blocks):
    return lax.all_to_all(blocks, "seq", split_axis=0, concat_axis=0)


def relocate(masks, value, ties):
    levels = lax.axis_size("dp").bit_length() - 1
    for bit in range(levels):
        apart = 1 << bit
        pairs = [(source, source ^ apart) for source in range(lax.axis_size("dp"))]
        other = lax.ppermute(value, "dp", pairs)
        moving = (jnp.bitwise_and(masks, apart) != 0)[:, None, None]
        tie = ties[min(bit, len(ties) - 1)]
        other, value, _ = lax.optimization_barrier((other, value, tie))
        value = jnp.where(moving, other, value)
    return value


def edges(block):
    count = lax.axis_size("seq")
    forward = [(i, i + 1) for i in range(count - 1)]
    backward = [(target, source) for source, target in forward]
    low = lax.ppermute(block[:, -1:], "seq", forward)
    high = lax.ppermute(block[:, :1], "seq", backward)
    return low, high


def shifted(block, low, high):
    before = jnp.concatenate([low, block[:, :-1]], axis=1)
    after = jnp.concatenate([block[:, 1:], high], axis=1)
    flat = (-1, block.shape[-1])
    return before.reshape(flat), block.reshape(flat), after.reshape(flat)


def sum_plan(shapes, high):
    spans, start = [], 0
    for rows, columns in shapes:
        tall = rows // 8 // high
        count = tall * (columns // WIDE)
        spans.append((start, start + count, tall))
        start += count
    return spans, start


def sum_kernel(spans, total, high, lag, slots, *refs):
    count = len(spans)
    ins, outs = refs[:count], refs[count : 2 * count]
    own, rc, sc, s1a, s1b, r1a, r1b, r2a, r2b, s2, rz, sz, rm, tot = refs[2 * count : 2 * count + 14]
    sems = refs[2 * count + 14]
    credits = refs[2 * count + 15]
    half = WIDE // 2
    dp, z = lax.axis_index("dp"), lax.axis_index("seq")
    core, x, y = dp % 2, (dp // 2) % 2, dp // 4
    at_core = {"dp": dp + 1 - 2 * core}
    at_x = {"dp": dp + 2 - 4 * x}
    at_y = {"dp": dp + 4 - 8 * y}
    outer = (z % 3) == 0
    inner = (z % 3) != 0
    at_inner = {"seq": 1 + z // 3}
    at_middle = {"seq": (3 - z) % 4}
    at_outer = {"seq": (z // 2) * 3}

    barrier = pltpu.get_barrier_semaphore()

    def greet(where):
        pl.semaphore_signal(barrier, inc=1, device_id=where, device_id_type=pl.DeviceIdType.MESH)

    greet(at_core)
    greet(at_x)
    greet(at_y)

    @pl.when(outer)
    def _():
        greet(at_inner)
        pl.semaphore_wait(barrier, 4)

    @pl.when(inner)
    def _():
        greet(at_middle)
        greet(at_outer)
        pl.semaphore_wait(barrier, 5)

    def remote(source, target, name, slot, where):
        return pltpu.make_async_remote_copy(
            src_ref=source,
            dst_ref=target,
            send_sem=sems.at[2 * name, slot],
            recv_sem=sems.at[2 * name + 1, slot],
            device_id=where,
            device_id_type=pl.DeviceIdType.MESH,
        )

    CORE, X1, Y1, X2, Y2, OUTER, MIDDLE, FINAL, LOCAL = range(9)

    def give_credit(name, k, where):
        @pl.when(k + slots < total)
        def _():
            pl.semaphore_signal(
                credits.at[name], inc=1, device_id=where, device_id_type=pl.DeviceIdType.MESH
            )

    def take_credit(name, k):
        @pl.when(k >= slots)
        def _():
            pl.semaphore_wait(credits.at[name], 1)

    def send_core(slot, source):
        return remote(source, rc.at[slot], CORE, slot, at_core)

    def send_x1(slot):
        return remote(sc.at[slot, :, 1 - x, :, :half], r1a.at[slot], X1, slot, at_x)

    def send_y1(slot):
        return remote(sc.at[slot, 1 - y, :, :, half:], r1b.at[slot], Y1, slot, at_y)

    def send_y2(slot):
        return remote(s1a.at[slot, 1 - y], r2a.at[slot], Y2, slot, at_y)

    def send_x2(slot):
        return remote(s1b.at[slot, 1 - x], r2b.at[slot], X2, slot, at_x)

    def send_outer(slot):
        return remote(s2.at[slot], rz.at[slot], OUTER, slot, at_inner)

    def send_middle(slot):
        return remote(sz.at[slot], rm.at[slot], MIDDLE, slot, at_middle)

    def send_final(slot, target):
        return remote(tot.at[slot], target, FINAL, slot, at_outer)

    def load(slot, source):
        return pltpu.make_async_copy(source, own.at[slot], sems.at[2 * LOCAL, slot])

    def save(slot, target):
        return pltpu.make_async_copy(tot.at[slot], target, sems.at[2 * LOCAL + 1, slot])

    def window(ref, j, tall):
        return pl.ds((j % tall) * high, high), pl.ds((j // tall) * WIDE, WIDE)

    def add(left, right):
        return (left.astype(F32) + right.astype(F32)).astype(BF)

    def stage(k, run):
        @pl.when((k >= 0) & (k < total))
        def _():
            run(k, lax.rem(jnp.maximum(k, 0), slots))

    first = ins[0].at[:, core, pl.ds(0, high), pl.ds(0, WIDE)]
    final = outs[0].at[pl.ds(0, high), pl.ds(0, WIDE)]

    @pl.loop(0, total + 6 * lag)
    def _(t):
        def begin(k, slot):
            take_credit(CORE, k)
            for (start, stop, tall), ref in zip(spans, ins):

                @pl.when((k >= start) & (k < stop))
                def _():
                    rows, columns = window(ref, k - start, tall)
                    send_core(slot, ref.at[:, 1 - core, rows, columns]).start()
                    load(slot, ref.at[:, core, rows, columns]).start()

        def add_core(k, slot):
            load(slot, first).wait()
            send_core(slot, first).wait()
            both = add(own[slot], rc[slot])
            sc[slot] = both.reshape(2, 2, high, WIDE)
            give_credit(CORE, k, at_core)

        def add_one(k, slot):
            send_x1(slot).wait()
            send_y1(slot).wait()
            s1a[slot] = add(sc[slot, :, x, :, :half], r1a[slot])
            s1b[slot] = add(sc[slot, y, :, :, half:], r1b[slot])
            give_credit(X1, k, at_x)
            give_credit(Y1, k, at_y)

        def add_two(k, slot):
            send_y2(slot).wait()
            send_x2(slot).wait()
            s2[slot, :, :half] = add(s1a[slot, y], r2a[slot])
            s2[slot, :, half:] = add(s1b[slot, x], r2b[slot])
            give_credit(Y2, k, at_y)
            give_credit(X2, k, at_x)

        def add_outer(k, slot):
            @pl.when(outer)
            def _():
                send_outer(slot).wait_send()

            @pl.when(inner)
            def _():
                send_outer(slot).wait_recv()
                sz[slot] = add(s2[slot], rz[slot])
                give_credit(OUTER, k, at_outer)

        def add_middle(k, slot):
            @pl.when(inner)
            def _():
                send_middle(slot).wait()
                tot[slot] = add(sz[slot], rm[slot])
                give_credit(MIDDLE, k, at_middle)

        def finish(k, slot):
            @pl.when(inner)
            def _():
                save(slot, final).wait()
                send_final(slot, final).wait_send()

            @pl.when(outer)
            def _():
                send_final(slot, final).wait_recv()
                give_credit(FINAL, k, at_inner)

        def go_one(k, slot):
            take_credit(X1, k)
            send_x1(slot).start()
            take_credit(Y1, k)
            send_y1(slot).start()

        def go_two(k, slot):
            take_credit(Y2, k)
            send_y2(slot).start()
            take_credit(X2, k)
            send_x2(slot).start()

        def go_outer(k, slot):
            @pl.when(outer)
            def _():
                take_credit(OUTER, k)
                send_outer(slot).start()

        def go_middle(k, slot):
            @pl.when(inner)
            def _():
                take_credit(MIDDLE, k)
                send_middle(slot).start()

        def go_final(k, slot):
            @pl.when(inner)
            def _():
                take_credit(FINAL, k)
                for (start, stop, tall), ref in zip(spans, outs):

                    @pl.when((k >= start) & (k < stop))
                    def _():
                        rows, columns = window(ref, k - start, tall)
                        save(slot, ref.at[rows, columns]).start()
                        send_final(slot, ref.at[rows, columns]).start()

        stage(t, begin)
        stage(t - lag, add_core)
        stage(t - 2 * lag, add_one)
        stage(t - 3 * lag, add_two)
        stage(t - 4 * lag, add_outer)
        stage(t - 5 * lag, add_middle)
        stage(t - lag, go_one)
        stage(t - 2 * lag, go_two)
        stage(t - 3 * lag, go_outer)
        stage(t - 4 * lag, go_middle)
        stage(t - 5 * lag, go_final)
        stage(t - 6 * lag, finish)


def sum_grads(grads, high=48, lag=2, slots=4):
    shapes = [grad.shape for grad in grads]
    spans, total = sum_plan(shapes, high)
    half = WIDE // 2
    anywhere = pl.BlockSpec(memory_space=pl.ANY)
    blocks = [grad.reshape(4, 2, grad.shape[0] // 8, grad.shape[1]) for grad in grads]
    return pl.pallas_call(
        partial(sum_kernel, spans, total, high, lag, slots),
        in_specs=[anywhere] * len(grads),
        out_specs=[anywhere] * len(grads),
        out_shape=[jax.ShapeDtypeStruct((rows // 8, columns), BF) for rows, columns in shapes],
        scratch_shapes=[
            pltpu.VMEM((slots, 4, high, WIDE), BF),
            pltpu.VMEM((slots, 4, high, WIDE), BF),
            pltpu.VMEM((slots, 2, 2, high, WIDE), BF),
            pltpu.VMEM((slots, 2, high, half), BF),
            pltpu.VMEM((slots, 2, high, half), BF),
            pltpu.VMEM((slots, 2, high, half), BF),
            pltpu.VMEM((slots, 2, high, half), BF),
            pltpu.VMEM((slots, high, half), BF),
            pltpu.VMEM((slots, high, half), BF),
            pltpu.VMEM((slots, high, WIDE), BF),
            pltpu.VMEM((slots, high, WIDE), BF),
            pltpu.VMEM((slots, high, WIDE), BF),
            pltpu.VMEM((slots, high, WIDE), BF),
            pltpu.VMEM((slots, high, WIDE), BF),
            pltpu.SemaphoreType.DMA((18, slots)),
            pltpu.SemaphoreType.REGULAR((8,)),
        ],
        compiler_params=pltpu.CompilerParams(collective_id=1, has_side_effects=True),
        name="sum_grads",
    )(*blocks)


def heads_first(weight, parts):
    rows = weight.shape[0]
    split = weight.reshape(rows, 3, parts, WIDE // parts)
    return split.transpose(0, 2, 1, 3).reshape(rows, 3 * WIDE)


def heads_last(weight, parts):
    rows = weight.shape[0]
    split = weight.reshape(rows, parts, 3, WIDE // parts)
    return split.transpose(0, 2, 1, 3).reshape(rows, 3 * WIDE)


def gather_weights(big, small):
    copies = [piece.astype(BF) for piece in big]
    sizes = [piece.size for piece in small]
    flat = jnp.concatenate([piece.reshape(-1) for piece in small]).astype(BF)
    columns = copies[0].shape[1]
    high = -(-flat.size // columns)
    high = -(-high // 8) * 8
    flat = jnp.pad(flat, (0, high * columns - flat.size)).reshape(high, columns)
    rows = copies[-1].shape[0]
    copies[-1] = jnp.concatenate([copies[-1], flat], axis=0)
    full = [lax.all_gather(piece, "dp", axis=0) for piece in copies]
    last = full[-1]
    full[-1] = last[:, :rows]
    full = [piece.reshape(-1, piece.shape[-1]) for piece in full]
    table = last[:, rows:].reshape(last.shape[0], -1)
    vectors = []
    start = 0
    for piece, size in zip(small, sizes):
        part = table[:, start : start + size]
        vectors.append(part.reshape((-1,) + piece.shape[1:]).astype(F32))
        start += size
    return full, vectors


def pack_small(small, groups, multiple):
    flat = jnp.concatenate([piece.reshape(groups, -1) for piece in small], axis=1)
    high = -(-flat.shape[1] // WIDE)
    high = -(-high // multiple) * multiple
    flat = jnp.pad(flat, ((0, 0), (0, high * WIDE - flat.shape[1])))
    return flat.reshape(groups * high, WIDE).astype(BF)


def sum_grads_plain(grads):
    groups = lax.axis_size("dp")
    blocks = []
    for grad in grads:
        rows, columns = grad.shape
        for start in range(0, columns, WIDE):
            blocks.append(grad[:, start : start + WIDE].reshape(groups, rows // groups, WIDE))
    packed = jnp.concatenate(blocks, axis=1)
    mine = lax.psum_scatter(packed, "dp", scatter_dimension=0, tiled=False)
    mine = lax.psum(mine, "seq")
    outs, at = [], 0
    for grad in grads:
        rows, columns = grad.shape[0] // groups, grad.shape[1]
        parts = []
        for _ in range(columns // WIDE):
            parts.append(mine[at : at + rows])
            at += rows
        outs.append(jnp.concatenate(parts, axis=1))
    return outs


def reduce_grads(big, small):
    groups = lax.axis_size("dp")
    ours = groups == 8 and lax.axis_size("seq") == 4
    grads = [grad.astype(BF) for grad in big] + [pack_small(small, groups, 48)]
    outs = sum_grads(grads) if ours else sum_grads_plain(grads)
    outs = [piece.astype(F32) for piece in outs]
    tail = outs.pop().reshape(-1)
    start = 0
    for piece in small:
        size = piece.size // groups
        shape = (piece.shape[0] // groups,) + piece.shape[1:]
        outs.append(tail[start : start + size].reshape(shape))
        start += size
    return outs


def body(
    tokens,
    chars,
    char_counts,
    lengths,
    perm,
    token_cot,
    char_cot,
    w_qkv,
    b_qv,
    w_out,
    w_in,
    b_in,
    w_back,
    gru_x,
    gru_h,
    gru_bias,
    blend_w,
    conv_w,
    conv_b,
    norm_gain,
    norm_bias,
    row_bias,
):
    parts = lax.axis_size("seq")
    seqs, local, width = tokens.shape
    rows = seqs * local
    per = width // HEAD // parts
    three = 3 * H
    masks = perm[:, 0]
    place = lax.axis_index("dp")
    own_lengths = lax.dynamic_slice(lengths, (place * seqs,), (seqs,))
    big = (heads_first(w_qkv, parts), gru_x, w_out, w_in, w_back, blend_w, conv_w, gru_h)
    small = (b_qv, b_in, gru_bias, conv_b, norm_gain, norm_bias, row_bias)
    full, vectors = gather_weights(big, small)
    w_qkv, gru_x, w_out, w_in, w_back, blend_w, conv_w, gru_h = full
    b_qv, b_in, gru_bias, conv_b, norm_gain, norm_bias, row_bias = vectors

    flat_tokens = tokens.reshape(rows, width)
    bias = jnp.concatenate([b_qv[:width], jnp.zeros((width,), F32), b_qv[width:]])
    bias = heads_first(bias[None], parts)[0]
    project = (dot_plain(flat_tokens, w_qkv) + bias).astype(BF)
    span = 3 * per * HEAD
    qkv = project.reshape(seqs, local, parts, span).transpose(2, 0, 1, 3)
    qkv = exchange(qkv)
    context = exchange(attention_forward(qkv, own_lengths, per))
    context = context.transpose(1, 2, 0, 3).reshape(rows, width)

    counts = char_counts.reshape(rows, 1)
    flat_chars = chars.transpose(2, 0, 1, 3).reshape(NCHAR * rows, width)
    gates = (dot_plain(flat_chars, gru_x) + gru_bias[:, 0]).reshape(NCHAR, rows, 2 * three)
    sides = []
    for side in range(2):
        columns = slice(side * three, (side + 1) * three)
        state = jnp.zeros((rows, H), F32)
        steps = []
        for order in range(NCHAR):
            position = order if side == 0 else NCHAR - 1 - order
            live = position < counts
            low = state.astype(BF)
            recur = dot_plain(low, gru_h[:, columns]) + gru_bias[columns, 1]
            steps.append((position, live, low, recur, state))
            state = gru_cell(live, gates[position, :, columns], recur, state)
        sides.append((state, steps))
    char_state = jnp.concatenate([sides[0][0], sides[1][0]], axis=-1)

    cots = jnp.concatenate([token_cot, char_cot], axis=-1)
    cots = relocate(masks, cots, (project, context, context))
    summed_first = flat_tokens.astype(F32) + dot_plain(context, w_out) + row_bias[:, 0]
    hidden1 = norm_rows(summed_first, norm_gain[:, 0], norm_bias[:, 0])
    hidden1_low = hidden1.astype(BF)
    inner = dot_plain(hidden1_low, w_in) + b_in
    activated = gelu_exact(inner).astype(BF)
    summed_second = hidden1 + dot_plain(activated, w_back) + row_bias[:, 1]
    hidden2 = norm_rows(summed_second, norm_gain[:, 1], norm_bias[:, 1])
    hidden2_low = hidden2.astype(BF)
    char_low = char_state.astype(BF)
    token_side = dot_plain(hidden2_low, blend_w[:, :width]) + row_bias[:, 2]
    char_side = dot_plain(char_low, blend_w[:, width:]) + row_bias[:, 3]
    joined = jnp.concatenate([token_side, char_side], axis=-1).astype(BF)
    joined = joined.reshape(seqs, local, 2 * width)
    taps = shifted(joined, *edges(joined))
    stacked = jnp.concatenate(taps, axis=-1)
    mixed = dot_plain(stacked, conv_w) + conv_b
    lifted = gelu_exact(mixed)
    token_pre = hidden2 + lifted[:, :width]
    char_pre = char_state + lifted[:, width:]
    token_out = norm_rows(token_pre, norm_gain[:, 2], norm_bias[:, 2]).astype(BF)
    char_out = norm_rows(char_pre, norm_gain[:, 3], norm_bias[:, 3]).astype(BF)
    outs = jnp.concatenate([token_out, char_out], axis=-1).reshape(seqs, local, 2 * width)

    flat_cots = cots.reshape(rows, 2 * width).astype(F32)
    d_token_pre, gain_token, shift_token = norm_back(
        token_pre, norm_gain[:, 2], flat_cots[:, :width]
    )
    d_char_pre, gain_char, shift_char = norm_back(char_pre, norm_gain[:, 3], flat_cots[:, width:])
    d_mixed = jnp.concatenate([d_token_pre, d_char_pre], axis=-1) * gelu_slope(mixed)
    d_mixed = d_mixed.astype(BF)
    grad_conv = dot_left(stacked, d_mixed)
    beside = d_mixed.reshape(seqs, local, 2 * width)
    before, same, after = shifted(beside, *edges(beside))
    taps_w = conv_w.reshape(3, 2 * width, 2 * width)
    d_joined = dot_right(after, taps_w[0]) + dot_right(same, taps_w[1])
    d_joined = (d_joined + dot_right(before, taps_w[2])).astype(BF)
    d_token_side = d_joined[:, :width]
    d_char_side = d_joined[:, width:]
    grad_blend = jnp.concatenate(
        [dot_left(hidden2_low, d_token_side), dot_left(char_low, d_char_side)], axis=-1
    )
    d_hidden2 = d_token_pre + dot_right(d_token_side, blend_w[:, :width])
    d_char_state = d_char_pre + dot_right(d_char_side, blend_w[:, width:])

    d_second, gain_second, shift_second = norm_back(summed_second, norm_gain[:, 1], d_hidden2)
    d_branch = d_second.astype(BF)
    grad_back = dot_left(activated, d_branch)
    d_inner = (dot_right(d_branch, w_back) * gelu_slope(inner)).astype(BF)
    grad_in = dot_left(hidden1_low, d_inner)
    d_hidden1 = d_second + dot_right(d_inner, w_in)
    d_first, gain_first, shift_first = norm_back(summed_first, norm_gain[:, 0], d_hidden1)
    d_attend = d_first.astype(BF)
    grad_out = dot_left(context, d_attend)
    d_context = dot_right(d_attend, w_out).astype(BF)
    d_context = d_context.reshape(seqs, local, parts, per * HEAD).transpose(2, 0, 1, 3)
    d_project = exchange(attention_backward(qkv, exchange(d_context), own_lengths, per))
    d_project = d_project.transpose(1, 2, 0, 3).reshape(rows, 3 * width)

    d_gates = [[None, None] for _ in range(NCHAR)]
    grad_side, bias_side = [], []
    for side in range(2):
        columns = slice(side * three, (side + 1) * three)
        d_state = d_char_state[:, side * H : (side + 1) * H]
        lows, recurs = [], []
        for position, live, low, recur, state in reversed(sides[side][1]):
            _, pull = jax.vjp(
                partial(gru_cell, live), gates[position, :, columns], recur, state
            )
            d_gate, d_recur, d_keep = pull(d_state)
            d_recur = d_recur.astype(BF)
            lows.append(low)
            recurs.append(d_recur)
            d_state = d_keep + dot_right(d_recur, gru_h[:, columns])
            d_gates[position][side] = d_gate.astype(BF)
        lows, recurs = jnp.concatenate(lows, axis=0), jnp.concatenate(recurs, axis=0)
        grad_side.append(dot_left(lows, recurs))
        bias_side.append(column_sum(recurs))
    d_gates = jnp.concatenate([jnp.concatenate(pair, axis=-1) for pair in d_gates], axis=0)
    grad_gru_x = dot_left(flat_chars, d_gates)
    chars_back = dot_right(d_gates, gru_x).astype(BF)
    chars_back = chars_back.reshape(NCHAR, seqs, local, width).transpose(1, 2, 0, 3)
    grad_gru_h = jnp.concatenate(grad_side, axis=-1)
    grad_gru_bias = jnp.stack([column_sum(d_gates), jnp.concatenate(bias_side)], axis=-1)

    outs = relocate(masks, outs, (d_joined, d_inner, d_context))
    grad_qkv = dot_left(flat_tokens, d_project)
    sums = heads_last(column_sum(d_project)[None], parts)[0]
    grad_b_qv = jnp.concatenate([sums[:width], sums[2 * width :]])
    tokens_back = (d_first + dot_right(d_project, w_qkv)).astype(BF)
    grad_gain = jnp.stack([gain_first, gain_second, gain_token, gain_char], axis=-1)
    grad_shift = jnp.stack([shift_first, shift_second, shift_token, shift_char], axis=-1)
    grad_rows = jnp.stack(
        [
            column_sum(d_attend),
            column_sum(d_branch),
            column_sum(d_token_side),
            column_sum(d_char_side),
        ],
        axis=-1,
    )
    big = (grad_qkv, grad_gru_x, grad_out, grad_in, grad_back, grad_blend, grad_conv, grad_gru_h)
    small = (
        grad_b_qv,
        column_sum(d_inner),
        grad_gru_bias,
        column_sum(d_mixed),
        grad_gain,
        grad_shift,
        grad_rows,
    )
    summed = reduce_grads(big, small)
    g_qkv, g_gru_x, g_out, g_in, g_back, g_blend, g_conv, g_gru_h = summed[:8]
    g_b_qv, g_b_in, g_gru_bias, g_conv_b, g_gain, g_shift, g_rows = summed[8:]
    return (
        outs[..., :width],
        outs[..., width:],
        tokens_back.reshape(seqs, local, width),
        chars_back,
        heads_last(g_qkv, parts),
        g_b_qv,
        g_out,
        g_in,
        g_b_in,
        g_back,
        g_gru_x,
        g_gru_h,
        g_gru_bias,
        g_blend,
        g_conv,
        g_conv_b,
        g_gain,
        g_shift,
        g_rows,
    )


def solution(mesh):
    rows, vector, seq = P("dp", None), P("dp"), P("dp", "seq", None)
    weights = (
        rows,
        vector,
        rows,
        rows,
        vector,
        rows,
        rows,
        rows,
        rows,
        rows,
        rows,
        vector,
        rows,
        rows,
        rows,
    )
    return jax.shard_map(
        body,
        mesh=mesh,
        in_specs=(seq, P("dp", "seq", None, None), P("dp", "seq"), P(), P(), seq, seq) + weights,
        out_specs=(seq, seq, seq, P("dp", "seq", None, None)) + weights,
        check_vma=False,
    )
```

```python
from functools import partial

import jax
import jax.numpy as jnp
from jax import lax
from jax.experimental import pallas as pl
from jax.experimental.pallas import tpu as pltpu
from jax.sharding import PartitionSpec as P

HEAD = 64
H = 384
NCHAR = 4
WIDE = 768
BF = jnp.bfloat16
F32 = jnp.float32


def dot_plain(left, right):
    return jnp.dot(left, right, preferred_element_type=F32)


def dot_left(left, right):
    return lax.dot_general(left, right, (((0,), (0,)), ((), ())), preferred_element_type=F32)


def dot_right(left, right):
    return lax.dot_general(left, right, (((1,), (1,)), ((), ())), preferred_element_type=F32)


def column_sum(values):
    return jnp.sum(values.astype(F32), axis=0)


def norm_rows(values, gain, shift):
    center = values - jnp.mean(values, axis=-1, keepdims=True)
    spread = jnp.mean(center * center, axis=-1, keepdims=True)
    rstd = lax.rsqrt(spread + 1e-06)
    return center * rstd * gain + shift


def norm_back(values, gain, grad):
    center = values - jnp.mean(values, axis=-1, keepdims=True)
    spread = jnp.mean(center * center, axis=-1, keepdims=True)
    rstd = lax.rsqrt(spread + 1e-06)
    hat = center * rstd
    lead = grad * gain
    back = rstd * (
        lead
        - jnp.mean(lead, axis=-1, keepdims=True)
        - hat * jnp.mean(lead * hat, axis=-1, keepdims=True)
    )
    return back, jnp.sum(grad * hat, axis=0), jnp.sum(grad, axis=0)


def gelu_exact(values):
    return jax.nn.gelu(values, approximate=False)


def gelu_slope(values):
    cdf = 0.5 * (1.0 + lax.erf(values * (0.5**0.5)))
    pdf = jnp.exp(-0.5 * values * values) * 0.3989422804014327
    return cdf + values * pdf


def gru_cell(live, gates, recur, state):
    width = state.shape[-1]
    reset = jax.nn.sigmoid(gates[:, :width] + recur[:, :width])
    update = jax.nn.sigmoid(gates[:, width : 2 * width] + recur[:, width : 2 * width])
    fresh = jnp.tanh(gates[:, 2 * width :] + reset * recur[:, 2 * width :])
    return jnp.where(live, (1.0 - update) * fresh + update * state, state)


def attention_forward_kernel(per, len_ref, qkv_ref, out_ref):
    block = pl.program_id(1)
    length = len_ref[pl.program_id(0)]
    span = per * HEAD
    total = qkv_ref.shape[0] * qkv_ref.shape[2]
    rows = qkv_ref.shape[2]
    q_all = qkv_ref[block, 0, :, :span]
    k_all = qkv_ref[:, 0, :, span : 2 * span].reshape(total, span)
    v_all = qkv_ref[:, 0, :, 2 * span :].reshape(total, span)
    valid = lax.broadcasted_iota(jnp.int32, (rows, total), 1) < length
    pieces = []
    for j in range(per):
        part = slice(j * HEAD, (j + 1) * HEAD)
        scores = dot_right(q_all[:, part], k_all[:, part]) * HEAD ** (-0.5)
        scores = jnp.where(valid, scores, -1e30)
        raised = jnp.exp(scores - jnp.max(scores, axis=-1, keepdims=True))
        probs = (raised / jnp.sum(raised, axis=-1, keepdims=True)).astype(BF)
        pieces.append(dot_plain(probs, v_all[:, part]))
    out_ref[0, 0] = jnp.concatenate(pieces, axis=-1).astype(BF)


def attention_forward(qkv, lengths, per):
    seqs, rows = qkv.shape[1], qkv.shape[2]
    parts = qkv.shape[0]
    span = per * HEAD
    return pl.pallas_call(
        partial(attention_forward_kernel, per),
        grid_spec=pltpu.PrefetchScalarGridSpec(
            num_scalar_prefetch=1,
            grid=(seqs, parts),
            in_specs=[pl.BlockSpec((parts, 1, rows, 3 * span), lambda m, b, n: (0, m, 0, 0))],
            out_specs=pl.BlockSpec((1, 1, rows, span), lambda m, b, n: (b, m, 0, 0)),
        ),
        out_shape=jax.ShapeDtypeStruct((parts, seqs, rows, span), BF),
        name="attend_forward",
    )(lengths, qkv)


def attention_backward_kernel(per, len_ref, qkv_ref, grad_ref, out_ref, key_acc, value_acc):
    block = pl.program_id(1)
    length = len_ref[pl.program_id(0)]
    span = per * HEAD
    parts, rows = qkv_ref.shape[0], qkv_ref.shape[2]
    total = parts * rows
    scale = HEAD ** (-0.5)

    @pl.when(block == 0)
    def _():
        key_acc[...] = jnp.zeros_like(key_acc)
        value_acc[...] = jnp.zeros_like(value_acc)

    q_all = qkv_ref[block, 0, :, :span]
    g_all = grad_ref[block, 0]
    k_all = qkv_ref[:, 0, :, span : 2 * span].reshape(total, span)
    v_all = qkv_ref[:, 0, :, 2 * span :].reshape(total, span)
    valid = lax.broadcasted_iota(jnp.int32, (total, rows), 0) < length
    q_pieces, k_pieces, v_pieces = [], [], []
    for j in range(per):
        part = slice(j * HEAD, (j + 1) * HEAD)
        q, g, k, v = q_all[:, part], g_all[:, part], k_all[:, part], v_all[:, part]
        scores = jnp.where(valid, dot_right(k, q) * scale, -1e30)
        raised = jnp.exp(scores - jnp.max(scores, axis=0, keepdims=True))
        probs = raised / jnp.sum(raised, axis=0, keepdims=True)
        d_probs = dot_right(v, g)
        delta = jnp.sum(d_probs * probs, axis=0, keepdims=True)
        d_scores = (probs * (d_probs - delta)).astype(BF)
        q_pieces.append(dot_left(d_scores, k) * scale)
        k_pieces.append(dot_plain(d_scores, q) * scale)
        v_pieces.append(dot_plain(probs.astype(BF), g))
    out_ref[block, 0, :, :span] = jnp.concatenate(q_pieces, axis=-1).astype(BF)
    key_acc[...] += jnp.concatenate(k_pieces, axis=-1)
    value_acc[...] += jnp.concatenate(v_pieces, axis=-1)

    @pl.when(block == parts - 1)
    def _():
        out_ref[:, 0, :, span : 2 * span] = key_acc[...].astype(BF).reshape(parts, rows, span)
        out_ref[:, 0, :, 2 * span :] = value_acc[...].astype(BF).reshape(parts, rows, span)


def attention_backward(qkv, grads, lengths, per):
    parts, seqs, rows, _ = qkv.shape
    span = per * HEAD
    return pl.pallas_call(
        partial(attention_backward_kernel, per),
        grid_spec=pltpu.PrefetchScalarGridSpec(
            num_scalar_prefetch=1,
            grid=(seqs, parts),
            in_specs=[
                pl.BlockSpec((parts, 1, rows, 3 * span), lambda m, b, n: (0, m, 0, 0)),
                pl.BlockSpec((parts, 1, rows, span), lambda m, b, n: (0, m, 0, 0)),
            ],
            out_specs=pl.BlockSpec((parts, 1, rows, 3 * span), lambda m, b, n: (0, m, 0, 0)),
            scratch_shapes=[
                pltpu.VMEM((parts * rows, span), F32),
                pltpu.VMEM((parts * rows, span), F32),
            ],
        ),
        out_shape=jax.ShapeDtypeStruct(qkv.shape, BF),
        name="attend_backward",
    )(lengths, qkv, grads)


def exchange(blocks):
    return lax.all_to_all(blocks, "seq", split_axis=0, concat_axis=0)


def relocate_step(masks, value, bit):
    count = lax.axis_size("dp")
    apart = 1 << bit
    pairs = [(source, source ^ apart) for source in range(count)]
    other = lax.ppermute(value, "dp", pairs)
    moving = (jnp.bitwise_and(masks, apart) != 0)[:, None, None]
    return other, value, moving


def relocate(masks, value, ties):
    levels = lax.axis_size("dp").bit_length() - 1
    for bit in range(levels):
        other, value, moving = relocate_step(masks, value, bit)
        tie = ties[min(bit, len(ties) - 1)]
        other, value, _ = lax.optimization_barrier((other, value, tie))
        value = jnp.where(moving, other, value)
    return value


def edges(block):
    count = lax.axis_size("seq")
    forward = [(i, i + 1) for i in range(count - 1)]
    backward = [(target, source) for source, target in forward]
    low = lax.ppermute(block[:, -1:], "seq", forward)
    high = lax.ppermute(block[:, :1], "seq", backward)
    return low, high


LINE = ([(0, 1), (3, 2)], [(1, 2), (2, 1)], [(1, 0), (2, 3)])


def line_sum(value, step):
    if lax.axis_size("seq") != 4:
        return lax.psum(value, "seq") if step == 0 else value
    other = lax.ppermute(value, "seq", LINE[step])
    if step < 2:
        return value + other
    return jnp.where((lax.axis_index("seq") % 3) == 0, other, value)


def shifted(block, low, high):
    before = jnp.concatenate([low, block[:, :-1]], axis=1)
    after = jnp.concatenate([block[:, 1:], high], axis=1)
    flat = (-1, block.shape[-1])
    return before.reshape(flat), block.reshape(flat), after.reshape(flat)


def sum_plan(shapes, high):
    spans, start = [], 0
    for rows, columns in shapes:
        tall = rows // high
        count = tall * (columns // WIDE)
        spans.append((start, start + count, tall))
        start += count
    return spans, start


def sum_kernel(spans, pre_spans, late, pre, high, lag, slots, *refs):
    whole = len(spans)
    count = whole + len(pre_spans)
    total = late + pre
    ins, outs = refs[:count], refs[count : 2 * count]
    own, rc, sc, s1a, s1b, r1a, r1b, r2a, r2b, s2, rz, sz, rm, tot, ready = refs[
        2 * count : 2 * count + 15
    ]
    sems = refs[2 * count + 15]
    credits = refs[2 * count + 16]
    half = WIDE // 2
    dp, z = lax.axis_index("dp"), lax.axis_index("seq")
    core, x, y = dp % 2, (dp // 2) % 2, dp // 4
    at_core = {"dp": dp + 1 - 2 * core}
    at_x = {"dp": dp + 2 - 4 * x}
    at_y = {"dp": dp + 4 - 8 * y}
    outer = (z % 3) == 0
    inner = (z % 3) != 0
    at_inner = {"seq": 1 + z // 3}
    at_middle = {"seq": (3 - z) % 4}
    at_outer = {"seq": (z // 2) * 3}

    barrier = pltpu.get_barrier_semaphore()

    def greet(where):
        pl.semaphore_signal(barrier, inc=1, device_id=where, device_id_type=pl.DeviceIdType.MESH)

    greet(at_core)
    greet(at_x)
    greet(at_y)

    @pl.when(outer)
    def _():
        greet(at_inner)
        pl.semaphore_wait(barrier, 4)

    @pl.when(inner)
    def _():
        greet(at_middle)
        greet(at_outer)
        pl.semaphore_wait(barrier, 5)

    def remote(source, target, name, slot, where):
        return pltpu.make_async_remote_copy(
            src_ref=source,
            dst_ref=target,
            send_sem=sems.at[2 * name, slot],
            recv_sem=sems.at[2 * name + 1, slot],
            device_id=where,
            device_id_type=pl.DeviceIdType.MESH,
        )

    CORE, X1, Y1, X2, Y2, OUTER, MIDDLE, FINAL, LOCAL, READY = range(10)

    def give_credit(name, k, where):
        @pl.when(k + slots < total)
        def _():
            pl.semaphore_signal(
                credits.at[name], inc=1, device_id=where, device_id_type=pl.DeviceIdType.MESH
            )

    def take_credit(name, k):
        @pl.when(k >= slots)
        def _():
            pl.semaphore_wait(credits.at[name], 1)

    def send_core(slot, source):
        return remote(source, rc.at[slot], CORE, slot, at_core)

    def send_x1(slot):
        return remote(sc.at[slot, :, 1 - x, :, :half], r1a.at[slot], X1, slot, at_x)

    def send_y1(slot):
        return remote(sc.at[slot, 1 - y, :, :, half:], r1b.at[slot], Y1, slot, at_y)

    def send_y2(slot):
        return remote(s1a.at[slot, 1 - y], r2a.at[slot], Y2, slot, at_y)

    def send_x2(slot):
        return remote(s1b.at[slot, 1 - x], r2b.at[slot], X2, slot, at_x)

    def send_outer(slot):
        return remote(s2.at[slot], rz.at[slot], OUTER, slot, at_inner)

    def send_middle(slot):
        return remote(sz.at[slot], rm.at[slot], MIDDLE, slot, at_middle)

    def send_final(slot, target):
        return remote(tot.at[slot], target, FINAL, slot, at_outer)

    def load(slot, source):
        return pltpu.make_async_copy(source, own.at[slot], sems.at[2 * LOCAL, slot])

    def load_ready(slot, source):
        return pltpu.make_async_copy(source, ready.at[slot], sems.at[2 * READY, slot])

    def save(slot, target):
        return pltpu.make_async_copy(tot.at[slot], target, sems.at[2 * LOCAL + 1, slot])

    def window(ref, j, tall):
        return pl.ds((j % tall) * high, high), pl.ds((j // tall) * WIDE, WIDE)

    def is_pre(k):
        return (k < 3 * pre) & (k % 3 == 2)

    def late_index(k):
        return jnp.where(k < 3 * pre, (k // 3) * 2 + k % 3, k - pre)

    def each(k, plan, parts, index, run):
        for (start, stop, tall), ref in zip(plan, parts):

            @pl.when((index >= start) & (index < stop))
            def _():
                run(ref, *window(ref, index - start, tall))

    def on_late(k, run):
        pl.when(jnp.logical_not(is_pre(k)))(run)

    def on_pre(k, run):
        pl.when(is_pre(k))(run)

    def add(left, right):
        return (left.astype(F32) + right.astype(F32)).astype(BF)

    def stage(k, run):
        @pl.when((k >= 0) & (k < total))
        def _():
            run(k, lax.rem(jnp.maximum(k, 0), slots))

    first = ins[0].at[:, core, pl.ds(0, high), pl.ds(0, WIDE)]
    final = outs[0].at[pl.ds(0, high), pl.ds(0, WIDE)]
    early = ins[whole].at[pl.ds(0, high), pl.ds(0, WIDE)]

    @pl.loop(0, total + 6 * lag)
    def _(t):
        def begin(k, slot):
            take_credit(CORE, k)

            def go():
                def run(ref, rows, columns):
                    send_core(slot, ref.at[:, 1 - core, rows, columns]).start()
                    load(slot, ref.at[:, core, rows, columns]).start()

                each(k, spans, ins[:whole], late_index(k), run)

            on_late(k, go)

        def add_core(k, slot):
            def go():
                load(slot, first).wait()
                send_core(slot, first).wait()
                both = add(own[slot], rc[slot])
                sc[slot] = both.reshape(2, 2, high, WIDE)

            on_late(k, go)
            give_credit(CORE, k, at_core)

        def add_one(k, slot):
            def go():
                send_x1(slot).wait()
                send_y1(slot).wait()
                s1a[slot] = add(sc[slot, :, x, :, :half], r1a[slot])
                s1b[slot] = add(sc[slot, y, :, :, half:], r1b[slot])

            on_late(k, go)
            give_credit(X1, k, at_x)
            give_credit(Y1, k, at_y)

        def add_two(k, slot):
            def go():
                send_y2(slot).wait()
                send_x2(slot).wait()
                s2[slot, :, :half] = add(s1a[slot, y], r2a[slot])
                s2[slot, :, half:] = add(s1b[slot, x], r2b[slot])

            def take():
                load_ready(slot, early).wait()
                s2[slot] = ready[slot]

            on_late(k, go)
            on_pre(k, take)
            give_credit(Y2, k, at_y)
            give_credit(X2, k, at_x)

        def add_outer(k, slot):
            @pl.when(outer)
            def _():
                send_outer(slot).wait_send()

            @pl.when(inner)
            def _():
                send_outer(slot).wait_recv()
                sz[slot] = add(s2[slot], rz[slot])
                give_credit(OUTER, k, at_outer)

        def add_middle(k, slot):
            @pl.when(inner)
            def _():
                send_middle(slot).wait()
                tot[slot] = add(sz[slot], rm[slot])
                give_credit(MIDDLE, k, at_middle)

        def finish(k, slot):
            @pl.when(inner)
            def _():
                save(slot, final).wait()
                send_final(slot, final).wait_send()

            @pl.when(outer)
            def _():
                send_final(slot, final).wait_recv()
                give_credit(FINAL, k, at_inner)

        def go_one(k, slot):
            take_credit(X1, k)
            take_credit(Y1, k)

            def go():
                send_x1(slot).start()
                send_y1(slot).start()

            on_late(k, go)

        def go_two(k, slot):
            take_credit(Y2, k)
            take_credit(X2, k)

            def go():
                send_y2(slot).start()
                send_x2(slot).start()

            def fetch():
                def run(ref, rows, columns):
                    load_ready(slot, ref.at[rows, columns]).start()

                each(k, pre_spans, ins[whole:], k // 3, run)

            on_late(k, go)
            on_pre(k, fetch)

        def go_outer(k, slot):
            @pl.when(outer)
            def _():
                take_credit(OUTER, k)
                send_outer(slot).start()

        def go_middle(k, slot):
            @pl.when(inner)
            def _():
                take_credit(MIDDLE, k)
                send_middle(slot).start()

        def go_final(k, slot):
            @pl.when(inner)
            def _():
                take_credit(FINAL, k)

                def run(ref, rows, columns):
                    save(slot, ref.at[rows, columns]).start()
                    send_final(slot, ref.at[rows, columns]).start()

                on_late(k, lambda: each(k, spans, outs[:whole], late_index(k), run))
                on_pre(k, lambda: each(k, pre_spans, outs[whole:], k // 3, run))

        stage(t, begin)
        stage(t - lag, add_core)
        stage(t - 2 * lag, add_one)
        stage(t - 3 * lag, add_two)
        stage(t - 4 * lag, add_outer)
        stage(t - 5 * lag, add_middle)
        stage(t - lag, go_one)
        stage(t - 2 * lag, go_two)
        stage(t - 3 * lag, go_outer)
        stage(t - 4 * lag, go_middle)
        stage(t - 5 * lag, go_final)
        stage(t - 6 * lag, finish)


def sum_grads(grads, pres, high=48, lag=2, slots=4):
    shapes = [(grad.shape[0] // 8, grad.shape[1]) for grad in grads]
    pre_shapes = [grad.shape for grad in pres]
    spans, late = sum_plan(shapes, high)
    pre_spans, pre = sum_plan(pre_shapes, high)
    half = WIDE // 2
    anywhere = pl.BlockSpec(memory_space=pl.ANY)
    blocks = [grad.reshape(4, 2, grad.shape[0] // 8, grad.shape[1]) for grad in grads]
    shapes = shapes + pre_shapes
    return pl.pallas_call(
        partial(sum_kernel, spans, pre_spans, late, pre, high, lag, slots),
        in_specs=[anywhere] * len(shapes),
        out_specs=[anywhere] * len(shapes),
        out_shape=[jax.ShapeDtypeStruct(shape, BF) for shape in shapes],
        scratch_shapes=[
            pltpu.VMEM((slots, 4, high, WIDE), BF),
            pltpu.VMEM((slots, 4, high, WIDE), BF),
            pltpu.VMEM((slots, 2, 2, high, WIDE), BF),
            pltpu.VMEM((slots, 2, high, half), BF),
            pltpu.VMEM((slots, 2, high, half), BF),
            pltpu.VMEM((slots, 2, high, half), BF),
            pltpu.VMEM((slots, 2, high, half), BF),
            pltpu.VMEM((slots, high, half), BF),
            pltpu.VMEM((slots, high, half), BF),
            pltpu.VMEM((slots, high, WIDE), BF),
            pltpu.VMEM((slots, high, WIDE), BF),
            pltpu.VMEM((slots, high, WIDE), BF),
            pltpu.VMEM((slots, high, WIDE), BF),
            pltpu.VMEM((slots, high, WIDE), BF),
            pltpu.VMEM((slots, high, WIDE), BF),
            pltpu.SemaphoreType.DMA((20, slots)),
            pltpu.SemaphoreType.REGULAR((8,)),
        ],
        compiler_params=pltpu.CompilerParams(collective_id=1, has_side_effects=True),
        name="sum_grads",
    )(*blocks, *pres)


def heads_first(weight, parts):
    rows = weight.shape[0]
    split = weight.reshape(rows, 3, parts, WIDE // parts)
    return split.transpose(0, 2, 1, 3).reshape(rows, 3 * WIDE)


def heads_last(weight, parts):
    rows = weight.shape[0]
    split = weight.reshape(rows, parts, 3, WIDE // parts)
    return split.transpose(0, 2, 1, 3).reshape(rows, 3 * WIDE)


def flat_small(small):
    return jnp.concatenate([piece.T.reshape(-1) for piece in small])


def gather_first(weight, shift):
    rows, columns = weight.shape
    tail = jnp.pad(shift[None], ((0, 7), (0, columns - shift.size)))
    both = jnp.concatenate([weight.astype(BF), tail.astype(BF)], axis=0)
    full = lax.all_gather(both, "dp", axis=0)
    return full[:, :rows].reshape(-1, columns), full[:, rows, : shift.size].reshape(-1).astype(F32)


def gather_middle(weights, small):
    pieces = []
    for weight in weights:
        low = weight.astype(BF)
        pieces += [low[:, start : start + WIDE] for start in range(0, low.shape[1], WIDE)]
    flat = flat_small(small).astype(BF)
    high = -(-flat.size // WIDE)
    high = -(-high // 8) * 8
    pieces.append(jnp.pad(flat, (0, high * WIDE - flat.size)).reshape(high, WIDE))
    full = lax.all_gather(jnp.concatenate(pieces, axis=0), "dp", axis=0)
    groups = full.shape[0]
    outs, at = [], 0
    for weight in weights:
        rows, columns = weight.shape
        blocks = columns // WIDE
        part = full[:, at : at + blocks * rows].reshape(groups, blocks, rows, WIDE)
        outs.append(part.transpose(0, 2, 1, 3).reshape(groups * rows, columns))
        at += blocks * rows
    table = full[:, at:].reshape(groups, -1).astype(F32)
    vectors, at = [], 0
    for piece in small:
        part = table[:, at : at + piece.size]
        if piece.ndim == 2:
            rows, columns = piece.shape
            part = part.reshape(groups, columns, rows).transpose(1, 0, 2)
            vectors.append(part.reshape(columns, groups * rows))
        else:
            vectors.append(part.reshape(-1))
        at += piece.size
    return outs, vectors


def pack_small(small, groups, multiple):
    pieces = []
    for piece in small:
        columns = piece if isinstance(piece, list) else [piece]
        pieces += [column.reshape(groups, -1) for column in columns]
    flat = jnp.concatenate(pieces, axis=1)
    high = -(-flat.shape[1] // WIDE)
    high = -(-high // multiple) * multiple
    flat = jnp.pad(flat.astype(BF), ((0, 0), (0, high * WIDE - flat.shape[1])))
    return flat.reshape(groups * high, WIDE)


def sum_grads_plain(grads, pres):
    outs = [lax.psum_scatter(grad, "dp", scatter_dimension=0, tiled=True) for grad in grads]
    return [lax.psum(part, "seq") for part in outs + list(pres)]


def reduce_grads(big, pres, small):
    groups = lax.axis_size("dp")
    ours = groups == 8 and lax.axis_size("seq") == 4
    grads = [grad.astype(BF) for grad in big] + [pack_small(small, groups, 48)]
    outs = sum_grads(grads, pres) if ours else sum_grads_plain(grads, pres)
    tail = outs[len(big)]
    sizes = []
    for piece in small:
        columns = piece if isinstance(piece, list) else [piece]
        sizes.append((len(columns), columns[0].size // groups, isinstance(piece, list)))
    used = -(-sum(many * size for many, size, _ in sizes) // WIDE)
    tail = tail[:used].astype(F32).reshape(-1)
    vectors, at = [], 0
    for many, size, matrix in sizes:
        part = tail[at : at + many * size]
        vectors.append(part.reshape(many, size).T if matrix else part)
        at += many * size
    bigs = [piece.astype(F32) for piece in outs[: len(big)]]
    return bigs, [piece.astype(F32) for piece in outs[len(big) + 1 :]], vectors


def scatter_sum(grad):
    return lax.psum_scatter(grad.astype(BF), "dp", scatter_dimension=0, tiled=True)


def body(
    tokens,
    chars,
    char_counts,
    lengths,
    perm,
    token_cot,
    char_cot,
    w_qkv,
    b_qv,
    w_out,
    w_in,
    b_in,
    w_back,
    gru_x,
    gru_h,
    gru_bias,
    blend_w,
    conv_w,
    conv_b,
    norm_gain,
    norm_bias,
    row_bias,
):
    parts = lax.axis_size("seq")
    seqs, local, width = tokens.shape
    rows = seqs * local
    per = width // HEAD // parts
    three = 3 * H
    masks = perm[:, 0]
    place = lax.axis_index("dp")
    own_lengths = lax.dynamic_slice(lengths, (place * seqs,), (seqs,))
    w_qkv, b_qv = gather_first(heads_first(w_qkv, parts), b_qv)
    middle = (gru_x, gru_h, w_out, w_in, w_back, blend_w)
    small = (b_in, gru_bias, conv_b, norm_gain, norm_bias, row_bias)
    middle, small = gather_middle(middle, small)
    gru_x, gru_h, w_out, w_in, w_back, blend_w = middle
    b_in, gru_bias, conv_b, norm_gain, norm_bias, row_bias = small
    conv_w = lax.all_gather(conv_w.astype(BF), "dp", axis=0, tiled=True)

    flat_tokens = tokens.reshape(rows, width)
    bias = jnp.concatenate([b_qv[:width], jnp.zeros((width,), F32), b_qv[width:]])
    bias = heads_first(bias[None], parts)[0]
    project = (dot_plain(flat_tokens, w_qkv) + bias).astype(BF)
    span = 3 * per * HEAD
    qkv = project.reshape(seqs, local, parts, span).transpose(2, 0, 1, 3)
    qkv = exchange(qkv)
    context = exchange(attention_forward(qkv, own_lengths, per))
    context = context.transpose(1, 2, 0, 3).reshape(rows, width)

    counts = char_counts.reshape(rows, 1)
    flat_chars = chars.transpose(2, 0, 1, 3).reshape(NCHAR * rows, width)
    gates = (dot_plain(flat_chars, gru_x) + gru_bias[0]).reshape(NCHAR, rows, 2 * three)
    sides = []
    for side in range(2):
        columns = slice(side * three, (side + 1) * three)
        state = jnp.zeros((rows, H), F32)
        steps = []
        for order in range(NCHAR):
            position = order if side == 0 else NCHAR - 1 - order
            live = position < counts
            low = state.astype(BF)
            recur = dot_plain(low, gru_h[:, columns]) + gru_bias[1, columns]
            steps.append((position, live, low, recur, state))
            state = gru_cell(live, gates[position, :, columns], recur, state)
        sides.append((state, steps))
    char_state = jnp.concatenate([sides[0][0], sides[1][0]], axis=-1)

    cots = jnp.concatenate([token_cot, char_cot], axis=-1)
    cots = relocate(masks, cots, (project, context, context))
    summed_first = flat_tokens.astype(F32) + dot_plain(context, w_out) + row_bias[0]
    hidden1 = norm_rows(summed_first, norm_gain[0], norm_bias[0])
    hidden1_low = hidden1.astype(BF)
    inner = dot_plain(hidden1_low, w_in) + b_in
    activated = gelu_exact(inner).astype(BF)
    summed_second = hidden1 + dot_plain(activated, w_back) + row_bias[1]
    hidden2 = norm_rows(summed_second, norm_gain[1], norm_bias[1])
    hidden2_low = hidden2.astype(BF)
    char_low = char_state.astype(BF)
    token_side = dot_plain(hidden2_low, blend_w[:, :width]) + row_bias[2]
    char_side = dot_plain(char_low, blend_w[:, width:]) + row_bias[3]
    joined = jnp.concatenate([token_side, char_side], axis=-1).astype(BF)
    joined = joined.reshape(seqs, local, 2 * width)
    taps = shifted(joined, *edges(joined))
    stacked = jnp.concatenate(taps, axis=-1)
    mixed = dot_plain(stacked, conv_w) + conv_b
    lifted = gelu_exact(mixed)
    token_pre = hidden2 + lifted[:, :width]
    char_pre = char_state + lifted[:, width:]
    token_out = norm_rows(token_pre, norm_gain[2], norm_bias[2]).astype(BF)
    char_out = norm_rows(char_pre, norm_gain[3], norm_bias[3]).astype(BF)
    outs = jnp.concatenate([token_out, char_out], axis=-1).reshape(seqs, local, 2 * width)

    flat_cots = cots.reshape(rows, 2 * width).astype(F32)
    d_token_pre, gain_token, shift_token = norm_back(
        token_pre, norm_gain[2], flat_cots[:, :width]
    )
    d_char_pre, gain_char, shift_char = norm_back(char_pre, norm_gain[3], flat_cots[:, width:])
    d_mixed = jnp.concatenate([d_token_pre, d_char_pre], axis=-1) * gelu_slope(mixed)
    d_mixed = d_mixed.astype(BF)
    grad_conv = dot_left(stacked, d_mixed).astype(BF)
    grad_conv, d_mixed = lax.optimization_barrier((grad_conv, d_mixed))
    sum_conv = scatter_sum(grad_conv)
    other, kept, moving = relocate_step(masks, outs, 0)
    other, kept, d_mixed = lax.optimization_barrier((other, kept, d_mixed))
    outs = jnp.where(moving, other, kept)
    beside = d_mixed.reshape(seqs, local, 2 * width)
    before, same, after = shifted(beside, *edges(beside))
    taps_w = conv_w.reshape(3, 2 * width, 2 * width)
    d_joined = dot_right(after, taps_w[0]) + dot_right(same, taps_w[1])
    d_joined = (d_joined + dot_right(before, taps_w[2])).astype(BF)
    d_token_side = d_joined[:, :width]
    d_char_side = d_joined[:, width:]
    grad_blend = jnp.concatenate(
        [dot_left(hidden2_low, d_token_side), dot_left(char_low, d_char_side)], axis=-1
    )
    grad_blend, d_token_side, d_char_side = lax.optimization_barrier(
        (grad_blend.astype(BF), d_token_side, d_char_side)
    )
    sum_blend = scatter_sum(grad_blend)
    d_hidden2 = d_token_pre + dot_right(d_token_side, blend_w[:, :width])
    d_char_state = d_char_pre + dot_right(d_char_side, blend_w[:, width:])

    d_second, gain_second, shift_second = norm_back(summed_second, norm_gain[1], d_hidden2)
    d_branch = d_second.astype(BF)
    grad_back = dot_left(activated, d_branch).astype(BF)
    grad_back, d_branch = lax.optimization_barrier((grad_back, d_branch))
    sum_back = scatter_sum(grad_back)
    d_inner = (dot_right(d_branch, w_back) * gelu_slope(inner)).astype(BF)
    grad_in = dot_left(hidden1_low, d_inner)
    d_hidden1 = d_second + dot_right(d_inner, w_in)
    d_first, gain_first, shift_first = norm_back(summed_first, norm_gain[0], d_hidden1)
    d_attend = d_first.astype(BF)
    other, kept, moving = relocate_step(masks, outs, 1)
    other, kept, d_attend = lax.optimization_barrier((other, kept, d_attend))
    outs = jnp.where(moving, other, kept)
    grad_out = dot_left(context, d_attend)
    d_context = dot_right(d_attend, w_out).astype(BF)
    d_context = d_context.reshape(seqs, local, parts, per * HEAD).transpose(2, 0, 1, 3)
    d_project = attention_backward(qkv, exchange(d_context), own_lengths, per)
    sum_conv, d_char_state, d_project = lax.optimization_barrier((sum_conv, d_char_state, d_project))
    d_project = exchange(d_project)
    sum_conv = line_sum(sum_conv, 0)
    d_project = d_project.transpose(1, 2, 0, 3).reshape(rows, 3 * width)

    d_gates = [[None, None] for _ in range(NCHAR)]
    grad_side, bias_side = [], []
    for side in range(2):
        columns = slice(side * three, (side + 1) * three)
        d_state = d_char_state[:, side * H : (side + 1) * H]
        lows, recurs = [], []
        for position, live, low, recur, state in reversed(sides[side][1]):
            _, pull = jax.vjp(
                partial(gru_cell, live), gates[position, :, columns], recur, state
            )
            d_gate, d_recur, d_keep = pull(d_state)
            d_recur = d_recur.astype(BF)
            lows.append(low)
            recurs.append(d_recur)
            d_state = d_keep + dot_right(d_recur, gru_h[:, columns])
            d_gates[position][side] = d_gate.astype(BF)
        lows, recurs = jnp.concatenate(lows, axis=0), jnp.concatenate(recurs, axis=0)
        if side == 0:
            sum_conv, recurs, d_char_state = lax.optimization_barrier(
                (sum_conv, recurs, d_char_state)
            )
            sum_conv = line_sum(sum_conv, 1)
        grad_side.append(dot_left(lows, recurs))
        bias_side.append(column_sum(recurs))
    d_gates = jnp.concatenate([jnp.concatenate(pair, axis=-1) for pair in d_gates], axis=0)
    sum_conv, d_gates = lax.optimization_barrier((sum_conv, d_gates))
    grad_gru_x = dot_left(flat_chars, d_gates)
    chars_back = dot_right(d_gates, gru_x).astype(BF)
    chars_back = chars_back.reshape(NCHAR, seqs, local, width).transpose(1, 2, 0, 3)
    grad_gru_h = jnp.concatenate(grad_side, axis=-1)
    grad_gru_bias = [column_sum(d_gates), jnp.concatenate(bias_side)]

    grad_qkv = dot_left(flat_tokens, d_project)
    sums = heads_last(column_sum(d_project)[None], parts)[0]
    grad_b_qv = jnp.concatenate([sums[:width], sums[2 * width :]])
    tokens_back = (d_first + dot_right(d_project, w_qkv)).astype(BF)
    big = (grad_in, grad_qkv, grad_gru_x, grad_gru_h, grad_out)
    small = (
        grad_b_qv,
        column_sum(d_inner),
        grad_gru_bias,
        column_sum(d_mixed),
        [gain_first, gain_second, gain_token, gain_char],
        [shift_first, shift_second, shift_token, shift_char],
        [
            column_sum(d_attend),
            column_sum(d_branch),
            column_sum(d_token_side),
            column_sum(d_char_side),
        ],
    )
    big, early, small = reduce_grads(big, (sum_back, sum_blend), small)
    other, kept, moving = relocate_step(masks, outs, 2)
    for bit in range(3, lax.axis_size("dp").bit_length() - 1):
        outs = jnp.where(moving, other, kept)
        other, kept, moving = relocate_step(masks, outs, bit)
    other, kept, _ = lax.optimization_barrier((other, kept, big[-1]))
    outs = jnp.where(moving, other, kept)
    g_in, g_qkv, g_gru_x, g_gru_h, g_out = big
    g_back, g_blend = early
    g_conv = line_sum(sum_conv, 2).astype(F32)
    g_b_qv, g_b_in, g_gru_bias, g_conv_b, g_gain, g_shift, g_rows = small
    return (
        outs[..., :width],
        outs[..., width:],
        tokens_back.reshape(seqs, local, width),
        chars_back,
        heads_last(g_qkv, parts),
        g_b_qv,
        g_out,
        g_in,
        g_b_in,
        g_back,
        g_gru_x,
        g_gru_h,
        g_gru_bias,
        g_blend,
        g_conv,
        g_conv_b,
        g_gain,
        g_shift,
        g_rows,
    )


def solution(mesh):
    rows, vector, seq = P("dp", None), P("dp"), P("dp", "seq", None)
    weights = (
        rows,
        vector,
        rows,
        rows,
        vector,
        rows,
        rows,
        rows,
        rows,
        rows,
        rows,
        vector,
        rows,
        rows,
        rows,
    )
    return jax.shard_map(
        body,
        mesh=mesh,
        in_specs=(seq, P("dp", "seq", None, None), P("dp", "seq"), P(), P(), seq, seq) + weights,
        out_specs=(seq, seq, seq, P("dp", "seq", None, None)) + weights,
        check_vma=False,
    )
```

```python
from functools import partial

import jax
import jax.numpy as jnp
from jax import lax
from jax.experimental import pallas as pl
from jax.experimental.pallas import tpu as pltpu
from jax.sharding import PartitionSpec as P

HEAD = 64
H = 384
NCHAR = 4
WIDE = 768
BF = jnp.bfloat16
F32 = jnp.float32


def dot_plain(left, right):
    return jnp.dot(left, right, preferred_element_type=F32)


def dot_left(left, right):
    return lax.dot_general(left, right, (((0,), (0,)), ((), ())), preferred_element_type=F32)


def dot_right(left, right):
    return lax.dot_general(left, right, (((1,), (1,)), ((), ())), preferred_element_type=F32)


def column_sum(values):
    return jnp.sum(values.astype(F32), axis=0)


def norm_rows(values, gain, shift):
    center = values - jnp.mean(values, axis=-1, keepdims=True)
    spread = jnp.mean(center * center, axis=-1, keepdims=True)
    rstd = lax.rsqrt(spread + 1e-06)
    return center * rstd * gain + shift


def norm_back(values, gain, grad):
    center = values - jnp.mean(values, axis=-1, keepdims=True)
    spread = jnp.mean(center * center, axis=-1, keepdims=True)
    rstd = lax.rsqrt(spread + 1e-06)
    hat = center * rstd
    lead = grad * gain
    back = rstd * (
        lead
        - jnp.mean(lead, axis=-1, keepdims=True)
        - hat * jnp.mean(lead * hat, axis=-1, keepdims=True)
    )
    return back, jnp.sum(grad * hat, axis=0), jnp.sum(grad, axis=0)


def gelu_both(values):
    cdf = 0.5 * (1.0 + lax.erf(values * (0.5**0.5)))
    pdf = jnp.exp(-0.5 * values * values) * 0.3989422804014327
    return values * cdf, cdf + values * pdf


def gru_order(side):
    return range(NCHAR) if side == 0 else range(NCHAR - 1, -1, -1)


def gru_cell(live, gates, recur, state):
    width = state.shape[-1]
    reset = jax.nn.sigmoid(gates[:, :width] + recur[:, :width])
    update = jax.nn.sigmoid(gates[:, width : 2 * width] + recur[:, width : 2 * width])
    fresh = jnp.tanh(gates[:, 2 * width :] + reset * recur[:, 2 * width :])
    after = jnp.where(live, (1.0 - update) * fresh + update * state, state)
    return reset, update, fresh, after


def gru_forward_kernel(count_ref, chars_ref, x_ref, h_ref, bias_ref, out_ref, gate_ref):
    rows = chars_ref.shape[1]
    three = 3 * H
    counts = jnp.broadcast_to(count_ref[...], (rows, H))
    chars = chars_ref[...].reshape(NCHAR * rows, chars_ref.shape[2])
    for side in range(2):
        columns = slice(side * three, (side + 1) * three)
        gate_ref[...] = dot_plain(chars, x_ref[:, columns]) + bias_ref[0:1, columns]
        state = jnp.zeros((rows, H), F32)
        for position in gru_order(side):
            recur = dot_plain(state.astype(BF), h_ref[:, columns]) + bias_ref[1:2, columns]
            gates = gate_ref[position * rows : (position + 1) * rows, :]
            state = gru_cell(position < counts, gates, recur, state)[3]
        out_ref[:, side * H : (side + 1) * H] = state


def gru_specs(high, width):
    three = 3 * H
    return [
        pl.BlockSpec((high, 1), lambda i: (i, 0)),
        pl.BlockSpec((NCHAR, high, width), lambda i: (0, i, 0)),
        pl.BlockSpec((width, 2 * three), lambda i: (0, 0)),
        pl.BlockSpec((H, 2 * three), lambda i: (0, 0)),
        pl.BlockSpec((2, 2 * three), lambda i: (0, 0)),
    ]


def gru_forward(counts, chars, gru_x, gru_h, gru_bias, high=256):
    rows, width = chars.shape[1:]
    products = NCHAR * rows * (width + H) * 6 * H
    return pl.pallas_call(
        gru_forward_kernel,
        grid=(rows // high,),
        in_specs=gru_specs(high, width),
        out_specs=pl.BlockSpec((high, 2 * H), lambda i: (i, 0)),
        out_shape=jax.ShapeDtypeStruct((rows, 2 * H), F32),
        scratch_shapes=[pltpu.VMEM((NCHAR * high, 3 * H), F32)],
        cost_estimate=pl.CostEstimate(
            flops=2 * products, bytes_accessed=10_000_000, transcendentals=24 * rows * H
        ),
        name="gru_forward",
    )(counts, chars, gru_x, gru_h, gru_bias)


def gru_backward_kernel(
    count_ref,
    chars_ref,
    x_ref,
    h_ref,
    bias_ref,
    grad_ref,
    gates_out,
    h_out,
    bias_out,
    gate_ref,
    keep_ref,
    state_ref,
    low_ref,
    recur_ref,
    total_ref,
):
    rows = chars_ref.shape[1]
    three = 3 * H
    counts = jnp.broadcast_to(count_ref[...], (rows, H))
    chars = chars_ref[...].reshape(NCHAR * rows, chars_ref.shape[2])

    @pl.when(pl.program_id(0) == 0)
    def _():
        bias_out[...] = jnp.zeros_like(bias_out)
        total_ref[...] = jnp.zeros_like(total_ref)

    for side in range(2):
        columns = slice(side * three, (side + 1) * three)
        gate_ref[...] = dot_plain(chars, x_ref[:, columns]) + bias_ref[0:1, columns]
        state = jnp.zeros((rows, H), F32)
        for position in gru_order(side):
            part = slice(position * rows, (position + 1) * rows)
            low = state.astype(BF)
            low_ref[part, :] = low
            state_ref[part, :] = state
            recur = dot_plain(low, h_ref[:, columns]) + bias_ref[1:2, columns]
            keep_ref[part, :] = recur[:, 2 * H :]
            reset, update, fresh, state = gru_cell(
                position < counts, gate_ref[part, :], recur, state
            )
            gate_ref[part, :H] = reset
            gate_ref[part, H : 2 * H] = update
            gate_ref[part, 2 * H :] = fresh
        grad = grad_ref[:, side * H : (side + 1) * H]
        gate_sum = jnp.zeros((1, three), F32)
        recur_sum = jnp.zeros((1, three), F32)
        for position in reversed(gru_order(side)):
            part = slice(position * rows, (position + 1) * rows)
            live = position < counts
            reset = gate_ref[part, :H]
            update = gate_ref[part, H : 2 * H]
            fresh = gate_ref[part, 2 * H :]
            moved = jnp.where(live, grad, 0.0)
            d_fresh = moved * (1.0 - update) * (1.0 - fresh * fresh)
            d_update = moved * (state_ref[part, :] - fresh) * update * (1.0 - update)
            d_reset = d_fresh * keep_ref[part, :] * reset * (1.0 - reset)
            d_gate = jnp.concatenate([d_reset, d_update, d_fresh], axis=-1).astype(BF)
            d_recur = jnp.concatenate([d_reset, d_update, d_fresh * reset], axis=-1).astype(BF)
            gates_out[position, :, columns] = d_gate
            recur_ref[part, :] = d_recur
            gate_sum += jnp.sum(d_gate.astype(F32), axis=0, keepdims=True)
            recur_sum += jnp.sum(d_recur.astype(F32), axis=0, keepdims=True)
            grad = jnp.where(live, moved * update, grad) + dot_right(d_recur, h_ref[:, columns])
        bias_out[0:1, columns] += gate_sum
        bias_out[1:2, columns] += recur_sum
        total_ref[:, columns] += dot_left(low_ref[...], recur_ref[...])

    @pl.when(pl.program_id(0) == pl.num_programs(0) - 1)
    def _():
        h_out[...] = total_ref[...].astype(BF)


def gru_backward(counts, chars, gru_x, gru_h, gru_bias, grad, high=256):
    rows, width = chars.shape[1:]
    three = 3 * H
    products = NCHAR * rows * (width + 3 * H) * 6 * H
    return pl.pallas_call(
        gru_backward_kernel,
        grid=(rows // high,),
        in_specs=gru_specs(high, width) + [pl.BlockSpec((high, 2 * H), lambda i: (i, 0))],
        out_specs=[
            pl.BlockSpec((NCHAR, high, 2 * three), lambda i: (0, i, 0)),
            pl.BlockSpec((H, 2 * three), lambda i: (0, 0)),
            pl.BlockSpec((2, 2 * three), lambda i: (0, 0)),
        ],
        out_shape=[
            jax.ShapeDtypeStruct((NCHAR, rows, 2 * three), BF),
            jax.ShapeDtypeStruct((H, 2 * three), BF),
            jax.ShapeDtypeStruct((2, 2 * three), F32),
        ],
        scratch_shapes=[
            pltpu.VMEM((NCHAR * high, three), F32),
            pltpu.VMEM((NCHAR * high, H), F32),
            pltpu.VMEM((NCHAR * high, H), F32),
            pltpu.VMEM((NCHAR * high, H), BF),
            pltpu.VMEM((NCHAR * high, three), BF),
            pltpu.VMEM((H, 2 * three), F32),
        ],
        cost_estimate=pl.CostEstimate(
            flops=2 * products, bytes_accessed=30_000_000, transcendentals=24 * rows * H
        ),
        name="gru_backward",
    )(counts, chars, gru_x, gru_h, gru_bias, grad)


def attention_forward_kernel(per, len_ref, qkv_ref, out_ref):
    block = pl.program_id(1)
    length = len_ref[pl.program_id(0)]
    span = per * HEAD
    total = qkv_ref.shape[0] * qkv_ref.shape[2]
    rows = qkv_ref.shape[2]
    q_all = qkv_ref[block, 0, :, :span] * BF(HEAD ** (-0.5))
    k_all = qkv_ref[:, 0, :, span : 2 * span].reshape(total, span)
    v_all = qkv_ref[:, 0, :, 2 * span :].reshape(total, span)
    valid = lax.broadcasted_iota(jnp.int32, (rows, total), 1) < length
    pieces = []
    for j in range(per):
        part = slice(j * HEAD, (j + 1) * HEAD)
        scores = jnp.where(valid, dot_right(q_all[:, part], k_all[:, part]), -1e30)
        raised = jnp.exp(scores - jnp.max(scores, axis=-1, keepdims=True))
        share = 1.0 / jnp.sum(raised, axis=-1, keepdims=True)
        probs = (raised * share).astype(BF)
        pieces.append(dot_plain(probs, v_all[:, part]))
    out_ref[0, 0] = jnp.concatenate(pieces, axis=-1).astype(BF)


def attention_forward(qkv, lengths, per):
    seqs, rows = qkv.shape[1], qkv.shape[2]
    parts = qkv.shape[0]
    span = per * HEAD
    return pl.pallas_call(
        partial(attention_forward_kernel, per),
        grid_spec=pltpu.PrefetchScalarGridSpec(
            num_scalar_prefetch=1,
            grid=(seqs, parts),
            in_specs=[pl.BlockSpec((parts, 1, rows, 3 * span), lambda m, b, n: (0, m, 0, 0))],
            out_specs=pl.BlockSpec((1, 1, rows, span), lambda m, b, n: (b, m, 0, 0)),
        ),
        out_shape=jax.ShapeDtypeStruct((parts, seqs, rows, span), BF),
        name="attend_forward",
    )(lengths, qkv)


def attention_backward_kernel(per, len_ref, qkv_ref, grad_ref, out_ref, key_acc, value_acc):
    block = pl.program_id(1)
    length = len_ref[pl.program_id(0)]
    span = per * HEAD
    parts, rows = qkv_ref.shape[0], qkv_ref.shape[2]
    total = parts * rows
    scale = HEAD ** (-0.5)

    @pl.when(block == 0)
    def _():
        key_acc[...] = jnp.zeros_like(key_acc)
        value_acc[...] = jnp.zeros_like(value_acc)

    q_all = qkv_ref[block, 0, :, :span] * BF(scale)
    g_all = grad_ref[block, 0]
    k_all = qkv_ref[:, 0, :, span : 2 * span].reshape(total, span)
    v_all = qkv_ref[:, 0, :, 2 * span :].reshape(total, span)
    valid = lax.broadcasted_iota(jnp.int32, (total, rows), 0) < length
    q_pieces, k_pieces, v_pieces = [], [], []
    for j in range(per):
        part = slice(j * HEAD, (j + 1) * HEAD)
        q, g, k, v = q_all[:, part], g_all[:, part], k_all[:, part], v_all[:, part]
        scores = jnp.where(valid, dot_right(k, q), -1e30)
        raised = jnp.exp(scores - jnp.max(scores, axis=0, keepdims=True))
        probs = raised * (1.0 / jnp.sum(raised, axis=0, keepdims=True))
        d_probs = dot_right(v, g)
        delta = jnp.sum(d_probs * probs, axis=0, keepdims=True)
        d_scores = (probs * (d_probs - delta)).astype(BF)
        q_pieces.append(dot_left(d_scores, k) * scale)
        k_pieces.append(dot_plain(d_scores, q))
        v_pieces.append(dot_plain(probs.astype(BF), g))
    out_ref[block, 0, :, :span] = jnp.concatenate(q_pieces, axis=-1).astype(BF)
    key_acc[...] += jnp.concatenate(k_pieces, axis=-1)
    value_acc[...] += jnp.concatenate(v_pieces, axis=-1)

    @pl.when(block == parts - 1)
    def _():
        out_ref[:, 0, :, span : 2 * span] = key_acc[...].astype(BF).reshape(parts, rows, span)
        out_ref[:, 0, :, 2 * span :] = value_acc[...].astype(BF).reshape(parts, rows, span)


def attention_backward(qkv, grads, lengths, per):
    parts, seqs, rows, _ = qkv.shape
    span = per * HEAD
    return pl.pallas_call(
        partial(attention_backward_kernel, per),
        grid_spec=pltpu.PrefetchScalarGridSpec(
            num_scalar_prefetch=1,
            grid=(seqs, parts),
            in_specs=[
                pl.BlockSpec((parts, 1, rows, 3 * span), lambda m, b, n: (0, m, 0, 0)),
                pl.BlockSpec((parts, 1, rows, span), lambda m, b, n: (0, m, 0, 0)),
            ],
            out_specs=pl.BlockSpec((parts, 1, rows, 3 * span), lambda m, b, n: (0, m, 0, 0)),
            scratch_shapes=[
                pltpu.VMEM((parts * rows, span), F32),
                pltpu.VMEM((parts * rows, span), F32),
            ],
        ),
        out_shape=jax.ShapeDtypeStruct(qkv.shape, BF),
        name="attend_backward",
    )(lengths, qkv, grads)


def exchange(blocks):
    return lax.all_to_all(blocks, "seq", split_axis=0, concat_axis=0)


def relocate_begin(pair, step):
    count = lax.axis_size("dp")
    levels = count.bit_length() - 1
    bits = (step, step if step == 0 else levels - step)
    others = []
    for value, bit in zip(pair, bits):
        apart = 1 << bit
        pairs = [(source, source ^ apart) for source in range(count)]
        others.append(lax.ppermute(value, "dp", pairs))
    return bits, tuple(others)


def relocate_end(masks, pair, begun):
    done = []
    for value, bit, other in zip(pair, *begun):
        moving = (jnp.bitwise_and(masks, 1 << bit) != 0)[:, None, None]
        done.append(jnp.where(moving, other, value))
    return tuple(done)


def relocate_one(masks, pair, step, tie):
    bits, others = relocate_begin(pair, step)
    others, pair, tie = lax.optimization_barrier((others, pair, tie))
    return relocate_end(masks, pair, (bits, others)), tie


def relocate_last(masks, pair, first, tie):
    levels = lax.axis_size("dp").bit_length() - 1
    for step in range(first, levels):
        bits, others = relocate_begin(pair, step)
        if step == levels - 1:
            others, pair, _ = lax.optimization_barrier((others, pair, tie))
        pair = relocate_end(masks, pair, (bits, others))
    return pair


def edges(block):
    count = lax.axis_size("seq")
    forward = [(i, i + 1) for i in range(count - 1)]
    backward = [(target, source) for source, target in forward]
    low = lax.ppermute(block[:, -1:], "seq", forward)
    high = lax.ppermute(block[:, :1], "seq", backward)
    return low, high


LINE = ([(0, 1), (3, 2)], [(1, 2), (2, 1)], [(1, 0), (2, 3)])


def line_sum(value, step):
    if lax.axis_size("seq") != 4:
        return lax.psum(value, "seq") if step == 0 else value
    other = lax.ppermute(value, "seq", LINE[step])
    if step < 2:
        return value + other
    return jnp.where((lax.axis_index("seq") % 3) == 0, other, value)


def shifted(block, low, high):
    before = jnp.concatenate([low, block[:, :-1]], axis=1)
    after = jnp.concatenate([block[:, 1:], high], axis=1)
    flat = (-1, block.shape[-1])
    return before.reshape(flat), block.reshape(flat), after.reshape(flat)


def sum_plan(shapes, high):
    spans, start = [], 0
    for rows, columns in shapes:
        tall = rows // high
        count = tall * (columns // WIDE)
        spans.append((start, start + count, tall))
        start += count
    return spans, start


def sum_kernel(spans, pre_spans, late, pre, high, lag, slots, *refs):
    whole = len(spans)
    count = whole + len(pre_spans)
    total = late + pre
    ins, outs = refs[:count], refs[count : 2 * count]
    own, rc, sc, s1a, s1b, r1a, r1b, r2a, r2b, s2, rz, sz, rm, tot, ready = refs[
        2 * count : 2 * count + 15
    ]
    sems = refs[2 * count + 15]
    credits = refs[2 * count + 16]
    half = WIDE // 2
    dp, z = lax.axis_index("dp"), lax.axis_index("seq")
    core, x, y = dp % 2, (dp // 2) % 2, dp // 4
    at_core = {"dp": dp + 1 - 2 * core}
    at_x = {"dp": dp + 2 - 4 * x}
    at_y = {"dp": dp + 4 - 8 * y}
    outer = (z % 3) == 0
    inner = (z % 3) != 0
    at_inner = {"seq": 1 + z // 3}
    at_middle = {"seq": (3 - z) % 4}
    at_outer = {"seq": (z // 2) * 3}

    barrier = pltpu.get_barrier_semaphore()

    def greet(where):
        pl.semaphore_signal(barrier, inc=1, device_id=where, device_id_type=pl.DeviceIdType.MESH)

    greet(at_core)
    greet(at_x)
    greet(at_y)

    @pl.when(outer)
    def _():
        greet(at_inner)
        pl.semaphore_wait(barrier, 4)

    @pl.when(inner)
    def _():
        greet(at_middle)
        greet(at_outer)
        pl.semaphore_wait(barrier, 5)

    def remote(source, target, name, slot, where):
        return pltpu.make_async_remote_copy(
            src_ref=source,
            dst_ref=target,
            send_sem=sems.at[2 * name, slot],
            recv_sem=sems.at[2 * name + 1, slot],
            device_id=where,
            device_id_type=pl.DeviceIdType.MESH,
        )

    CORE, X1, Y1, X2, Y2, OUTER, MIDDLE, FINAL, LOCAL, READY = range(10)

    def give_credit(name, k, where):
        @pl.when(k + slots < total)
        def _():
            pl.semaphore_signal(
                credits.at[name], inc=1, device_id=where, device_id_type=pl.DeviceIdType.MESH
            )

    def take_credit(name, k):
        @pl.when(k >= slots)
        def _():
            pl.semaphore_wait(credits.at[name], 1)

    def send_core(slot, source):
        return remote(source, rc.at[slot], CORE, slot, at_core)

    def send_x1(slot):
        return remote(sc.at[slot, :, 1 - x, :, :half], r1a.at[slot], X1, slot, at_x)

    def send_y1(slot):
        return remote(sc.at[slot, 1 - y, :, :, half:], r1b.at[slot], Y1, slot, at_y)

    def send_y2(slot):
        return remote(s1a.at[slot, 1 - y], r2a.at[slot], Y2, slot, at_y)

    def send_x2(slot):
        return remote(s1b.at[slot, 1 - x], r2b.at[slot], X2, slot, at_x)

    def send_outer(slot):
        return remote(s2.at[slot], rz.at[slot], OUTER, slot, at_inner)

    def send_middle(slot):
        return remote(sz.at[slot], rm.at[slot], MIDDLE, slot, at_middle)

    def send_final(slot, target):
        return remote(tot.at[slot], target, FINAL, slot, at_outer)

    def load(slot, source):
        return pltpu.make_async_copy(source, own.at[slot], sems.at[2 * LOCAL, slot])

    def load_ready(slot, source):
        return pltpu.make_async_copy(source, ready.at[slot], sems.at[2 * READY, slot])

    def save(slot, target):
        return pltpu.make_async_copy(tot.at[slot], target, sems.at[2 * LOCAL + 1, slot])

    def window(ref, j, tall):
        return pl.ds((j % tall) * high, high), pl.ds((j // tall) * WIDE, WIDE)

    def is_pre(k):
        return (k < 3 * pre) & (k % 3 == 2)

    def late_index(k):
        return jnp.where(k < 3 * pre, (k // 3) * 2 + k % 3, k - pre)

    def each(k, plan, parts, index, run):
        for (start, stop, tall), ref in zip(plan, parts):

            @pl.when((index >= start) & (index < stop))
            def _():
                run(ref, *window(ref, index - start, tall))

    def on_late(k, run):
        pl.when(jnp.logical_not(is_pre(k)))(run)

    def on_pre(k, run):
        pl.when(is_pre(k))(run)

    def add(left, right):
        return (left.astype(F32) + right.astype(F32)).astype(BF)

    def stage(k, run):
        @pl.when((k >= 0) & (k < total))
        def _():
            run(k, lax.rem(jnp.maximum(k, 0), slots))

    first = ins[0].at[:, core, pl.ds(0, high), pl.ds(0, WIDE)]
    final = outs[0].at[pl.ds(0, high), pl.ds(0, WIDE)]
    early = ins[whole].at[pl.ds(0, high), pl.ds(0, WIDE)]

    @pl.loop(0, total + 6 * lag)
    def _(t):
        def begin(k, slot):
            take_credit(CORE, k)

            def go():
                def run(ref, rows, columns):
                    send_core(slot, ref.at[:, 1 - core, rows, columns]).start()
                    load(slot, ref.at[:, core, rows, columns]).start()

                each(k, spans, ins[:whole], late_index(k), run)

            on_late(k, go)

        def add_core(k, slot):
            def go():
                load(slot, first).wait()
                send_core(slot, first).wait()
                both = add(own[slot], rc[slot])
                sc[slot] = both.reshape(2, 2, high, WIDE)

            on_late(k, go)
            give_credit(CORE, k, at_core)

        def add_one(k, slot):
            def go():
                send_x1(slot).wait()
                send_y1(slot).wait()
                s1a[slot] = add(sc[slot, :, x, :, :half], r1a[slot])
                s1b[slot] = add(sc[slot, y, :, :, half:], r1b[slot])

            on_late(k, go)
            give_credit(X1, k, at_x)
            give_credit(Y1, k, at_y)

        def add_two(k, slot):
            def go():
                send_y2(slot).wait()
                send_x2(slot).wait()
                s2[slot, :, :half] = add(s1a[slot, y], r2a[slot])
                s2[slot, :, half:] = add(s1b[slot, x], r2b[slot])

            def take():
                load_ready(slot, early).wait()
                s2[slot] = ready[slot]

            on_late(k, go)
            on_pre(k, take)
            give_credit(Y2, k, at_y)
            give_credit(X2, k, at_x)

        def add_outer(k, slot):
            @pl.when(outer)
            def _():
                send_outer(slot).wait_send()

            @pl.when(inner)
            def _():
                send_outer(slot).wait_recv()
                sz[slot] = add(s2[slot], rz[slot])
                give_credit(OUTER, k, at_outer)

        def add_middle(k, slot):
            @pl.when(inner)
            def _():
                send_middle(slot).wait()
                tot[slot] = add(sz[slot], rm[slot])
                give_credit(MIDDLE, k, at_middle)

        def finish(k, slot):
            @pl.when(inner)
            def _():
                save(slot, final).wait()
                send_final(slot, final).wait_send()

            @pl.when(outer)
            def _():
                send_final(slot, final).wait_recv()
                give_credit(FINAL, k, at_inner)

        def go_one(k, slot):
            take_credit(X1, k)
            take_credit(Y1, k)

            def go():
                send_x1(slot).start()
                send_y1(slot).start()

            on_late(k, go)

        def go_two(k, slot):
            take_credit(Y2, k)
            take_credit(X2, k)

            def go():
                send_y2(slot).start()
                send_x2(slot).start()

            def fetch():
                def run(ref, rows, columns):
                    load_ready(slot, ref.at[rows, columns]).start()

                each(k, pre_spans, ins[whole:], k // 3, run)

            on_late(k, go)
            on_pre(k, fetch)

        def go_outer(k, slot):
            @pl.when(outer)
            def _():
                take_credit(OUTER, k)
                send_outer(slot).start()

        def go_middle(k, slot):
            @pl.when(inner)
            def _():
                take_credit(MIDDLE, k)
                send_middle(slot).start()

        def go_final(k, slot):
            @pl.when(inner)
            def _():
                take_credit(FINAL, k)

                def run(ref, rows, columns):
                    save(slot, ref.at[rows, columns]).start()
                    send_final(slot, ref.at[rows, columns]).start()

                on_late(k, lambda: each(k, spans, outs[:whole], late_index(k), run))
                on_pre(k, lambda: each(k, pre_spans, outs[whole:], k // 3, run))

        stage(t, begin)
        stage(t - lag, add_core)
        stage(t - 2 * lag, add_one)
        stage(t - 3 * lag, add_two)
        stage(t - 4 * lag, add_outer)
        stage(t - 5 * lag, add_middle)
        stage(t - lag, go_one)
        stage(t - 2 * lag, go_two)
        stage(t - 3 * lag, go_outer)
        stage(t - 4 * lag, go_middle)
        stage(t - 5 * lag, go_final)
        stage(t - 6 * lag, finish)


def sum_grads(grads, pres, high=48, lag=3, slots=6):
    shapes = [(grad.shape[0] // 8, grad.shape[1]) for grad in grads]
    pre_shapes = [grad.shape for grad in pres]
    spans, late = sum_plan(shapes, high)
    pre_spans, pre = sum_plan(pre_shapes, high)
    half = WIDE // 2
    anywhere = pl.BlockSpec(memory_space=pl.ANY)
    blocks = [grad.reshape(4, 2, grad.shape[0] // 8, grad.shape[1]) for grad in grads]
    shapes = shapes + pre_shapes
    return pl.pallas_call(
        partial(sum_kernel, spans, pre_spans, late, pre, high, lag, slots),
        in_specs=[anywhere] * len(shapes),
        out_specs=[anywhere] * len(shapes),
        out_shape=[jax.ShapeDtypeStruct(shape, BF) for shape in shapes],
        scratch_shapes=[
            pltpu.VMEM((slots, 4, high, WIDE), BF),
            pltpu.VMEM((slots, 4, high, WIDE), BF),
            pltpu.VMEM((slots, 2, 2, high, WIDE), BF),
            pltpu.VMEM((slots, 2, high, half), BF),
            pltpu.VMEM((slots, 2, high, half), BF),
            pltpu.VMEM((slots, 2, high, half), BF),
            pltpu.VMEM((slots, 2, high, half), BF),
            pltpu.VMEM((slots, high, half), BF),
            pltpu.VMEM((slots, high, half), BF),
            pltpu.VMEM((slots, high, WIDE), BF),
            pltpu.VMEM((slots, high, WIDE), BF),
            pltpu.VMEM((slots, high, WIDE), BF),
            pltpu.VMEM((slots, high, WIDE), BF),
            pltpu.VMEM((slots, high, WIDE), BF),
            pltpu.VMEM((slots, high, WIDE), BF),
            pltpu.SemaphoreType.DMA((20, slots)),
            pltpu.SemaphoreType.REGULAR((8,)),
        ],
        compiler_params=pltpu.CompilerParams(collective_id=1, has_side_effects=True),
        name="sum_grads",
    )(*blocks, *pres)


def heads_first(weight, parts):
    rows = weight.shape[0]
    split = weight.reshape(rows, 3, parts, WIDE // parts)
    return split.transpose(0, 2, 1, 3).reshape(rows, 3 * WIDE)


def heads_last(weight, parts):
    rows = weight.shape[0]
    split = weight.reshape(rows, parts, 3, WIDE // parts)
    return split.transpose(0, 2, 1, 3).reshape(rows, 3 * WIDE)


def flat_small(small):
    return jnp.concatenate([piece.T.reshape(-1) for piece in small])


def gather_packed(weights, small, wide):
    return unpack(pack(weights, small, wide), weights, small, wide)


def pack(weights, small, wide):
    pieces = []
    for weight in weights:
        low = weight.astype(BF)
        pieces += [low[:, start : start + wide] for start in range(0, low.shape[1], wide)]
    flat = flat_small(small).astype(BF)
    high = -(-flat.size // wide)
    high = -(-high // 8) * 8
    pieces.append(jnp.pad(flat, (0, high * wide - flat.size)).reshape(high, wide))
    return lax.all_gather(jnp.concatenate(pieces, axis=0), "dp", axis=0)


def unpack(full, weights, small, wide):
    groups = full.shape[0]
    outs, at = [], 0
    for weight in weights:
        rows, columns = weight.shape
        blocks = columns // wide
        part = full[:, at : at + blocks * rows].reshape(groups, blocks, rows, wide)
        outs.append(part.transpose(0, 2, 1, 3).reshape(groups * rows, columns))
        at += blocks * rows
    used = -(-sum(piece.size for piece in small) // wide)
    table = full[:, at : at + used].astype(F32).reshape(groups, -1)
    vectors, at = [], 0
    for piece in small:
        part = table[:, at : at + piece.size]
        if piece.ndim == 2:
            rows, columns = piece.shape
            part = part.reshape(groups, columns, rows).transpose(1, 0, 2)
            vectors.append(part.reshape(columns, groups * rows))
        else:
            vectors.append(part.reshape(-1))
        at += piece.size
    return outs, vectors


def pack_small(small, groups, multiple):
    pieces = []
    for piece in small:
        columns = piece if isinstance(piece, list) else [piece]
        pieces += [column.reshape(groups, -1) for column in columns]
    flat = jnp.concatenate(pieces, axis=1)
    high = -(-flat.shape[1] // WIDE)
    high = -(-high // multiple) * multiple
    flat = jnp.pad(flat.astype(BF), ((0, 0), (0, high * WIDE - flat.shape[1])))
    return flat.reshape(groups * high, WIDE)


def sum_grads_plain(grads, pres):
    outs = [lax.psum_scatter(grad, "dp", scatter_dimension=0, tiled=True) for grad in grads]
    return [lax.psum(part, "seq") for part in outs + list(pres)]


def reduce_grads(big, pres, small):
    groups = lax.axis_size("dp")
    ours = groups == 8 and lax.axis_size("seq") == 4
    grads = [grad.astype(BF) for grad in big] + [pack_small(small, groups, 48)]
    outs = sum_grads(grads, pres) if ours else sum_grads_plain(grads, pres)
    tail = outs[len(big)]
    sizes = []
    for piece in small:
        columns = piece if isinstance(piece, list) else [piece]
        sizes.append((len(columns), columns[0].size // groups, isinstance(piece, list)))
    used = -(-sum(many * size for many, size, _ in sizes) // WIDE)
    tail = tail[:used].astype(F32).reshape(-1)
    vectors, at = [], 0
    for many, size, matrix in sizes:
        part = tail[at : at + many * size]
        vectors.append(part.reshape(many, size).T if matrix else part)
        at += many * size
    bigs = [piece.astype(F32) for piece in outs[: len(big)]]
    return bigs, [piece.astype(F32) for piece in outs[len(big) + 1 :]], vectors


def scatter_sum(grad):
    return lax.psum_scatter(grad.astype(BF), "dp", scatter_dimension=0, tiled=True)


def body(
    tokens,
    chars,
    char_counts,
    lengths,
    perm,
    token_cot,
    char_cot,
    w_qkv,
    b_qv,
    w_out,
    w_in,
    b_in,
    w_back,
    gru_x,
    gru_h,
    gru_bias,
    blend_w,
    conv_w,
    conv_b,
    norm_gain,
    norm_bias,
    row_bias,
):
    parts = lax.axis_size("seq")
    seqs, local, width = tokens.shape
    rows = seqs * local
    per = width // HEAD // parts
    three = 3 * H
    masks = perm[:, 0]
    place = lax.axis_index("dp")
    own_lengths = lax.dynamic_slice(lengths, (place * seqs,), (seqs,))
    first = (heads_first(w_qkv, parts), gru_x, gru_h)
    (w_qkv, gru_x, gru_h), (b_qv, gru_bias) = gather_packed(first, (b_qv, gru_bias), 3 * width)
    middle = (w_out, w_in, w_back, blend_w)
    small = (b_in, conv_b, norm_gain, norm_bias, row_bias)
    packed = pack(middle, small, width)
    conv_w = lax.all_gather(conv_w.astype(BF), "dp", axis=0, tiled=True)

    flat_tokens = tokens.reshape(rows, width)
    counts = char_counts.reshape(rows, 1)
    row_chars = chars.transpose(2, 0, 1, 3).reshape(NCHAR, rows, width)
    flat_chars = row_chars.reshape(NCHAR * rows, width)
    bias = jnp.concatenate([b_qv[:width], jnp.zeros((width,), F32), b_qv[width:]])
    bias = heads_first(bias[None], parts)[0]
    project = (dot_plain(flat_tokens, w_qkv) + bias).astype(BF)
    cots = (token_cot, char_cot)
    cots, project = relocate_one(masks, cots, 0, project)
    project, row_chars = lax.optimization_barrier((project, row_chars))
    span = 3 * per * HEAD
    qkv = project.reshape(seqs, local, parts, span).transpose(2, 0, 1, 3)
    qkv = exchange(qkv)
    char_state = gru_forward(counts, row_chars, gru_x, gru_h, gru_bias)
    qkv, char_state = lax.optimization_barrier((qkv, char_state))
    context = attention_forward(qkv, own_lengths, per)
    context, packed = lax.optimization_barrier((context, packed))
    middle, small = unpack(packed, middle, small, width)
    w_out, w_in, w_back, blend_w = middle
    b_in, conv_b, norm_gain, norm_bias, row_bias = small
    context = exchange(context)
    context = context.transpose(1, 2, 0, 3).reshape(rows, width)

    cots, context = relocate_one(masks, cots, 1, context)
    summed_first = flat_tokens.astype(F32) + dot_plain(context, w_out) + row_bias[0]
    hidden1 = norm_rows(summed_first, norm_gain[0], norm_bias[0])
    hidden1_low = hidden1.astype(BF)
    inner = dot_plain(hidden1_low, w_in) + b_in
    activated, inner_slope = gelu_both(inner)
    activated, inner_slope = lax.optimization_barrier((activated.astype(BF), inner_slope))
    summed_second = hidden1 + dot_plain(activated, w_back) + row_bias[1]
    hidden2 = norm_rows(summed_second, norm_gain[1], norm_bias[1])
    hidden2_low = hidden2.astype(BF)
    char_low = char_state.astype(BF)
    token_side = dot_plain(hidden2_low, blend_w[:, :width]) + row_bias[2]
    char_side = dot_plain(char_low, blend_w[:, width:]) + row_bias[3]
    joined = jnp.concatenate([token_side, char_side], axis=-1).astype(BF)
    joined = joined.reshape(seqs, local, 2 * width)
    cots, joined = lax.optimization_barrier((cots, joined))
    taps = shifted(joined, *edges(joined))
    stacked = jnp.concatenate(taps, axis=-1)
    mixed = dot_plain(stacked, conv_w) + conv_b
    lifted, mixed_slope = lax.optimization_barrier(gelu_both(mixed))
    token_pre = hidden2 + lifted[:, :width]
    char_pre = char_state + lifted[:, width:]
    token_out = norm_rows(token_pre, norm_gain[2], norm_bias[2]).astype(BF)
    char_out = norm_rows(char_pre, norm_gain[3], norm_bias[3]).astype(BF)
    outs = (token_out.reshape(seqs, local, width), char_out.reshape(seqs, local, width))
    cots = relocate_last(masks, cots, 2, (token_out, char_out))

    token_cots, char_cots = (part.reshape(rows, width).astype(F32) for part in cots)
    d_token_pre, gain_token, shift_token = norm_back(
        token_pre, norm_gain[2], token_cots
    )
    d_char_pre, gain_char, shift_char = norm_back(char_pre, norm_gain[3], char_cots)
    d_mixed = jnp.concatenate([d_token_pre, d_char_pre], axis=-1) * mixed_slope
    d_mixed = d_mixed.astype(BF)
    grad_conv = dot_left(stacked, d_mixed).astype(BF)
    grad_conv, d_mixed = lax.optimization_barrier((grad_conv, d_mixed))
    sum_conv = scatter_sum(grad_conv)
    outs, d_mixed = relocate_one(masks, outs, 0, d_mixed)
    beside = d_mixed.reshape(seqs, local, 2 * width)
    before, same, after = shifted(beside, *edges(beside))
    taps_w = conv_w.reshape(3, 2 * width, 2 * width)
    d_joined = dot_right(after, taps_w[0]) + dot_right(same, taps_w[1])
    d_joined = (d_joined + dot_right(before, taps_w[2])).astype(BF)
    d_token_side = d_joined[:, :width]
    d_char_side = d_joined[:, width:]
    grad_blend = jnp.concatenate(
        [dot_left(hidden2_low, d_token_side), dot_left(char_low, d_char_side)], axis=-1
    )
    grad_blend, d_token_side, d_char_side = lax.optimization_barrier(
        (grad_blend.astype(BF), d_token_side, d_char_side)
    )
    sum_blend = scatter_sum(grad_blend)
    d_hidden2 = d_token_pre + dot_right(d_token_side, blend_w[:, :width])
    d_char_state = d_char_pre + dot_right(d_char_side, blend_w[:, width:])

    d_second, gain_second, shift_second = norm_back(summed_second, norm_gain[1], d_hidden2)
    d_branch = d_second.astype(BF)
    grad_back = dot_left(activated, d_branch).astype(BF)
    grad_back, d_branch = lax.optimization_barrier((grad_back, d_branch))
    sum_back = scatter_sum(grad_back)
    d_inner = (dot_right(d_branch, w_back) * inner_slope).astype(BF)
    grad_in = dot_left(hidden1_low, d_inner)
    d_hidden1 = d_second + dot_right(d_inner, w_in)
    d_first, gain_first, shift_first = norm_back(summed_first, norm_gain[0], d_hidden1)
    d_attend = d_first.astype(BF)
    outs, d_attend = relocate_one(masks, outs, 1, d_attend)
    grad_out = dot_left(context, d_attend)
    d_context = dot_right(d_attend, w_out).astype(BF)
    d_context = d_context.reshape(seqs, local, parts, per * HEAD).transpose(2, 0, 1, 3)
    d_project = attention_backward(qkv, exchange(d_context), own_lengths, per)
    sum_conv, d_char_state, d_project = lax.optimization_barrier((sum_conv, d_char_state, d_project))
    d_project = exchange(d_project)
    sum_conv = line_sum(sum_conv, 0)
    d_project = d_project.transpose(1, 2, 0, 3).reshape(rows, 3 * width)

    d_gates, grad_gru_h, grad_gru_bias = gru_backward(
        counts, row_chars, gru_x, gru_h, gru_bias, d_char_state
    )
    sum_conv, d_gates = lax.optimization_barrier((sum_conv, d_gates))
    sum_conv = line_sum(sum_conv, 1)
    d_gates = d_gates.reshape(NCHAR * rows, 2 * three)
    grad_gru_x = dot_left(flat_chars, d_gates)
    chars_back = dot_right(d_gates, gru_x).astype(BF)
    chars_back, sum_conv = lax.optimization_barrier((chars_back, sum_conv))
    chars_back = chars_back.reshape(NCHAR, seqs, local, width).transpose(1, 2, 0, 3)

    grad_qkv = dot_left(flat_tokens, d_project)
    sums = heads_last(column_sum(d_project)[None], parts)[0]
    grad_b_qv = jnp.concatenate([sums[:width], sums[2 * width :]])
    tokens_back = (d_first + dot_right(d_project, w_qkv)).astype(BF)
    big = (grad_in, grad_qkv, grad_gru_x, grad_gru_h, grad_out)
    small = (
        grad_b_qv,
        column_sum(d_inner),
        [grad_gru_bias[0], grad_gru_bias[1]],
        column_sum(d_mixed),
        [gain_first, gain_second, gain_token, gain_char],
        [shift_first, shift_second, shift_token, shift_char],
        [
            column_sum(d_attend),
            column_sum(d_branch),
            column_sum(d_token_side),
            column_sum(d_char_side),
        ],
    )
    big, early, small = reduce_grads(big, (sum_back, sum_blend), small)
    outs, big[-1] = lax.optimization_barrier((outs, big[-1]))
    outs = relocate_last(masks, outs, 2, big[-1])
    g_in, g_qkv, g_gru_x, g_gru_h, g_out = big
    g_back, g_blend = early
    g_conv = line_sum(sum_conv, 2).astype(F32)
    g_b_qv, g_b_in, g_gru_bias, g_conv_b, g_gain, g_shift, g_rows = small
    return (
        outs[0],
        outs[1],
        tokens_back.reshape(seqs, local, width),
        chars_back,
        heads_last(g_qkv, parts),
        g_b_qv,
        g_out,
        g_in,
        g_b_in,
        g_back,
        g_gru_x,
        g_gru_h,
        g_gru_bias,
        g_blend,
        g_conv,
        g_conv_b,
        g_gain,
        g_shift,
        g_rows,
    )


def solution(mesh):
    rows, vector, seq = P("dp", None), P("dp"), P("dp", "seq", None)
    weights = (
        rows,
        vector,
        rows,
        rows,
        vector,
        rows,
        rows,
        rows,
        rows,
        rows,
        rows,
        vector,
        rows,
        rows,
        rows,
    )
    return jax.shard_map(
        body,
        mesh=mesh,
        in_specs=(seq, P("dp", "seq", None, None), P("dp", "seq"), P(), P(), seq, seq) + weights,
        out_specs=(seq, seq, seq, P("dp", "seq", None, None)) + weights,
        check_vma=False,
    )
```

```python
from functools import partial

import jax
import jax.numpy as jnp
from jax import lax
from jax.experimental import pallas as pl
from jax.experimental.pallas import tpu as pltpu
from jax.sharding import PartitionSpec as P

HEAD = 64
H = 384
NCHAR = 4
WIDE = 768
BF = jnp.bfloat16
F32 = jnp.float32


def dot_plain(left, right):
    return jnp.dot(left, right, preferred_element_type=F32)


def dot_left(left, right):
    return lax.dot_general(left, right, (((0,), (0,)), ((), ())), preferred_element_type=F32)


def dot_right(left, right):
    return lax.dot_general(left, right, (((1,), (1,)), ((), ())), preferred_element_type=F32)


def column_sum(values):
    return jnp.sum(values.astype(F32), axis=0)


def norm_rows(values, gain, shift):
    center = values - jnp.mean(values, axis=-1, keepdims=True)
    spread = jnp.mean(center * center, axis=-1, keepdims=True)
    rstd = lax.rsqrt(spread + 1e-06)
    return center * rstd * gain + shift


def norm_back(values, gain, grad):
    center = values - jnp.mean(values, axis=-1, keepdims=True)
    spread = jnp.mean(center * center, axis=-1, keepdims=True)
    rstd = lax.rsqrt(spread + 1e-06)
    hat = center * rstd
    lead = grad * gain
    back = rstd * (
        lead
        - jnp.mean(lead, axis=-1, keepdims=True)
        - hat * jnp.mean(lead * hat, axis=-1, keepdims=True)
    )
    return back, jnp.sum(grad * hat, axis=0), jnp.sum(grad, axis=0)


def gelu_both(values):
    cdf = 0.5 * (1.0 + lax.erf(values * (0.5**0.5)))
    pdf = jnp.exp(-0.5 * values * values) * 0.3989422804014327
    return values * cdf, cdf + values * pdf


def gru_order(side):
    return range(NCHAR) if side == 0 else range(NCHAR - 1, -1, -1)


def gru_cell(live, gates, recur, state):
    width = state.shape[-1]
    reset = jax.nn.sigmoid(gates[:, :width] + recur[:, :width])
    update = jax.nn.sigmoid(gates[:, width : 2 * width] + recur[:, width : 2 * width])
    fresh = jnp.tanh(gates[:, 2 * width :] + reset * recur[:, 2 * width :])
    after = jnp.where(live, (1.0 - update) * fresh + update * state, state)
    return reset, update, fresh, after


def gru_forward_kernel(count_ref, chars_ref, x_ref, h_ref, bias_ref, out_ref, gate_ref):
    rows = chars_ref.shape[1]
    three = 3 * H
    counts = jnp.broadcast_to(count_ref[...], (rows, H))
    chars = chars_ref[...].reshape(NCHAR * rows, chars_ref.shape[2])
    for side in range(2):
        columns = slice(side * three, (side + 1) * three)
        gate_ref[...] = dot_plain(chars, x_ref[:, columns]) + bias_ref[0:1, columns]
        state = jnp.zeros((rows, H), F32)
        for position in gru_order(side):
            recur = dot_plain(state.astype(BF), h_ref[:, columns]) + bias_ref[1:2, columns]
            gates = gate_ref[position * rows : (position + 1) * rows, :]
            state = gru_cell(position < counts, gates, recur, state)[3]
        out_ref[:, side * H : (side + 1) * H] = state


def gru_specs(high, width):
    three = 3 * H
    return [
        pl.BlockSpec((high, 1), lambda i: (i, 0)),
        pl.BlockSpec((NCHAR, high, width), lambda i: (0, i, 0)),
        pl.BlockSpec((width, 2 * three), lambda i: (0, 0)),
        pl.BlockSpec((H, 2 * three), lambda i: (0, 0)),
        pl.BlockSpec((2, 2 * three), lambda i: (0, 0)),
    ]


def gru_forward(counts, chars, gru_x, gru_h, gru_bias, high=256):
    rows, width = chars.shape[1:]
    products = NCHAR * rows * (width + H) * 6 * H
    return pl.pallas_call(
        gru_forward_kernel,
        grid=(rows // high,),
        in_specs=gru_specs(high, width),
        out_specs=pl.BlockSpec((high, 2 * H), lambda i: (i, 0)),
        out_shape=jax.ShapeDtypeStruct((rows, 2 * H), F32),
        scratch_shapes=[pltpu.VMEM((NCHAR * high, 3 * H), F32)],
        cost_estimate=pl.CostEstimate(
            flops=2 * products, bytes_accessed=10_000_000, transcendentals=24 * rows * H
        ),
        name="gru_forward",
    )(counts, chars, gru_x, gru_h, gru_bias)


def gru_backward_kernel(
    count_ref,
    chars_ref,
    x_ref,
    h_ref,
    bias_ref,
    grad_ref,
    gates_out,
    h_out,
    bias_out,
    gate_ref,
    keep_ref,
    state_ref,
    low_ref,
    recur_ref,
    total_ref,
):
    rows = chars_ref.shape[1]
    three = 3 * H
    counts = jnp.broadcast_to(count_ref[...], (rows, H))
    chars = chars_ref[...].reshape(NCHAR * rows, chars_ref.shape[2])

    @pl.when(pl.program_id(0) == 0)
    def _():
        bias_out[...] = jnp.zeros_like(bias_out)
        total_ref[...] = jnp.zeros_like(total_ref)

    for side in range(2):
        columns = slice(side * three, (side + 1) * three)
        gate_ref[...] = dot_plain(chars, x_ref[:, columns]) + bias_ref[0:1, columns]
        state = jnp.zeros((rows, H), F32)
        for position in gru_order(side):
            part = slice(position * rows, (position + 1) * rows)
            low = state.astype(BF)
            low_ref[part, :] = low
            state_ref[part, :] = state
            recur = dot_plain(low, h_ref[:, columns]) + bias_ref[1:2, columns]
            keep_ref[part, :] = recur[:, 2 * H :]
            reset, update, fresh, state = gru_cell(
                position < counts, gate_ref[part, :], recur, state
            )
            gate_ref[part, :H] = reset
            gate_ref[part, H : 2 * H] = update
            gate_ref[part, 2 * H :] = fresh
        grad = grad_ref[:, side * H : (side + 1) * H]
        gate_sum = jnp.zeros((1, three), F32)
        recur_sum = jnp.zeros((1, three), F32)
        for position in reversed(gru_order(side)):
            part = slice(position * rows, (position + 1) * rows)
            live = position < counts
            reset = gate_ref[part, :H]
            update = gate_ref[part, H : 2 * H]
            fresh = gate_ref[part, 2 * H :]
            moved = jnp.where(live, grad, 0.0)
            d_fresh = moved * (1.0 - update) * (1.0 - fresh * fresh)
            d_update = moved * (state_ref[part, :] - fresh) * update * (1.0 - update)
            d_reset = d_fresh * keep_ref[part, :] * reset * (1.0 - reset)
            d_gate = jnp.concatenate([d_reset, d_update, d_fresh], axis=-1).astype(BF)
            d_recur = jnp.concatenate([d_reset, d_update, d_fresh * reset], axis=-1).astype(BF)
            gates_out[position, :, columns] = d_gate
            recur_ref[part, :] = d_recur
            gate_sum += jnp.sum(d_gate.astype(F32), axis=0, keepdims=True)
            recur_sum += jnp.sum(d_recur.astype(F32), axis=0, keepdims=True)
            grad = jnp.where(live, moved * update, grad) + dot_right(d_recur, h_ref[:, columns])
        bias_out[0:1, columns] += gate_sum
        bias_out[1:2, columns] += recur_sum
        total_ref[:, columns] += dot_left(low_ref[...], recur_ref[...])

    @pl.when(pl.program_id(0) == pl.num_programs(0) - 1)
    def _():
        h_out[...] = total_ref[...].astype(BF)


def gru_backward(counts, chars, gru_x, gru_h, gru_bias, grad, high=256):
    rows, width = chars.shape[1:]
    three = 3 * H
    products = NCHAR * rows * (width + 3 * H) * 6 * H
    return pl.pallas_call(
        gru_backward_kernel,
        grid=(rows // high,),
        in_specs=gru_specs(high, width) + [pl.BlockSpec((high, 2 * H), lambda i: (i, 0))],
        out_specs=[
            pl.BlockSpec((NCHAR, high, 2 * three), lambda i: (0, i, 0)),
            pl.BlockSpec((H, 2 * three), lambda i: (0, 0)),
            pl.BlockSpec((2, 2 * three), lambda i: (0, 0)),
        ],
        out_shape=[
            jax.ShapeDtypeStruct((NCHAR, rows, 2 * three), BF),
            jax.ShapeDtypeStruct((H, 2 * three), BF),
            jax.ShapeDtypeStruct((2, 2 * three), F32),
        ],
        scratch_shapes=[
            pltpu.VMEM((NCHAR * high, three), F32),
            pltpu.VMEM((NCHAR * high, H), F32),
            pltpu.VMEM((NCHAR * high, H), F32),
            pltpu.VMEM((NCHAR * high, H), BF),
            pltpu.VMEM((NCHAR * high, three), BF),
            pltpu.VMEM((H, 2 * three), F32),
        ],
        cost_estimate=pl.CostEstimate(
            flops=2 * products, bytes_accessed=30_000_000, transcendentals=24 * rows * H
        ),
        name="gru_backward",
    )(counts, chars, gru_x, gru_h, gru_bias, grad)


def attention_forward_kernel(per, len_ref, qkv_ref, out_ref):
    block = pl.program_id(1)
    length = len_ref[pl.program_id(0)]
    span = per * HEAD
    total = qkv_ref.shape[0] * qkv_ref.shape[2]
    rows = qkv_ref.shape[2]
    q_all = qkv_ref[block, 0, :, :span] * BF(HEAD ** (-0.5))
    k_all = qkv_ref[:, 0, :, span : 2 * span].reshape(total, span)
    v_all = qkv_ref[:, 0, :, 2 * span :].reshape(total, span)
    valid = lax.broadcasted_iota(jnp.int32, (rows, total), 1) < length
    pieces = []
    for j in range(per):
        part = slice(j * HEAD, (j + 1) * HEAD)
        scores = jnp.where(valid, dot_right(q_all[:, part], k_all[:, part]), -1e30)
        raised = jnp.exp(scores - jnp.max(scores, axis=-1, keepdims=True))
        share = 1.0 / jnp.sum(raised, axis=-1, keepdims=True)
        probs = (raised * share).astype(BF)
        pieces.append(dot_plain(probs, v_all[:, part]))
    out_ref[0, 0] = jnp.concatenate(pieces, axis=-1).astype(BF)


def attention_forward(qkv, lengths, per):
    seqs, rows = qkv.shape[1], qkv.shape[2]
    parts = qkv.shape[0]
    span = per * HEAD
    return pl.pallas_call(
        partial(attention_forward_kernel, per),
        grid_spec=pltpu.PrefetchScalarGridSpec(
            num_scalar_prefetch=1,
            grid=(seqs, parts),
            in_specs=[pl.BlockSpec((parts, 1, rows, 3 * span), lambda m, b, n: (0, m, 0, 0))],
            out_specs=pl.BlockSpec((1, 1, rows, span), lambda m, b, n: (b, m, 0, 0)),
        ),
        out_shape=jax.ShapeDtypeStruct((parts, seqs, rows, span), BF),
        name="attend_forward",
    )(lengths, qkv)


def attention_backward_kernel(per, len_ref, qkv_ref, grad_ref, out_ref, key_acc, value_acc):
    block = pl.program_id(1)
    length = len_ref[pl.program_id(0)]
    span = per * HEAD
    parts, rows = qkv_ref.shape[0], qkv_ref.shape[2]
    total = parts * rows
    scale = HEAD ** (-0.5)

    @pl.when(block == 0)
    def _():
        key_acc[...] = jnp.zeros_like(key_acc)
        value_acc[...] = jnp.zeros_like(value_acc)

    q_all = qkv_ref[block, 0, :, :span] * BF(scale)
    g_all = grad_ref[block, 0]
    k_all = qkv_ref[:, 0, :, span : 2 * span].reshape(total, span)
    v_all = qkv_ref[:, 0, :, 2 * span :].reshape(total, span)
    valid = lax.broadcasted_iota(jnp.int32, (total, rows), 0) < length
    q_pieces, k_pieces, v_pieces = [], [], []
    for j in range(per):
        part = slice(j * HEAD, (j + 1) * HEAD)
        q, g, k, v = q_all[:, part], g_all[:, part], k_all[:, part], v_all[:, part]
        scores = jnp.where(valid, dot_right(k, q), -1e30)
        raised = jnp.exp(scores - jnp.max(scores, axis=0, keepdims=True))
        probs = raised * (1.0 / jnp.sum(raised, axis=0, keepdims=True))
        d_probs = dot_right(v, g)
        delta = jnp.sum(d_probs * probs, axis=0, keepdims=True)
        d_scores = (probs * (d_probs - delta)).astype(BF)
        q_pieces.append(dot_left(d_scores, k) * scale)
        k_pieces.append(dot_plain(d_scores, q))
        v_pieces.append(dot_plain(probs.astype(BF), g))
    out_ref[block, 0, :, :span] = jnp.concatenate(q_pieces, axis=-1).astype(BF)
    key_acc[...] += jnp.concatenate(k_pieces, axis=-1)
    value_acc[...] += jnp.concatenate(v_pieces, axis=-1)

    @pl.when(block == parts - 1)
    def _():
        out_ref[:, 0, :, span : 2 * span] = key_acc[...].astype(BF).reshape(parts, rows, span)
        out_ref[:, 0, :, 2 * span :] = value_acc[...].astype(BF).reshape(parts, rows, span)


def attention_backward(qkv, grads, lengths, per):
    parts, seqs, rows, _ = qkv.shape
    span = per * HEAD
    return pl.pallas_call(
        partial(attention_backward_kernel, per),
        grid_spec=pltpu.PrefetchScalarGridSpec(
            num_scalar_prefetch=1,
            grid=(seqs, parts),
            in_specs=[
                pl.BlockSpec((parts, 1, rows, 3 * span), lambda m, b, n: (0, m, 0, 0)),
                pl.BlockSpec((parts, 1, rows, span), lambda m, b, n: (0, m, 0, 0)),
            ],
            out_specs=pl.BlockSpec((parts, 1, rows, 3 * span), lambda m, b, n: (0, m, 0, 0)),
            scratch_shapes=[
                pltpu.VMEM((parts * rows, span), F32),
                pltpu.VMEM((parts * rows, span), F32),
            ],
        ),
        out_shape=jax.ShapeDtypeStruct(qkv.shape, BF),
        name="attend_backward",
    )(lengths, qkv, grads)


def exchange(blocks):
    return lax.all_to_all(blocks, "seq", split_axis=0, concat_axis=0)


def relocate_begin(pair, step):
    count = lax.axis_size("dp")
    levels = count.bit_length() - 1
    bits = (step, step if step == 0 else levels - step)
    others = []
    for value, bit in zip(pair, bits):
        apart = 1 << bit
        pairs = [(source, source ^ apart) for source in range(count)]
        others.append(lax.ppermute(value, "dp", pairs))
    return bits, tuple(others)


def relocate_end(masks, pair, begun):
    done = []
    for value, bit, other in zip(pair, *begun):
        moving = (jnp.bitwise_and(masks, 1 << bit) != 0)[:, None, None]
        done.append(jnp.where(moving, other, value))
    return tuple(done)


def relocate_one(masks, pair, step, tie):
    bits, others = relocate_begin(pair, step)
    others, pair, tie = lax.optimization_barrier((others, pair, tie))
    return relocate_end(masks, pair, (bits, others)), tie


def relocate_last(masks, pair, first, tie):
    levels = lax.axis_size("dp").bit_length() - 1
    for step in range(first, levels):
        bits, others = relocate_begin(pair, step)
        if step == levels - 1:
            others, pair, _ = lax.optimization_barrier((others, pair, tie))
        pair = relocate_end(masks, pair, (bits, others))
    return pair


def edges(block):
    count = lax.axis_size("seq")
    forward = [(i, i + 1) for i in range(count - 1)]
    backward = [(target, source) for source, target in forward]
    low = lax.ppermute(block[:, -1:], "seq", forward)
    high = lax.ppermute(block[:, :1], "seq", backward)
    return low, high


LINE = ([(0, 1), (3, 2)], [(1, 2), (2, 1)])


def line_sum(value, step):
    if lax.axis_size("seq") != 4:
        return lax.psum(value, "seq") if step == 0 else value
    other = lax.ppermute(value, "seq", LINE[step])
    return value + other


def shifted(block, low, high):
    before = jnp.concatenate([low, block[:, :-1]], axis=1)
    after = jnp.concatenate([block[:, 1:], high], axis=1)
    flat = (-1, block.shape[-1])
    return before.reshape(flat), block.reshape(flat), after.reshape(flat)


def sum_plan(shapes, high):
    spans, start = [], 0
    for rows, columns in shapes:
        tall = rows // high
        count = tall * (columns // WIDE)
        spans.append((start, start + count, tall))
        start += count
    return spans, start


def sum_kernel(spans, pre_spans, late, pre, high, lag, slots, *refs):
    whole = len(spans)
    count = whole + len(pre_spans)
    total = late + pre
    ins, middle_ref = refs[:count], refs[count]
    outs, ends_ref = refs[count + 1 : 2 * count + 1], refs[2 * count + 1]
    refs = refs[2:]
    own, rc, sc, s1a, s1b, r1a, r1b, r2a, r2b, s2, rz, sz, rm, tot, ready = refs[
        2 * count : 2 * count + 15
    ]
    sems = refs[2 * count + 15]
    credits = refs[2 * count + 16]
    ends_sems = refs[2 * count + 17]
    half = WIDE // 2
    dp, z = lax.axis_index("dp"), lax.axis_index("seq")
    core, x, y = dp % 2, (dp // 2) % 2, dp // 4
    at_core = {"dp": dp + 1 - 2 * core}
    at_x = {"dp": dp + 2 - 4 * x}
    at_y = {"dp": dp + 4 - 8 * y}
    outer = (z % 3) == 0
    inner = (z % 3) != 0
    at_inner = {"seq": 1 + z // 3}
    at_middle = {"seq": (3 - z) % 4}
    at_outer = {"seq": (z // 2) * 3}

    barrier = pltpu.get_barrier_semaphore()

    def greet(where):
        pl.semaphore_signal(barrier, inc=1, device_id=where, device_id_type=pl.DeviceIdType.MESH)

    greet(at_core)
    greet(at_x)
    greet(at_y)

    @pl.when(outer)
    def _():
        greet(at_inner)
        pl.semaphore_wait(barrier, 4)

    @pl.when(inner)
    def _():
        greet(at_middle)
        greet(at_outer)
        pl.semaphore_wait(barrier, 5)

    def remote(source, target, name, slot, where):
        return pltpu.make_async_remote_copy(
            src_ref=source,
            dst_ref=target,
            send_sem=sems.at[2 * name, slot],
            recv_sem=sems.at[2 * name + 1, slot],
            device_id=where,
            device_id_type=pl.DeviceIdType.MESH,
        )

    CORE, X1, Y1, X2, Y2, OUTER, MIDDLE, FINAL, LOCAL, READY = range(10)

    def give_credit(name, k, where):
        @pl.when(k + slots < total)
        def _():
            pl.semaphore_signal(
                credits.at[name], inc=1, device_id=where, device_id_type=pl.DeviceIdType.MESH
            )

    def take_credit(name, k):
        @pl.when(k >= slots)
        def _():
            pl.semaphore_wait(credits.at[name], 1)

    def send_core(slot, source):
        return remote(source, rc.at[slot], CORE, slot, at_core)

    def send_x1(slot):
        return remote(sc.at[slot, :, 1 - x, :, :half], r1a.at[slot], X1, slot, at_x)

    def send_y1(slot):
        return remote(sc.at[slot, 1 - y, :, :, half:], r1b.at[slot], Y1, slot, at_y)

    def send_y2(slot):
        return remote(s1a.at[slot, 1 - y], r2a.at[slot], Y2, slot, at_y)

    def send_x2(slot):
        return remote(s1b.at[slot, 1 - x], r2b.at[slot], X2, slot, at_x)

    def send_outer(slot):
        return remote(s2.at[slot], rz.at[slot], OUTER, slot, at_inner)

    def send_middle(slot):
        return remote(sz.at[slot], rm.at[slot], MIDDLE, slot, at_middle)

    def send_final(slot, target):
        return remote(tot.at[slot], target, FINAL, slot, at_outer)

    def load(slot, source):
        return pltpu.make_async_copy(source, own.at[slot], sems.at[2 * LOCAL, slot])

    def load_ready(slot, source):
        return pltpu.make_async_copy(source, ready.at[slot], sems.at[2 * READY, slot])

    def save(slot, target):
        return pltpu.make_async_copy(tot.at[slot], target, sems.at[2 * LOCAL + 1, slot])

    def window(ref, j, tall):
        return pl.ds((j % tall) * high, high), pl.ds((j // tall) * WIDE, WIDE)

    def is_pre(k):
        return (k < 3 * pre) & (k % 3 == 2)

    def late_index(k):
        return jnp.where(k < 3 * pre, (k // 3) * 2 + k % 3, k - pre)

    def each(k, plan, parts, index, run):
        for (start, stop, tall), ref in zip(plan, parts):

            @pl.when((index >= start) & (index < stop))
            def _():
                run(ref, *window(ref, index - start, tall))

    def on_late(k, run):
        pl.when(jnp.logical_not(is_pre(k)))(run)

    def on_pre(k, run):
        pl.when(is_pre(k))(run)

    def add(left, right):
        return (left.astype(F32) + right.astype(F32)).astype(BF)

    def stage(k, run):
        @pl.when((k >= 0) & (k < total))
        def _():
            run(k, lax.rem(jnp.maximum(k, 0), slots))

    ends = pltpu.make_async_remote_copy(
        src_ref=middle_ref,
        dst_ref=ends_ref,
        send_sem=ends_sems.at[0],
        recv_sem=ends_sems.at[1],
        device_id=at_outer,
        device_id_type=pl.DeviceIdType.MESH,
    )

    @pl.when(inner)
    def _():
        ends.start()

    first = ins[0].at[:, core, pl.ds(0, high), pl.ds(0, WIDE)]
    final = outs[0].at[pl.ds(0, high), pl.ds(0, WIDE)]
    early = ins[whole].at[pl.ds(0, high), pl.ds(0, WIDE)]

    @pl.loop(0, total + 6 * lag)
    def _(t):
        def begin(k, slot):
            take_credit(CORE, k)

            def go():
                def run(ref, rows, columns):
                    send_core(slot, ref.at[:, 1 - core, rows, columns]).start()
                    load(slot, ref.at[:, core, rows, columns]).start()

                each(k, spans, ins[:whole], late_index(k), run)

            on_late(k, go)

        def add_core(k, slot):
            def go():
                load(slot, first).wait()
                send_core(slot, first).wait()
                both = add(own[slot], rc[slot])
                sc[slot] = both.reshape(2, 2, high, WIDE)

            on_late(k, go)
            give_credit(CORE, k, at_core)

        def add_one(k, slot):
            def go():
                send_x1(slot).wait()
                send_y1(slot).wait()
                s1a[slot] = add(sc[slot, :, x, :, :half], r1a[slot])
                s1b[slot] = add(sc[slot, y, :, :, half:], r1b[slot])

            on_late(k, go)
            give_credit(X1, k, at_x)
            give_credit(Y1, k, at_y)

        def add_two(k, slot):
            def go():
                send_y2(slot).wait()
                send_x2(slot).wait()
                s2[slot, :, :half] = add(s1a[slot, y], r2a[slot])
                s2[slot, :, half:] = add(s1b[slot, x], r2b[slot])

            def take():
                load_ready(slot, early).wait()
                s2[slot] = ready[slot]

            on_late(k, go)
            on_pre(k, take)
            give_credit(Y2, k, at_y)
            give_credit(X2, k, at_x)

        def add_outer(k, slot):
            @pl.when(outer)
            def _():
                send_outer(slot).wait_send()

            @pl.when(inner)
            def _():
                send_outer(slot).wait_recv()
                sz[slot] = add(s2[slot], rz[slot])
                give_credit(OUTER, k, at_outer)

        def add_middle(k, slot):
            @pl.when(inner)
            def _():
                send_middle(slot).wait()
                tot[slot] = add(sz[slot], rm[slot])
                give_credit(MIDDLE, k, at_middle)

        def finish(k, slot):
            @pl.when(inner)
            def _():
                save(slot, final).wait()
                send_final(slot, final).wait_send()

            @pl.when(outer)
            def _():
                send_final(slot, final).wait_recv()
                give_credit(FINAL, k, at_inner)

        def go_one(k, slot):
            take_credit(X1, k)
            take_credit(Y1, k)

            def go():
                send_x1(slot).start()
                send_y1(slot).start()

            on_late(k, go)

        def go_two(k, slot):
            take_credit(Y2, k)
            take_credit(X2, k)

            def go():
                send_y2(slot).start()
                send_x2(slot).start()

            def fetch():
                def run(ref, rows, columns):
                    load_ready(slot, ref.at[rows, columns]).start()

                each(k, pre_spans, ins[whole:], k // 3, run)

            on_late(k, go)
            on_pre(k, fetch)

        def go_outer(k, slot):
            @pl.when(outer)
            def _():
                take_credit(OUTER, k)
                send_outer(slot).start()

        def go_middle(k, slot):
            @pl.when(inner)
            def _():
                take_credit(MIDDLE, k)
                send_middle(slot).start()

        def go_final(k, slot):
            @pl.when(inner)
            def _():
                take_credit(FINAL, k)

                def run(ref, rows, columns):
                    save(slot, ref.at[rows, columns]).start()
                    send_final(slot, ref.at[rows, columns]).start()

                on_late(k, lambda: each(k, spans, outs[:whole], late_index(k), run))
                on_pre(k, lambda: each(k, pre_spans, outs[whole:], k // 3, run))

        stage(t, begin)
        stage(t - lag, add_core)
        stage(t - 2 * lag, add_one)
        stage(t - 3 * lag, add_two)
        stage(t - 4 * lag, add_outer)
        stage(t - 5 * lag, add_middle)
        stage(t - lag, go_one)
        stage(t - 2 * lag, go_two)
        stage(t - 3 * lag, go_outer)
        stage(t - 4 * lag, go_middle)
        stage(t - 5 * lag, go_final)
        stage(t - 6 * lag, finish)

    @pl.when(inner)
    def _():
        ends.wait_send()

    @pl.when(outer)
    def _():
        ends.wait_recv()


def sum_grads(grads, pres, middle, high=48, lag=3, slots=6):
    shapes = [(grad.shape[0] // 8, grad.shape[1]) for grad in grads]
    pre_shapes = [grad.shape for grad in pres]
    spans, late = sum_plan(shapes, high)
    pre_spans, pre = sum_plan(pre_shapes, high)
    half = WIDE // 2
    anywhere = pl.BlockSpec(memory_space=pl.ANY)
    blocks = [grad.reshape(4, 2, grad.shape[0] // 8, grad.shape[1]) for grad in grads]
    shapes = shapes + pre_shapes
    return pl.pallas_call(
        partial(sum_kernel, spans, pre_spans, late, pre, high, lag, slots),
        in_specs=[anywhere] * (len(shapes) + 1),
        out_specs=[anywhere] * (len(shapes) + 1),
        out_shape=[jax.ShapeDtypeStruct(shape, BF) for shape in shapes + [middle.shape]],
        scratch_shapes=[
            pltpu.VMEM((slots, 4, high, WIDE), BF),
            pltpu.VMEM((slots, 4, high, WIDE), BF),
            pltpu.VMEM((slots, 2, 2, high, WIDE), BF),
            pltpu.VMEM((slots, 2, high, half), BF),
            pltpu.VMEM((slots, 2, high, half), BF),
            pltpu.VMEM((slots, 2, high, half), BF),
            pltpu.VMEM((slots, 2, high, half), BF),
            pltpu.VMEM((slots, high, half), BF),
            pltpu.VMEM((slots, high, half), BF),
            pltpu.VMEM((slots, high, WIDE), BF),
            pltpu.VMEM((slots, high, WIDE), BF),
            pltpu.VMEM((slots, high, WIDE), BF),
            pltpu.VMEM((slots, high, WIDE), BF),
            pltpu.VMEM((slots, high, WIDE), BF),
            pltpu.VMEM((slots, high, WIDE), BF),
            pltpu.SemaphoreType.DMA((20, slots)),
            pltpu.SemaphoreType.REGULAR((8,)),
            pltpu.SemaphoreType.DMA((2,)),
        ],
        compiler_params=pltpu.CompilerParams(collective_id=1, has_side_effects=True),
        name="sum_grads",
    )(*blocks, *pres, middle)


def heads_first(weight, parts):
    rows = weight.shape[0]
    split = weight.reshape(rows, 3, parts, WIDE // parts)
    return split.transpose(0, 2, 1, 3).reshape(rows, 3 * WIDE)


def heads_last(weight, parts):
    rows = weight.shape[0]
    split = weight.reshape(rows, parts, 3, WIDE // parts)
    return split.transpose(0, 2, 1, 3).reshape(rows, 3 * WIDE)


def flat_small(small):
    return jnp.concatenate([piece.T.reshape(-1) for piece in small])


def gather_packed(weights, small, wide):
    return unpack(pack(weights, small, wide), weights, small, wide)


def pack(weights, small, wide):
    pieces = []
    for weight in weights:
        low = weight.astype(BF)
        pieces += [low[:, start : start + wide] for start in range(0, low.shape[1], wide)]
    flat = flat_small(small).astype(BF)
    high = -(-flat.size // wide)
    high = -(-high // 8) * 8
    pieces.append(jnp.pad(flat, (0, high * wide - flat.size)).reshape(high, wide))
    return lax.all_gather(jnp.concatenate(pieces, axis=0), "dp", axis=0)


def unpack(full, weights, small, wide):
    groups = full.shape[0]
    outs, at = [], 0
    for weight in weights:
        rows, columns = weight.shape
        blocks = columns // wide
        part = full[:, at : at + blocks * rows].reshape(groups, blocks, rows, wide)
        outs.append(part.transpose(0, 2, 1, 3).reshape(groups * rows, columns))
        at += blocks * rows
    used = -(-sum(piece.size for piece in small) // wide)
    table = full[:, at : at + used].astype(F32).reshape(groups, -1)
    vectors, at = [], 0
    for piece in small:
        part = table[:, at : at + piece.size]
        if piece.ndim == 2:
            rows, columns = piece.shape
            part = part.reshape(groups, columns, rows).transpose(1, 0, 2)
            vectors.append(part.reshape(columns, groups * rows))
        else:
            vectors.append(part.reshape(-1))
        at += piece.size
    return outs, vectors


def pack_small(small, groups, multiple):
    pieces = []
    for piece in small:
        columns = piece if isinstance(piece, list) else [piece]
        pieces += [column.reshape(groups, -1) for column in columns]
    flat = jnp.concatenate(pieces, axis=1)
    high = -(-flat.shape[1] // WIDE)
    high = -(-high // multiple) * multiple
    flat = jnp.pad(flat.astype(BF), ((0, 0), (0, high * WIDE - flat.shape[1])))
    return flat.reshape(groups * high, WIDE)


def sum_grads_plain(grads, pres):
    outs = [lax.psum_scatter(grad, "dp", scatter_dimension=0, tiled=True) for grad in grads]
    return [lax.psum(part, "seq") for part in outs + list(pres)]


def reduce_grads(big, pres, middle, small):
    groups = lax.axis_size("dp")
    ours = groups == 8 and lax.axis_size("seq") == 4
    grads = [grad.astype(BF) for grad in big] + [pack_small(small, groups, 48)]
    if ours:
        *outs, ends = sum_grads(grads, pres, middle)
        middle = jnp.where((lax.axis_index("seq") % 3) == 0, ends, middle)
    else:
        outs = sum_grads_plain(grads, pres)
    tail = outs[len(big)]
    sizes = []
    for piece in small:
        columns = piece if isinstance(piece, list) else [piece]
        sizes.append((len(columns), columns[0].size // groups, isinstance(piece, list)))
    used = -(-sum(many * size for many, size, _ in sizes) // WIDE)
    tail = tail[:used].astype(F32).reshape(-1)
    vectors, at = [], 0
    for many, size, matrix in sizes:
        part = tail[at : at + many * size]
        vectors.append(part.reshape(many, size).T if matrix else part)
        at += many * size
    bigs = [piece.astype(F32) for piece in outs[: len(big)]]
    early = [piece.astype(F32) for piece in outs[len(big) + 1 :]]
    return bigs, early + [middle.astype(F32)], vectors


def scatter_sum(grad):
    return lax.psum_scatter(grad.astype(BF), "dp", scatter_dimension=0, tiled=True)


def body(
    tokens,
    chars,
    char_counts,
    lengths,
    perm,
    token_cot,
    char_cot,
    w_qkv,
    b_qv,
    w_out,
    w_in,
    b_in,
    w_back,
    gru_x,
    gru_h,
    gru_bias,
    blend_w,
    conv_w,
    conv_b,
    norm_gain,
    norm_bias,
    row_bias,
):
    parts = lax.axis_size("seq")
    seqs, local, width = tokens.shape
    rows = seqs * local
    per = width // HEAD // parts
    three = 3 * H
    masks = perm[:, 0]
    place = lax.axis_index("dp")
    own_lengths = lax.dynamic_slice(lengths, (place * seqs,), (seqs,))
    first = (heads_first(w_qkv, parts), gru_x, gru_h)
    (w_qkv, gru_x, gru_h), (b_qv, gru_bias) = gather_packed(first, (b_qv, gru_bias), 3 * width)
    middle = (w_out, w_in, w_back, blend_w)
    small = (b_in, conv_b, norm_gain, norm_bias, row_bias)
    packed = pack(middle, small, width)
    conv_w = lax.all_gather(conv_w.astype(BF), "dp", axis=0, tiled=True)

    flat_tokens = tokens.reshape(rows, width)
    counts = char_counts.reshape(rows, 1)
    row_chars = chars.transpose(2, 0, 1, 3).reshape(NCHAR, rows, width)
    flat_chars = row_chars.reshape(NCHAR * rows, width)
    bias = jnp.concatenate([b_qv[:width], jnp.zeros((width,), F32), b_qv[width:]])
    bias = heads_first(bias[None], parts)[0]
    project = (dot_plain(flat_tokens, w_qkv) + bias).astype(BF)
    cots = (token_cot, char_cot)
    cots, project = relocate_one(masks, cots, 0, project)
    project, row_chars = lax.optimization_barrier((project, row_chars))
    span = 3 * per * HEAD
    qkv = project.reshape(seqs, local, parts, span).transpose(2, 0, 1, 3)
    qkv = exchange(qkv)
    char_state = gru_forward(counts, row_chars, gru_x, gru_h, gru_bias)
    qkv, char_state = lax.optimization_barrier((qkv, char_state))
    context = attention_forward(qkv, own_lengths, per)
    context, packed = lax.optimization_barrier((context, packed))
    middle, small = unpack(packed, middle, small, width)
    w_out, w_in, w_back, blend_w = middle
    b_in, conv_b, norm_gain, norm_bias, row_bias = small
    context = exchange(context)
    context = context.transpose(1, 2, 0, 3).reshape(rows, width)

    cots, context = relocate_one(masks, cots, 1, context)
    summed_first = flat_tokens.astype(F32) + dot_plain(context, w_out) + row_bias[0]
    hidden1 = norm_rows(summed_first, norm_gain[0], norm_bias[0])
    hidden1_low = hidden1.astype(BF)
    inner = dot_plain(hidden1_low, w_in) + b_in
    activated, inner_slope = gelu_both(inner)
    activated, inner_slope = lax.optimization_barrier((activated.astype(BF), inner_slope))
    summed_second = hidden1 + dot_plain(activated, w_back) + row_bias[1]
    hidden2 = norm_rows(summed_second, norm_gain[1], norm_bias[1])
    hidden2_low = hidden2.astype(BF)
    char_low = char_state.astype(BF)
    token_side = dot_plain(hidden2_low, blend_w[:, :width]) + row_bias[2]
    char_side = dot_plain(char_low, blend_w[:, width:]) + row_bias[3]
    joined = jnp.concatenate([token_side, char_side], axis=-1).astype(BF)
    joined = joined.reshape(seqs, local, 2 * width)
    cots, joined = lax.optimization_barrier((cots, joined))
    taps = shifted(joined, *edges(joined))
    stacked = jnp.concatenate(taps, axis=-1)
    mixed = dot_plain(stacked, conv_w) + conv_b
    lifted, mixed_slope = lax.optimization_barrier(gelu_both(mixed))
    token_pre = hidden2 + lifted[:, :width]
    char_pre = char_state + lifted[:, width:]
    token_out = norm_rows(token_pre, norm_gain[2], norm_bias[2]).astype(BF)
    char_out = norm_rows(char_pre, norm_gain[3], norm_bias[3]).astype(BF)
    outs = (token_out.reshape(seqs, local, width), char_out.reshape(seqs, local, width))
    cots = relocate_last(masks, cots, 2, (token_out, char_out))

    token_cots, char_cots = (part.reshape(rows, width).astype(F32) for part in cots)
    d_token_pre, gain_token, shift_token = norm_back(
        token_pre, norm_gain[2], token_cots
    )
    d_char_pre, gain_char, shift_char = norm_back(char_pre, norm_gain[3], char_cots)
    d_mixed = jnp.concatenate([d_token_pre, d_char_pre], axis=-1) * mixed_slope
    d_mixed = d_mixed.astype(BF)
    grad_conv = dot_left(stacked, d_mixed).astype(BF)
    grad_conv, d_mixed = lax.optimization_barrier((grad_conv, d_mixed))
    sum_conv = scatter_sum(grad_conv)
    outs, d_mixed = relocate_one(masks, outs, 0, d_mixed)
    beside = d_mixed.reshape(seqs, local, 2 * width)
    before, same, after = shifted(beside, *edges(beside))
    taps_w = conv_w.reshape(3, 2 * width, 2 * width)
    d_joined = dot_right(after, taps_w[0]) + dot_right(same, taps_w[1])
    d_joined = (d_joined + dot_right(before, taps_w[2])).astype(BF)
    d_token_side = d_joined[:, :width]
    d_char_side = d_joined[:, width:]
    grad_blend = jnp.concatenate(
        [dot_left(hidden2_low, d_token_side), dot_left(char_low, d_char_side)], axis=-1
    )
    grad_blend, d_token_side, d_char_side = lax.optimization_barrier(
        (grad_blend.astype(BF), d_token_side, d_char_side)
    )
    sum_blend = scatter_sum(grad_blend)
    d_hidden2 = d_token_pre + dot_right(d_token_side, blend_w[:, :width])
    d_char_state = d_char_pre + dot_right(d_char_side, blend_w[:, width:])

    d_second, gain_second, shift_second = norm_back(summed_second, norm_gain[1], d_hidden2)
    d_branch = d_second.astype(BF)
    grad_back = dot_left(activated, d_branch).astype(BF)
    grad_back, d_branch = lax.optimization_barrier((grad_back, d_branch))
    sum_back = scatter_sum(grad_back)
    d_inner = (dot_right(d_branch, w_back) * inner_slope).astype(BF)
    grad_in = dot_left(hidden1_low, d_inner)
    d_hidden1 = d_second + dot_right(d_inner, w_in)
    d_first, gain_first, shift_first = norm_back(summed_first, norm_gain[0], d_hidden1)
    d_attend = d_first.astype(BF)
    outs, d_attend = relocate_one(masks, outs, 1, d_attend)
    grad_out = dot_left(context, d_attend)
    d_context = dot_right(d_attend, w_out).astype(BF)
    d_context = d_context.reshape(seqs, local, parts, per * HEAD).transpose(2, 0, 1, 3)
    d_context, sum_conv, grad_in, grad_out = lax.optimization_barrier(
        (exchange(d_context), sum_conv, grad_in.astype(BF), grad_out.astype(BF))
    )
    sum_conv = line_sum(sum_conv, 0)
    d_project = attention_backward(qkv, d_context, own_lengths, per)
    sum_conv, d_char_state, d_project = lax.optimization_barrier((sum_conv, d_char_state, d_project))
    sum_conv = line_sum(sum_conv, 1)
    d_project = exchange(d_project)

    d_gates, grad_gru_h, grad_gru_bias = gru_backward(
        counts, row_chars, gru_x, gru_h, gru_bias, d_char_state
    )
    d_gates = d_gates.reshape(NCHAR * rows, 2 * three)
    grad_gru_x = dot_left(flat_chars, d_gates)
    chars_back = dot_right(d_gates, gru_x).astype(BF)
    chars_back, d_project, sum_conv = lax.optimization_barrier((chars_back, d_project, sum_conv))
    d_project = d_project.transpose(1, 2, 0, 3).reshape(rows, 3 * width)
    chars_back = chars_back.reshape(NCHAR, seqs, local, width).transpose(1, 2, 0, 3)

    grad_qkv = dot_left(flat_tokens, d_project)
    sums = heads_last(column_sum(d_project)[None], parts)[0]
    grad_b_qv = jnp.concatenate([sums[:width], sums[2 * width :]])
    tokens_back = (d_first + dot_right(d_project, w_qkv)).astype(BF)
    big = (grad_in, grad_qkv, grad_gru_x, grad_gru_h, grad_out)
    small = (
        grad_b_qv,
        column_sum(d_inner),
        [grad_gru_bias[0], grad_gru_bias[1]],
        column_sum(d_mixed),
        [gain_first, gain_second, gain_token, gain_char],
        [shift_first, shift_second, shift_token, shift_char],
        [
            column_sum(d_attend),
            column_sum(d_branch),
            column_sum(d_token_side),
            column_sum(d_char_side),
        ],
    )
    big, early, small = reduce_grads(big, (sum_back, sum_blend), sum_conv, small)
    outs, big[-1] = lax.optimization_barrier((outs, big[-1]))
    outs = relocate_last(masks, outs, 2, big[-1])
    g_in, g_qkv, g_gru_x, g_gru_h, g_out = big
    g_back, g_blend, g_conv = early
    g_b_qv, g_b_in, g_gru_bias, g_conv_b, g_gain, g_shift, g_rows = small
    return (
        outs[0],
        outs[1],
        tokens_back.reshape(seqs, local, width),
        chars_back,
        heads_last(g_qkv, parts),
        g_b_qv,
        g_out,
        g_in,
        g_b_in,
        g_back,
        g_gru_x,
        g_gru_h,
        g_gru_bias,
        g_blend,
        g_conv,
        g_conv_b,
        g_gain,
        g_shift,
        g_rows,
    )


def solution(mesh):
    rows, vector, seq = P("dp", None), P("dp"), P("dp", "seq", None)
    weights = (
        rows,
        vector,
        rows,
        rows,
        vector,
        rows,
        rows,
        rows,
        rows,
        rows,
        rows,
        vector,
        rows,
        rows,
        rows,
    )
    return jax.shard_map(
        body,
        mesh=mesh,
        in_specs=(seq, P("dp", "seq", None, None), P("dp", "seq"), P(), P(), seq, seq) + weights,
        out_specs=(seq, seq, seq, P("dp", "seq", None, None)) + weights,
        check_vma=False,
    )
```

```python
from functools import partial

import jax
import jax.numpy as jnp
from jax import lax
from jax.experimental import pallas as pl
from jax.experimental.pallas import tpu as pltpu
from jax.sharding import PartitionSpec as P

HEAD = 64
H = 384
NCHAR = 4
WIDE = 768
BF = jnp.bfloat16
F32 = jnp.float32


def dot_plain(left, right):
    return jnp.dot(left, right, preferred_element_type=F32)


def dot_left(left, right):
    return lax.dot_general(left, right, (((0,), (0,)), ((), ())), preferred_element_type=F32)


def dot_right(left, right):
    return lax.dot_general(left, right, (((1,), (1,)), ((), ())), preferred_element_type=F32)


def column_sum(values):
    return jnp.sum(values.astype(F32), axis=0)


def norm_rows(values, gain, shift):
    center = values - jnp.mean(values, axis=-1, keepdims=True)
    spread = jnp.mean(center * center, axis=-1, keepdims=True)
    rstd = lax.rsqrt(spread + 1e-06)
    return center * rstd * gain + shift


def norm_back(values, gain, grad):
    center = values - jnp.mean(values, axis=-1, keepdims=True)
    spread = jnp.mean(center * center, axis=-1, keepdims=True)
    rstd = lax.rsqrt(spread + 1e-06)
    hat = center * rstd
    lead = grad * gain
    back = rstd * (
        lead
        - jnp.mean(lead, axis=-1, keepdims=True)
        - hat * jnp.mean(lead * hat, axis=-1, keepdims=True)
    )
    return back, jnp.sum(grad * hat, axis=0), jnp.sum(grad, axis=0)


def gelu_both(values):
    cdf = 0.5 * (1.0 + lax.erf(values * (0.5**0.5)))
    pdf = jnp.exp(-0.5 * values * values) * 0.3989422804014327
    return values * cdf, cdf + values * pdf


def gru_order(side):
    return range(NCHAR) if side == 0 else range(NCHAR - 1, -1, -1)


def gru_cell(live, gates, recur, state):
    width = state.shape[-1]
    reset = jax.nn.sigmoid(gates[:, :width] + recur[:, :width])
    update = jax.nn.sigmoid(gates[:, width : 2 * width] + recur[:, width : 2 * width])
    fresh = jnp.tanh(gates[:, 2 * width :] + reset * recur[:, 2 * width :])
    after = jnp.where(live, (1.0 - update) * fresh + update * state, state)
    return reset, update, fresh, after


def gru_forward_kernel(count_ref, chars_ref, x_ref, h_ref, bias_ref, out_ref, gate_ref):
    rows = chars_ref.shape[1]
    three = 3 * H
    counts = jnp.broadcast_to(count_ref[...], (rows, H))
    chars = chars_ref[...].reshape(NCHAR * rows, chars_ref.shape[2])
    for side in range(2):
        columns = slice(side * three, (side + 1) * three)
        gate_ref[...] = dot_plain(chars, x_ref[:, columns]) + bias_ref[0:1, columns]
        state = jnp.zeros((rows, H), F32)
        for position in gru_order(side):
            recur = dot_plain(state.astype(BF), h_ref[:, columns]) + bias_ref[1:2, columns]
            gates = gate_ref[position * rows : (position + 1) * rows, :]
            state = gru_cell(position < counts, gates, recur, state)[3]
        out_ref[:, side * H : (side + 1) * H] = state


def gru_specs(high, width):
    three = 3 * H
    return [
        pl.BlockSpec((high, 1), lambda i: (i, 0)),
        pl.BlockSpec((NCHAR, high, width), lambda i: (0, i, 0)),
        pl.BlockSpec((width, 2 * three), lambda i: (0, 0)),
        pl.BlockSpec((H, 2 * three), lambda i: (0, 0)),
        pl.BlockSpec((2, 2 * three), lambda i: (0, 0)),
    ]


def gru_forward(counts, chars, gru_x, gru_h, gru_bias, high=256):
    rows, width = chars.shape[1:]
    products = NCHAR * rows * (width + H) * 6 * H
    return pl.pallas_call(
        gru_forward_kernel,
        grid=(rows // high,),
        in_specs=gru_specs(high, width),
        out_specs=pl.BlockSpec((high, 2 * H), lambda i: (i, 0)),
        out_shape=jax.ShapeDtypeStruct((rows, 2 * H), F32),
        scratch_shapes=[pltpu.VMEM((NCHAR * high, 3 * H), F32)],
        cost_estimate=pl.CostEstimate(
            flops=2 * products, bytes_accessed=10_000_000, transcendentals=24 * rows * H
        ),
        name="gru_forward",
    )(counts, chars, gru_x, gru_h, gru_bias)


def gru_backward_kernel(
    count_ref,
    chars_ref,
    x_ref,
    h_ref,
    bias_ref,
    grad_ref,
    gates_out,
    h_out,
    bias_out,
    gate_ref,
    keep_ref,
    state_ref,
    low_ref,
    recur_ref,
    total_ref,
):
    rows = chars_ref.shape[1]
    three = 3 * H
    counts = jnp.broadcast_to(count_ref[...], (rows, H))
    chars = chars_ref[...].reshape(NCHAR * rows, chars_ref.shape[2])

    @pl.when(pl.program_id(0) == 0)
    def _():
        bias_out[...] = jnp.zeros_like(bias_out)
        total_ref[...] = jnp.zeros_like(total_ref)

    for side in range(2):
        columns = slice(side * three, (side + 1) * three)
        gate_ref[...] = dot_plain(chars, x_ref[:, columns]) + bias_ref[0:1, columns]
        state = jnp.zeros((rows, H), F32)
        for position in gru_order(side):
            part = slice(position * rows, (position + 1) * rows)
            low = state.astype(BF)
            low_ref[part, :] = low
            state_ref[part, :] = state
            recur = dot_plain(low, h_ref[:, columns]) + bias_ref[1:2, columns]
            keep_ref[part, :] = recur[:, 2 * H :]
            reset, update, fresh, state = gru_cell(
                position < counts, gate_ref[part, :], recur, state
            )
            gate_ref[part, :H] = reset
            gate_ref[part, H : 2 * H] = update
            gate_ref[part, 2 * H :] = fresh
        grad = grad_ref[:, side * H : (side + 1) * H]
        gate_sum = jnp.zeros((1, three), F32)
        recur_sum = jnp.zeros((1, three), F32)
        for position in reversed(gru_order(side)):
            part = slice(position * rows, (position + 1) * rows)
            live = position < counts
            reset = gate_ref[part, :H]
            update = gate_ref[part, H : 2 * H]
            fresh = gate_ref[part, 2 * H :]
            moved = jnp.where(live, grad, 0.0)
            d_fresh = moved * (1.0 - update) * (1.0 - fresh * fresh)
            d_update = moved * (state_ref[part, :] - fresh) * update * (1.0 - update)
            d_reset = d_fresh * keep_ref[part, :] * reset * (1.0 - reset)
            d_gate = jnp.concatenate([d_reset, d_update, d_fresh], axis=-1).astype(BF)
            d_recur = jnp.concatenate([d_reset, d_update, d_fresh * reset], axis=-1).astype(BF)
            gates_out[position, :, columns] = d_gate
            recur_ref[part, :] = d_recur
            gate_sum += jnp.sum(d_gate.astype(F32), axis=0, keepdims=True)
            recur_sum += jnp.sum(d_recur.astype(F32), axis=0, keepdims=True)
            grad = jnp.where(live, moved * update, grad) + dot_right(d_recur, h_ref[:, columns])
        bias_out[0:1, columns] += gate_sum
        bias_out[1:2, columns] += recur_sum
        total_ref[:, columns] += dot_left(low_ref[...], recur_ref[...])

    @pl.when(pl.program_id(0) == pl.num_programs(0) - 1)
    def _():
        h_out[...] = total_ref[...].astype(BF)


def gru_backward(counts, chars, gru_x, gru_h, gru_bias, grad, high=256):
    rows, width = chars.shape[1:]
    three = 3 * H
    products = NCHAR * rows * (width + 3 * H) * 6 * H
    return pl.pallas_call(
        gru_backward_kernel,
        grid=(rows // high,),
        in_specs=gru_specs(high, width) + [pl.BlockSpec((high, 2 * H), lambda i: (i, 0))],
        out_specs=[
            pl.BlockSpec((NCHAR, high, 2 * three), lambda i: (0, i, 0)),
            pl.BlockSpec((H, 2 * three), lambda i: (0, 0)),
            pl.BlockSpec((2, 2 * three), lambda i: (0, 0)),
        ],
        out_shape=[
            jax.ShapeDtypeStruct((NCHAR, rows, 2 * three), BF),
            jax.ShapeDtypeStruct((H, 2 * three), BF),
            jax.ShapeDtypeStruct((2, 2 * three), F32),
        ],
        scratch_shapes=[
            pltpu.VMEM((NCHAR * high, three), F32),
            pltpu.VMEM((NCHAR * high, H), F32),
            pltpu.VMEM((NCHAR * high, H), F32),
            pltpu.VMEM((NCHAR * high, H), BF),
            pltpu.VMEM((NCHAR * high, three), BF),
            pltpu.VMEM((H, 2 * three), F32),
        ],
        cost_estimate=pl.CostEstimate(
            flops=2 * products, bytes_accessed=30_000_000, transcendentals=24 * rows * H
        ),
        name="gru_backward",
    )(counts, chars, gru_x, gru_h, gru_bias, grad)


def attention_forward_kernel(per, len_ref, qkv_ref, out_ref):
    block = pl.program_id(1)
    length = len_ref[pl.program_id(0)]
    span = per * HEAD
    total = qkv_ref.shape[0] * qkv_ref.shape[2]
    rows = qkv_ref.shape[2]
    q_all = qkv_ref[block, 0, :, :span] * BF(HEAD ** (-0.5))
    k_all = qkv_ref[:, 0, :, span : 2 * span].reshape(total, span)
    v_all = qkv_ref[:, 0, :, 2 * span :].reshape(total, span)
    valid = lax.broadcasted_iota(jnp.int32, (rows, total), 1) < length
    pieces = []
    for j in range(per):
        part = slice(j * HEAD, (j + 1) * HEAD)
        scores = jnp.where(valid, dot_right(q_all[:, part], k_all[:, part]), -1e30)
        raised = jnp.exp(scores - jnp.max(scores, axis=-1, keepdims=True))
        share = 1.0 / jnp.sum(raised, axis=-1, keepdims=True)
        probs = (raised * share).astype(BF)
        pieces.append(dot_plain(probs, v_all[:, part]))
    out_ref[0, 0] = jnp.concatenate(pieces, axis=-1).astype(BF)


def attention_forward(qkv, lengths, per):
    seqs, rows = qkv.shape[1], qkv.shape[2]
    parts = qkv.shape[0]
    span = per * HEAD
    return pl.pallas_call(
        partial(attention_forward_kernel, per),
        grid_spec=pltpu.PrefetchScalarGridSpec(
            num_scalar_prefetch=1,
            grid=(seqs, parts),
            in_specs=[pl.BlockSpec((parts, 1, rows, 3 * span), lambda m, b, n: (0, m, 0, 0))],
            out_specs=pl.BlockSpec((1, 1, rows, span), lambda m, b, n: (b, m, 0, 0)),
        ),
        out_shape=jax.ShapeDtypeStruct((parts, seqs, rows, span), BF),
        name="attend_forward",
    )(lengths, qkv)


def attention_backward_kernel(per, len_ref, qkv_ref, grad_ref, out_ref, key_acc, value_acc):
    block = pl.program_id(1)
    length = len_ref[pl.program_id(0)]
    span = per * HEAD
    parts, rows = qkv_ref.shape[0], qkv_ref.shape[2]
    total = parts * rows
    scale = HEAD ** (-0.5)

    @pl.when(block == 0)
    def _():
        key_acc[...] = jnp.zeros_like(key_acc)
        value_acc[...] = jnp.zeros_like(value_acc)

    q_all = qkv_ref[block, 0, :, :span] * BF(scale)
    g_all = grad_ref[block, 0]
    k_all = qkv_ref[:, 0, :, span : 2 * span].reshape(total, span)
    v_all = qkv_ref[:, 0, :, 2 * span :].reshape(total, span)
    valid = lax.broadcasted_iota(jnp.int32, (total, rows), 0) < length
    q_pieces, k_pieces, v_pieces = [], [], []
    for j in range(per):
        part = slice(j * HEAD, (j + 1) * HEAD)
        q, g, k, v = q_all[:, part], g_all[:, part], k_all[:, part], v_all[:, part]
        scores = jnp.where(valid, dot_right(k, q), -1e30)
        raised = jnp.exp(scores - jnp.max(scores, axis=0, keepdims=True))
        probs = raised * (1.0 / jnp.sum(raised, axis=0, keepdims=True))
        d_probs = dot_right(v, g)
        delta = jnp.sum(d_probs * probs, axis=0, keepdims=True)
        d_scores = (probs * (d_probs - delta)).astype(BF)
        q_pieces.append(dot_left(d_scores, k) * scale)
        k_pieces.append(dot_plain(d_scores, q))
        v_pieces.append(dot_plain(probs.astype(BF), g))
    out_ref[block, 0, :, :span] = jnp.concatenate(q_pieces, axis=-1).astype(BF)
    key_acc[...] += jnp.concatenate(k_pieces, axis=-1)
    value_acc[...] += jnp.concatenate(v_pieces, axis=-1)

    @pl.when(block == parts - 1)
    def _():
        out_ref[:, 0, :, span : 2 * span] = key_acc[...].astype(BF).reshape(parts, rows, span)
        out_ref[:, 0, :, 2 * span :] = value_acc[...].astype(BF).reshape(parts, rows, span)


def attention_backward(qkv, grads, lengths, per):
    parts, seqs, rows, _ = qkv.shape
    span = per * HEAD
    return pl.pallas_call(
        partial(attention_backward_kernel, per),
        grid_spec=pltpu.PrefetchScalarGridSpec(
            num_scalar_prefetch=1,
            grid=(seqs, parts),
            in_specs=[
                pl.BlockSpec((parts, 1, rows, 3 * span), lambda m, b, n: (0, m, 0, 0)),
                pl.BlockSpec((parts, 1, rows, span), lambda m, b, n: (0, m, 0, 0)),
            ],
            out_specs=pl.BlockSpec((parts, 1, rows, 3 * span), lambda m, b, n: (0, m, 0, 0)),
            scratch_shapes=[
                pltpu.VMEM((parts * rows, span), F32),
                pltpu.VMEM((parts * rows, span), F32),
            ],
        ),
        out_shape=jax.ShapeDtypeStruct(qkv.shape, BF),
        name="attend_backward",
    )(lengths, qkv, grads)


def exchange(blocks):
    return lax.all_to_all(blocks, "seq", split_axis=0, concat_axis=0)


def relocate_begin(pair, step):
    count = lax.axis_size("dp")
    levels = count.bit_length() - 1
    bits = (step, step if step == 0 else levels - step)
    others = []
    for value, bit in zip(pair, bits):
        apart = 1 << bit
        pairs = [(source, source ^ apart) for source in range(count)]
        others.append(lax.ppermute(value, "dp", pairs))
    return bits, tuple(others)


def relocate_end(masks, pair, begun):
    done = []
    for value, bit, other in zip(pair, *begun):
        moving = (jnp.bitwise_and(masks, 1 << bit) != 0)[:, None, None]
        done.append(jnp.where(moving, other, value))
    return tuple(done)


def relocate_one(masks, pair, step, tie):
    bits, others = relocate_begin(pair, step)
    others, pair, tie = lax.optimization_barrier((others, pair, tie))
    return relocate_end(masks, pair, (bits, others)), tie


def relocate_last(masks, pair, first, tie):
    levels = lax.axis_size("dp").bit_length() - 1
    for step in range(first, levels):
        bits, others = relocate_begin(pair, step)
        if step == levels - 1:
            others, pair, _ = lax.optimization_barrier((others, pair, tie))
        pair = relocate_end(masks, pair, (bits, others))
    return pair


def edges(block):
    count = lax.axis_size("seq")
    forward = [(i, i + 1) for i in range(count - 1)]
    backward = [(target, source) for source, target in forward]
    low = lax.ppermute(block[:, -1:], "seq", forward)
    high = lax.ppermute(block[:, :1], "seq", backward)
    return low, high


LINE = ([(0, 1), (3, 2)], [(1, 2), (2, 1)])


def line_sum(value, step):
    if lax.axis_size("seq") != 4:
        return lax.psum(value, "seq") if step == 0 else value
    other = lax.ppermute(value, "seq", LINE[step])
    return value + other


def line_back(value):
    if lax.axis_size("seq") != 4:
        return value
    other = lax.ppermute(value, "seq", [(1, 0), (2, 3)])
    return jnp.where((lax.axis_index("seq") % 3) == 0, other, value)


def shifted(block, low, high):
    before = jnp.concatenate([low, block[:, :-1]], axis=1)
    after = jnp.concatenate([block[:, 1:], high], axis=1)
    flat = (-1, block.shape[-1])
    return before.reshape(flat), block.reshape(flat), after.reshape(flat)


def sum_plan(shapes, high):
    spans, start = [], 0
    for rows, columns in shapes:
        tall = rows // high
        count = tall * (columns // WIDE)
        spans.append((start, start + count, tall))
        start += count
    return spans, start


def sum_kernel(spans, pre_spans, late, pre, high, lag, slots, *refs):
    whole = len(spans)
    count = whole + len(pre_spans)
    total = late + pre
    ins, outs = refs[:count], refs[count : 2 * count]
    own, rc, sc, s1a, s1b, r1a, r1b, r2a, r2b, s2, rz, sz, rm, tot, ready = refs[
        2 * count : 2 * count + 15
    ]
    sems = refs[2 * count + 15]
    credits = refs[2 * count + 16]
    half = WIDE // 2
    dp, z = lax.axis_index("dp"), lax.axis_index("seq")
    core, x, y = dp % 2, (dp // 2) % 2, dp // 4
    at_core = {"dp": dp + 1 - 2 * core}
    at_x = {"dp": dp + 2 - 4 * x}
    at_y = {"dp": dp + 4 - 8 * y}
    outer = (z % 3) == 0
    inner = (z % 3) != 0
    at_inner = {"seq": 1 + z // 3}
    at_middle = {"seq": (3 - z) % 4}
    at_outer = {"seq": (z // 2) * 3}

    barrier = pltpu.get_barrier_semaphore()

    def greet(where):
        pl.semaphore_signal(barrier, inc=1, device_id=where, device_id_type=pl.DeviceIdType.MESH)

    greet(at_core)
    greet(at_x)
    greet(at_y)

    @pl.when(outer)
    def _():
        greet(at_inner)
        pl.semaphore_wait(barrier, 4)

    @pl.when(inner)
    def _():
        greet(at_middle)
        greet(at_outer)
        pl.semaphore_wait(barrier, 5)

    def remote(source, target, name, slot, where):
        return pltpu.make_async_remote_copy(
            src_ref=source,
            dst_ref=target,
            send_sem=sems.at[2 * name, slot],
            recv_sem=sems.at[2 * name + 1, slot],
            device_id=where,
            device_id_type=pl.DeviceIdType.MESH,
        )

    CORE, X1, Y1, X2, Y2, OUTER, MIDDLE, FINAL, LOCAL, READY = range(10)

    def give_credit(name, k, where):
        @pl.when(k + slots < total)
        def _():
            pl.semaphore_signal(
                credits.at[name], inc=1, device_id=where, device_id_type=pl.DeviceIdType.MESH
            )

    def take_credit(name, k):
        @pl.when(k >= slots)
        def _():
            pl.semaphore_wait(credits.at[name], 1)

    def send_core(slot, source):
        return remote(source, rc.at[slot], CORE, slot, at_core)

    def send_x1(slot):
        return remote(sc.at[slot, :, 1 - x, :, :half], r1a.at[slot], X1, slot, at_x)

    def send_y1(slot):
        return remote(sc.at[slot, 1 - y, :, :, half:], r1b.at[slot], Y1, slot, at_y)

    def send_y2(slot):
        return remote(s1a.at[slot, 1 - y], r2a.at[slot], Y2, slot, at_y)

    def send_x2(slot):
        return remote(s1b.at[slot, 1 - x], r2b.at[slot], X2, slot, at_x)

    def send_outer(slot):
        return remote(s2.at[slot], rz.at[slot], OUTER, slot, at_inner)

    def send_middle(slot):
        return remote(sz.at[slot], rm.at[slot], MIDDLE, slot, at_middle)

    def send_final(slot, target):
        return remote(tot.at[slot], target, FINAL, slot, at_outer)

    def load(slot, source):
        return pltpu.make_async_copy(source, own.at[slot], sems.at[2 * LOCAL, slot])

    def load_ready(slot, source):
        return pltpu.make_async_copy(source, ready.at[slot], sems.at[2 * READY, slot])

    def save(slot, target):
        return pltpu.make_async_copy(tot.at[slot], target, sems.at[2 * LOCAL + 1, slot])

    def window(ref, j, tall):
        return pl.ds((j % tall) * high, high), pl.ds((j // tall) * WIDE, WIDE)

    def is_pre(k):
        return (k < 3 * pre) & (k % 3 == 2)

    def late_index(k):
        return jnp.where(k < 3 * pre, (k // 3) * 2 + k % 3, k - pre)

    def each(k, plan, parts, index, run):
        for (start, stop, tall), ref in zip(plan, parts):

            @pl.when((index >= start) & (index < stop))
            def _():
                run(ref, *window(ref, index - start, tall))

    def on_late(k, run):
        pl.when(jnp.logical_not(is_pre(k)))(run)

    def on_pre(k, run):
        pl.when(is_pre(k))(run)

    def add(left, right):
        return (left.astype(F32) + right.astype(F32)).astype(BF)

    def stage(k, run):
        @pl.when((k >= 0) & (k < total))
        def _():
            run(k, lax.rem(jnp.maximum(k, 0), slots))

    first = ins[0].at[:, core, pl.ds(0, high), pl.ds(0, WIDE)]
    final = outs[0].at[pl.ds(0, high), pl.ds(0, WIDE)]
    early = ins[whole].at[pl.ds(0, high), pl.ds(0, WIDE)]

    @pl.loop(0, total + 6 * lag)
    def _(t):
        def begin(k, slot):
            take_credit(CORE, k)

            def go():
                def run(ref, rows, columns):
                    send_core(slot, ref.at[:, 1 - core, rows, columns]).start()
                    load(slot, ref.at[:, core, rows, columns]).start()

                each(k, spans, ins[:whole], late_index(k), run)

            on_late(k, go)

        def add_core(k, slot):
            def go():
                load(slot, first).wait()
                send_core(slot, first).wait()
                both = add(own[slot], rc[slot])
                sc[slot] = both.reshape(2, 2, high, WIDE)

            on_late(k, go)
            give_credit(CORE, k, at_core)

        def add_one(k, slot):
            def go():
                send_x1(slot).wait()
                send_y1(slot).wait()
                s1a[slot] = add(sc[slot, :, x, :, :half], r1a[slot])
                s1b[slot] = add(sc[slot, y, :, :, half:], r1b[slot])

            on_late(k, go)
            give_credit(X1, k, at_x)
            give_credit(Y1, k, at_y)

        def add_two(k, slot):
            def go():
                send_y2(slot).wait()
                send_x2(slot).wait()
                s2[slot, :, :half] = add(s1a[slot, y], r2a[slot])
                s2[slot, :, half:] = add(s1b[slot, x], r2b[slot])

            def take():
                load_ready(slot, early).wait()
                s2[slot] = ready[slot]

            on_late(k, go)
            on_pre(k, take)
            give_credit(Y2, k, at_y)
            give_credit(X2, k, at_x)

        def add_outer(k, slot):
            @pl.when(outer)
            def _():
                send_outer(slot).wait_send()

            @pl.when(inner)
            def _():
                send_outer(slot).wait_recv()
                sz[slot] = add(s2[slot], rz[slot])
                give_credit(OUTER, k, at_outer)

        def add_middle(k, slot):
            @pl.when(inner)
            def _():
                send_middle(slot).wait()
                tot[slot] = add(sz[slot], rm[slot])
                give_credit(MIDDLE, k, at_middle)

        def finish(k, slot):
            @pl.when(inner)
            def _():
                save(slot, final).wait()
                send_final(slot, final).wait_send()

            @pl.when(outer)
            def _():
                send_final(slot, final).wait_recv()
                give_credit(FINAL, k, at_inner)

        def go_one(k, slot):
            take_credit(X1, k)
            take_credit(Y1, k)

            def go():
                send_x1(slot).start()
                send_y1(slot).start()

            on_late(k, go)

        def go_two(k, slot):
            take_credit(Y2, k)
            take_credit(X2, k)

            def go():
                send_y2(slot).start()
                send_x2(slot).start()

            def fetch():
                def run(ref, rows, columns):
                    load_ready(slot, ref.at[rows, columns]).start()

                each(k, pre_spans, ins[whole:], k // 3, run)

            on_late(k, go)
            on_pre(k, fetch)

        def go_outer(k, slot):
            @pl.when(outer)
            def _():
                take_credit(OUTER, k)
                send_outer(slot).start()

        def go_middle(k, slot):
            @pl.when(inner)
            def _():
                take_credit(MIDDLE, k)
                send_middle(slot).start()

        def go_final(k, slot):
            @pl.when(inner)
            def _():
                take_credit(FINAL, k)

                def run(ref, rows, columns):
                    save(slot, ref.at[rows, columns]).start()
                    send_final(slot, ref.at[rows, columns]).start()

                on_late(k, lambda: each(k, spans, outs[:whole], late_index(k), run))
                on_pre(k, lambda: each(k, pre_spans, outs[whole:], k // 3, run))

        stage(t, begin)
        stage(t - lag, add_core)
        stage(t - 2 * lag, add_one)
        stage(t - 3 * lag, add_two)
        stage(t - 4 * lag, add_outer)
        stage(t - 5 * lag, add_middle)
        stage(t - lag, go_one)
        stage(t - 2 * lag, go_two)
        stage(t - 3 * lag, go_outer)
        stage(t - 4 * lag, go_middle)
        stage(t - 5 * lag, go_final)
        stage(t - 6 * lag, finish)


def sum_grads(grads, pres, high=48, lag=3, slots=6):
    shapes = [(grad.shape[0] // 8, grad.shape[1]) for grad in grads]
    pre_shapes = [grad.shape for grad in pres]
    spans, late = sum_plan(shapes, high)
    pre_spans, pre = sum_plan(pre_shapes, high)
    half = WIDE // 2
    anywhere = pl.BlockSpec(memory_space=pl.ANY)
    blocks = [grad.reshape(4, 2, grad.shape[0] // 8, grad.shape[1]) for grad in grads]
    shapes = shapes + pre_shapes
    return pl.pallas_call(
        partial(sum_kernel, spans, pre_spans, late, pre, high, lag, slots),
        in_specs=[anywhere] * len(shapes),
        out_specs=[anywhere] * len(shapes),
        out_shape=[jax.ShapeDtypeStruct(shape, BF) for shape in shapes],
        scratch_shapes=[
            pltpu.VMEM((slots, 4, high, WIDE), BF),
            pltpu.VMEM((slots, 4, high, WIDE), BF),
            pltpu.VMEM((slots, 2, 2, high, WIDE), BF),
            pltpu.VMEM((slots, 2, high, half), BF),
            pltpu.VMEM((slots, 2, high, half), BF),
            pltpu.VMEM((slots, 2, high, half), BF),
            pltpu.VMEM((slots, 2, high, half), BF),
            pltpu.VMEM((slots, high, half), BF),
            pltpu.VMEM((slots, high, half), BF),
            pltpu.VMEM((slots, high, WIDE), BF),
            pltpu.VMEM((slots, high, WIDE), BF),
            pltpu.VMEM((slots, high, WIDE), BF),
            pltpu.VMEM((slots, high, WIDE), BF),
            pltpu.VMEM((slots, high, WIDE), BF),
            pltpu.VMEM((slots, high, WIDE), BF),
            pltpu.SemaphoreType.DMA((20, slots)),
            pltpu.SemaphoreType.REGULAR((8,)),
        ],
        compiler_params=pltpu.CompilerParams(collective_id=1, has_side_effects=True),
        name="sum_grads",
    )(*blocks, *pres)


def heads_first(weight, parts):
    rows = weight.shape[0]
    split = weight.reshape(rows, 3, parts, WIDE // parts)
    return split.transpose(0, 2, 1, 3).reshape(rows, 3 * WIDE)


def heads_last(weight, parts):
    rows = weight.shape[0]
    split = weight.reshape(rows, parts, 3, WIDE // parts)
    return split.transpose(0, 2, 1, 3).reshape(rows, 3 * WIDE)


def flat_small(small):
    return jnp.concatenate([piece.T.reshape(-1) for piece in small])


def gather_packed(weights, small, wide):
    return unpack(pack(weights, small, wide), weights, small, wide)


def pack(weights, small, wide):
    pieces = []
    for weight in weights:
        low = weight.astype(BF)
        pieces += [low[:, start : start + wide] for start in range(0, low.shape[1], wide)]
    flat = flat_small(small).astype(BF)
    high = -(-flat.size // wide)
    high = -(-high // 8) * 8
    pieces.append(jnp.pad(flat, (0, high * wide - flat.size)).reshape(high, wide))
    return lax.all_gather(jnp.concatenate(pieces, axis=0), "dp", axis=0)


def unpack(full, weights, small, wide):
    groups = full.shape[0]
    outs, at = [], 0
    for weight in weights:
        rows, columns = weight.shape
        blocks = columns // wide
        part = full[:, at : at + blocks * rows].reshape(groups, blocks, rows, wide)
        outs.append(part.transpose(0, 2, 1, 3).reshape(groups * rows, columns))
        at += blocks * rows
    used = -(-sum(piece.size for piece in small) // wide)
    table = full[:, at : at + used].astype(F32).reshape(groups, -1)
    vectors, at = [], 0
    for piece in small:
        part = table[:, at : at + piece.size]
        if piece.ndim == 2:
            rows, columns = piece.shape
            part = part.reshape(groups, columns, rows).transpose(1, 0, 2)
            vectors.append(part.reshape(columns, groups * rows))
        else:
            vectors.append(part.reshape(-1))
        at += piece.size
    return outs, vectors


def pack_small(small, groups, multiple):
    pieces = []
    for piece in small:
        columns = piece if isinstance(piece, list) else [piece]
        pieces += [column.reshape(groups, -1) for column in columns]
    flat = jnp.concatenate(pieces, axis=1)
    high = -(-flat.shape[1] // WIDE)
    high = -(-high // multiple) * multiple
    flat = jnp.pad(flat.astype(BF), ((0, 0), (0, high * WIDE - flat.shape[1])))
    return flat.reshape(groups * high, WIDE)


def sum_grads_plain(grads, pres):
    outs = [lax.psum_scatter(grad, "dp", scatter_dimension=0, tiled=True) for grad in grads]
    return [lax.psum(part, "seq") for part in outs + list(pres)]


def reduce_grads(big, pres, small):
    groups = lax.axis_size("dp")
    ours = groups == 8 and lax.axis_size("seq") == 4
    grads = [grad.astype(BF) for grad in big] + [pack_small(small, groups, 48)]
    outs = sum_grads(grads, pres) if ours else sum_grads_plain(grads, pres)
    tail = outs[len(big)]
    sizes = []
    for piece in small:
        columns = piece if isinstance(piece, list) else [piece]
        sizes.append((len(columns), columns[0].size // groups, isinstance(piece, list)))
    used = -(-sum(many * size for many, size, _ in sizes) // WIDE)
    tail = tail[:used].astype(F32).reshape(-1)
    vectors, at = [], 0
    for many, size, matrix in sizes:
        part = tail[at : at + many * size]
        vectors.append(part.reshape(many, size).T if matrix else part)
        at += many * size
    bigs = [piece.astype(F32) for piece in outs[: len(big)]]
    early = [piece.astype(F32) for piece in outs[len(big) + 1 :]]
    return bigs, early, vectors


def scatter_sum(grad):
    return lax.psum_scatter(grad.astype(BF), "dp", scatter_dimension=0, tiled=True)


def body(
    tokens,
    chars,
    char_counts,
    lengths,
    perm,
    token_cot,
    char_cot,
    w_qkv,
    b_qv,
    w_out,
    w_in,
    b_in,
    w_back,
    gru_x,
    gru_h,
    gru_bias,
    blend_w,
    conv_w,
    conv_b,
    norm_gain,
    norm_bias,
    row_bias,
):
    parts = lax.axis_size("seq")
    seqs, local, width = tokens.shape
    rows = seqs * local
    per = width // HEAD // parts
    three = 3 * H
    masks = perm[:, 0]
    place = lax.axis_index("dp")
    own_lengths = lax.dynamic_slice(lengths, (place * seqs,), (seqs,))
    first = (heads_first(w_qkv, parts), gru_x, gru_h)
    (w_qkv, gru_x, gru_h), (b_qv, gru_bias) = gather_packed(first, (b_qv, gru_bias), 3 * width)
    middle = (w_out, w_in, w_back, blend_w)
    small = (b_in, conv_b, norm_gain, norm_bias, row_bias)
    packed = pack(middle, small, width)
    conv_w = lax.all_gather(conv_w.astype(BF), "dp", axis=0, tiled=True)

    flat_tokens = tokens.reshape(rows, width)
    counts = char_counts.reshape(rows, 1)
    row_chars = chars.transpose(2, 0, 1, 3).reshape(NCHAR, rows, width)
    flat_chars = row_chars.reshape(NCHAR * rows, width)
    bias = jnp.concatenate([b_qv[:width], jnp.zeros((width,), F32), b_qv[width:]])
    bias = heads_first(bias[None], parts)[0]
    project = (dot_plain(flat_tokens, w_qkv) + bias).astype(BF)
    cots = (token_cot, char_cot)
    cots, project = relocate_one(masks, cots, 0, project)
    project, row_chars = lax.optimization_barrier((project, row_chars))
    span = 3 * per * HEAD
    qkv = project.reshape(seqs, local, parts, span).transpose(2, 0, 1, 3)
    qkv = exchange(qkv)
    char_state = gru_forward(counts, row_chars, gru_x, gru_h, gru_bias)
    qkv, char_state = lax.optimization_barrier((qkv, char_state))
    context = attention_forward(qkv, own_lengths, per)
    context, packed = lax.optimization_barrier((context, packed))
    middle, small = unpack(packed, middle, small, width)
    w_out, w_in, w_back, blend_w = middle
    b_in, conv_b, norm_gain, norm_bias, row_bias = small
    context = exchange(context)
    context = context.transpose(1, 2, 0, 3).reshape(rows, width)

    cots, context = relocate_one(masks, cots, 1, context)
    summed_first = flat_tokens.astype(F32) + dot_plain(context, w_out) + row_bias[0]
    hidden1 = norm_rows(summed_first, norm_gain[0], norm_bias[0])
    hidden1_low = hidden1.astype(BF)
    inner = dot_plain(hidden1_low, w_in) + b_in
    activated, inner_slope = gelu_both(inner)
    activated, inner_slope = lax.optimization_barrier((activated.astype(BF), inner_slope))
    summed_second = hidden1 + dot_plain(activated, w_back) + row_bias[1]
    hidden2 = norm_rows(summed_second, norm_gain[1], norm_bias[1])
    hidden2_low = hidden2.astype(BF)
    char_low = char_state.astype(BF)
    token_side = dot_plain(hidden2_low, blend_w[:, :width]) + row_bias[2]
    char_side = dot_plain(char_low, blend_w[:, width:]) + row_bias[3]
    joined = jnp.concatenate([token_side, char_side], axis=-1).astype(BF)
    joined = joined.reshape(seqs, local, 2 * width)
    cots, joined = lax.optimization_barrier((cots, joined))
    taps = shifted(joined, *edges(joined))
    stacked = jnp.concatenate(taps, axis=-1)
    mixed = dot_plain(stacked, conv_w) + conv_b
    lifted, mixed_slope = lax.optimization_barrier(gelu_both(mixed))
    token_pre = hidden2 + lifted[:, :width]
    char_pre = char_state + lifted[:, width:]
    token_out = norm_rows(token_pre, norm_gain[2], norm_bias[2]).astype(BF)
    char_out = norm_rows(char_pre, norm_gain[3], norm_bias[3]).astype(BF)
    outs = (token_out.reshape(seqs, local, width), char_out.reshape(seqs, local, width))
    cots = relocate_last(masks, cots, 2, (token_out, char_out))

    token_cots, char_cots = (part.reshape(rows, width).astype(F32) for part in cots)
    d_token_pre, gain_token, shift_token = norm_back(
        token_pre, norm_gain[2], token_cots
    )
    d_char_pre, gain_char, shift_char = norm_back(char_pre, norm_gain[3], char_cots)
    d_mixed = jnp.concatenate([d_token_pre, d_char_pre], axis=-1) * mixed_slope
    d_mixed = d_mixed.astype(BF)
    grad_conv = dot_left(stacked, d_mixed).astype(BF)
    grad_conv, d_mixed = lax.optimization_barrier((grad_conv, d_mixed))
    sum_conv = scatter_sum(grad_conv)
    outs, d_mixed = relocate_one(masks, outs, 0, d_mixed)
    beside = d_mixed.reshape(seqs, local, 2 * width)
    before, same, after = shifted(beside, *edges(beside))
    taps_w = conv_w.reshape(3, 2 * width, 2 * width)
    d_joined = dot_right(after, taps_w[0]) + dot_right(same, taps_w[1])
    d_joined = (d_joined + dot_right(before, taps_w[2])).astype(BF)
    d_token_side = d_joined[:, :width]
    d_char_side = d_joined[:, width:]
    grad_blend = jnp.concatenate(
        [dot_left(hidden2_low, d_token_side), dot_left(char_low, d_char_side)], axis=-1
    )
    grad_blend, d_token_side, d_char_side = lax.optimization_barrier(
        (grad_blend.astype(BF), d_token_side, d_char_side)
    )
    sum_blend = scatter_sum(grad_blend)
    d_hidden2 = d_token_pre + dot_right(d_token_side, blend_w[:, :width])
    d_char_state = d_char_pre + dot_right(d_char_side, blend_w[:, width:])

    d_second, gain_second, shift_second = norm_back(summed_second, norm_gain[1], d_hidden2)
    d_branch = d_second.astype(BF)
    grad_back = dot_left(activated, d_branch).astype(BF)
    grad_back, d_branch = lax.optimization_barrier((grad_back, d_branch))
    sum_back = scatter_sum(grad_back)
    d_inner = (dot_right(d_branch, w_back) * inner_slope).astype(BF)
    grad_in = dot_left(hidden1_low, d_inner)
    d_hidden1 = d_second + dot_right(d_inner, w_in)
    d_first, gain_first, shift_first = norm_back(summed_first, norm_gain[0], d_hidden1)
    d_attend = d_first.astype(BF)
    outs, d_attend = relocate_one(masks, outs, 1, d_attend)
    grad_out = dot_left(context, d_attend)
    d_context = dot_right(d_attend, w_out).astype(BF)
    d_context = d_context.reshape(seqs, local, parts, per * HEAD).transpose(2, 0, 1, 3)
    d_project = attention_backward(qkv, exchange(d_context), own_lengths, per)
    sum_conv, d_char_state, d_project = lax.optimization_barrier((sum_conv, d_char_state, d_project))
    sum_conv = line_sum(sum_conv, 0)
    d_project = exchange(d_project)

    d_gates, grad_gru_h, grad_gru_bias = gru_backward(
        counts, row_chars, gru_x, gru_h, gru_bias, d_char_state
    )
    sum_conv, d_gates = lax.optimization_barrier((sum_conv, d_gates))
    sum_conv = line_sum(sum_conv, 1)
    d_gates = d_gates.reshape(NCHAR * rows, 2 * three)
    grad_gru_x = dot_left(flat_chars, d_gates)
    chars_back = dot_right(d_gates, gru_x).astype(BF)
    chars_back, d_project = lax.optimization_barrier((chars_back, d_project))
    chars_back = chars_back.reshape(NCHAR, seqs, local, width).transpose(1, 2, 0, 3)
    d_project = d_project.transpose(1, 2, 0, 3).reshape(rows, 3 * width)

    grad_qkv = dot_left(flat_tokens, d_project)
    sums = heads_last(column_sum(d_project)[None], parts)[0]
    grad_b_qv = jnp.concatenate([sums[:width], sums[2 * width :]])
    tokens_back = (d_first + dot_right(d_project, w_qkv)).astype(BF)
    big = (grad_in, grad_qkv, grad_gru_x, grad_gru_h, grad_out)
    small = (
        grad_b_qv,
        column_sum(d_inner),
        [grad_gru_bias[0], grad_gru_bias[1]],
        column_sum(d_mixed),
        [gain_first, gain_second, gain_token, gain_char],
        [shift_first, shift_second, shift_token, shift_char],
        [
            column_sum(d_attend),
            column_sum(d_branch),
            column_sum(d_token_side),
            column_sum(d_char_side),
        ],
    )
    big, early, small = reduce_grads(big, (sum_back, sum_blend), small)
    outs, big[-1] = lax.optimization_barrier((outs, big[-1]))
    outs = relocate_last(masks, outs, 2, big[-1])
    g_in, g_qkv, g_gru_x, g_gru_h, g_out = big
    g_back, g_blend = early
    g_conv = line_back(sum_conv).astype(F32)
    g_b_qv, g_b_in, g_gru_bias, g_conv_b, g_gain, g_shift, g_rows = small
    return (
        outs[0],
        outs[1],
        tokens_back.reshape(seqs, local, width),
        chars_back,
        heads_last(g_qkv, parts),
        g_b_qv,
        g_out,
        g_in,
        g_b_in,
        g_back,
        g_gru_x,
        g_gru_h,
        g_gru_bias,
        g_blend,
        g_conv,
        g_conv_b,
        g_gain,
        g_shift,
        g_rows,
    )


def solution(mesh):
    rows, vector, seq = P("dp", None), P("dp"), P("dp", "seq", None)
    weights = (
        rows,
        vector,
        rows,
        rows,
        vector,
        rows,
        rows,
        rows,
        rows,
        rows,
        rows,
        vector,
        rows,
        rows,
        rows,
    )
    return jax.shard_map(
        body,
        mesh=mesh,
        in_specs=(seq, P("dp", "seq", None, None), P("dp", "seq"), P(), P(), seq, seq) + weights,
        out_specs=(seq, seq, seq, P("dp", "seq", None, None)) + weights,
        check_vma=False,
    )
```

```python
from functools import partial

import jax
import jax.numpy as jnp
from jax import lax
from jax.experimental import pallas as pl
from jax.experimental.pallas import tpu as pltpu
from jax.sharding import PartitionSpec as P

HEAD = 64
H = 384
NCHAR = 4
WIDE = 768
BF = jnp.bfloat16
F32 = jnp.float32


def dot_plain(left, right):
    return jnp.dot(left, right, preferred_element_type=F32)


def dot_left(left, right):
    return lax.dot_general(left, right, (((0,), (0,)), ((), ())), preferred_element_type=F32)


def dot_right(left, right):
    return lax.dot_general(left, right, (((1,), (1,)), ((), ())), preferred_element_type=F32)


def column_sum(values):
    return jnp.sum(values.astype(F32), axis=0)


def norm_rows(values, gain, shift):
    center = values - jnp.mean(values, axis=-1, keepdims=True)
    spread = jnp.mean(center * center, axis=-1, keepdims=True)
    rstd = lax.rsqrt(spread + 1e-06)
    return center * rstd * gain + shift


def norm_back(values, gain, grad):
    center = values - jnp.mean(values, axis=-1, keepdims=True)
    spread = jnp.mean(center * center, axis=-1, keepdims=True)
    rstd = lax.rsqrt(spread + 1e-06)
    hat = center * rstd
    lead = grad * gain
    back = rstd * (
        lead
        - jnp.mean(lead, axis=-1, keepdims=True)
        - hat * jnp.mean(lead * hat, axis=-1, keepdims=True)
    )
    return back, jnp.sum(grad * hat, axis=0), jnp.sum(grad, axis=0)


def gelu_both(values):
    cdf = 0.5 * (1.0 + lax.erf(values * (0.5**0.5)))
    pdf = jnp.exp(-0.5 * values * values) * 0.3989422804014327
    return values * cdf, cdf + values * pdf


def gru_order(side):
    return range(NCHAR) if side == 0 else range(NCHAR - 1, -1, -1)


def gru_cell(live, gates, recur, state):
    width = state.shape[-1]
    reset = jax.nn.sigmoid(gates[:, :width] + recur[:, :width])
    update = jax.nn.sigmoid(gates[:, width : 2 * width] + recur[:, width : 2 * width])
    fresh = jnp.tanh(gates[:, 2 * width :] + reset * recur[:, 2 * width :])
    after = jnp.where(live, (1.0 - update) * fresh + update * state, state)
    return reset, update, fresh, after


def gru_forward_kernel(count_ref, chars_ref, x_ref, h_ref, bias_ref, out_ref, gate_ref):
    rows = chars_ref.shape[1]
    three = 3 * H
    counts = jnp.broadcast_to(count_ref[...], (rows, H))
    chars = chars_ref[...].reshape(NCHAR * rows, chars_ref.shape[2])
    for side in range(2):
        columns = slice(side * three, (side + 1) * three)
        gate_ref[...] = dot_plain(chars, x_ref[:, columns]) + bias_ref[0:1, columns]
        state = jnp.zeros((rows, H), F32)
        for position in gru_order(side):
            recur = dot_plain(state.astype(BF), h_ref[:, columns]) + bias_ref[1:2, columns]
            gates = gate_ref[position * rows : (position + 1) * rows, :]
            state = gru_cell(position < counts, gates, recur, state)[3]
        out_ref[:, side * H : (side + 1) * H] = state


def gru_specs(high, width):
    three = 3 * H
    return [
        pl.BlockSpec((high, 1), lambda i: (i, 0)),
        pl.BlockSpec((NCHAR, high, width), lambda i: (0, i, 0)),
        pl.BlockSpec((width, 2 * three), lambda i: (0, 0)),
        pl.BlockSpec((H, 2 * three), lambda i: (0, 0)),
        pl.BlockSpec((2, 2 * three), lambda i: (0, 0)),
    ]


def gru_forward(counts, chars, gru_x, gru_h, gru_bias, high=256):
    rows, width = chars.shape[1:]
    products = NCHAR * rows * (width + H) * 6 * H
    return pl.pallas_call(
        gru_forward_kernel,
        grid=(rows // high,),
        in_specs=gru_specs(high, width),
        out_specs=pl.BlockSpec((high, 2 * H), lambda i: (i, 0)),
        out_shape=jax.ShapeDtypeStruct((rows, 2 * H), F32),
        scratch_shapes=[pltpu.VMEM((NCHAR * high, 3 * H), F32)],
        cost_estimate=pl.CostEstimate(
            flops=2 * products, bytes_accessed=10_000_000, transcendentals=24 * rows * H
        ),
        name="gru_forward",
    )(counts, chars, gru_x, gru_h, gru_bias)


def gru_backward_kernel(
    count_ref,
    chars_ref,
    x_ref,
    h_ref,
    bias_ref,
    grad_ref,
    gates_out,
    h_out,
    bias_out,
    gate_ref,
    keep_ref,
    state_ref,
    low_ref,
    recur_ref,
    total_ref,
):
    rows = chars_ref.shape[1]
    three = 3 * H
    counts = jnp.broadcast_to(count_ref[...], (rows, H))
    chars = chars_ref[...].reshape(NCHAR * rows, chars_ref.shape[2])

    @pl.when(pl.program_id(0) == 0)
    def _():
        bias_out[...] = jnp.zeros_like(bias_out)
        total_ref[...] = jnp.zeros_like(total_ref)

    for side in range(2):
        columns = slice(side * three, (side + 1) * three)
        gate_ref[...] = dot_plain(chars, x_ref[:, columns]) + bias_ref[0:1, columns]
        state = jnp.zeros((rows, H), F32)
        for position in gru_order(side):
            part = slice(position * rows, (position + 1) * rows)
            low = state.astype(BF)
            low_ref[part, :] = low
            state_ref[part, :] = state
            recur = dot_plain(low, h_ref[:, columns]) + bias_ref[1:2, columns]
            keep_ref[part, :] = recur[:, 2 * H :]
            reset, update, fresh, state = gru_cell(
                position < counts, gate_ref[part, :], recur, state
            )
            gate_ref[part, :H] = reset
            gate_ref[part, H : 2 * H] = update
            gate_ref[part, 2 * H :] = fresh
        grad = grad_ref[:, side * H : (side + 1) * H]
        gate_sum = jnp.zeros((1, three), F32)
        recur_sum = jnp.zeros((1, three), F32)
        for position in reversed(gru_order(side)):
            part = slice(position * rows, (position + 1) * rows)
            live = position < counts
            reset = gate_ref[part, :H]
            update = gate_ref[part, H : 2 * H]
            fresh = gate_ref[part, 2 * H :]
            moved = jnp.where(live, grad, 0.0)
            d_fresh = moved * (1.0 - update) * (1.0 - fresh * fresh)
            d_update = moved * (state_ref[part, :] - fresh) * update * (1.0 - update)
            d_reset = d_fresh * keep_ref[part, :] * reset * (1.0 - reset)
            d_gate = jnp.concatenate([d_reset, d_update, d_fresh], axis=-1).astype(BF)
            d_recur = jnp.concatenate([d_reset, d_update, d_fresh * reset], axis=-1).astype(BF)
            gates_out[position, :, columns] = d_gate
            recur_ref[part, :] = d_recur
            gate_sum += jnp.sum(d_gate.astype(F32), axis=0, keepdims=True)
            recur_sum += jnp.sum(d_recur.astype(F32), axis=0, keepdims=True)
            grad = jnp.where(live, moved * update, grad) + dot_right(d_recur, h_ref[:, columns])
        bias_out[0:1, columns] += gate_sum
        bias_out[1:2, columns] += recur_sum
        total_ref[:, columns] += dot_left(low_ref[...], recur_ref[...])

    @pl.when(pl.program_id(0) == pl.num_programs(0) - 1)
    def _():
        h_out[...] = total_ref[...].astype(BF)


def gru_backward(counts, chars, gru_x, gru_h, gru_bias, grad, high=256):
    rows, width = chars.shape[1:]
    three = 3 * H
    products = NCHAR * rows * (width + 3 * H) * 6 * H
    return pl.pallas_call(
        gru_backward_kernel,
        grid=(rows // high,),
        in_specs=gru_specs(high, width) + [pl.BlockSpec((high, 2 * H), lambda i: (i, 0))],
        out_specs=[
            pl.BlockSpec((NCHAR, high, 2 * three), lambda i: (0, i, 0)),
            pl.BlockSpec((H, 2 * three), lambda i: (0, 0)),
            pl.BlockSpec((2, 2 * three), lambda i: (0, 0)),
        ],
        out_shape=[
            jax.ShapeDtypeStruct((NCHAR, rows, 2 * three), BF),
            jax.ShapeDtypeStruct((H, 2 * three), BF),
            jax.ShapeDtypeStruct((2, 2 * three), F32),
        ],
        scratch_shapes=[
            pltpu.VMEM((NCHAR * high, three), F32),
            pltpu.VMEM((NCHAR * high, H), F32),
            pltpu.VMEM((NCHAR * high, H), F32),
            pltpu.VMEM((NCHAR * high, H), BF),
            pltpu.VMEM((NCHAR * high, three), BF),
            pltpu.VMEM((H, 2 * three), F32),
        ],
        cost_estimate=pl.CostEstimate(
            flops=2 * products, bytes_accessed=30_000_000, transcendentals=24 * rows * H
        ),
        name="gru_backward",
    )(counts, chars, gru_x, gru_h, gru_bias, grad)


def attention_forward_kernel(per, len_ref, qkv_ref, out_ref):
    block = pl.program_id(1)
    length = len_ref[pl.program_id(0)]
    span = per * HEAD
    total = qkv_ref.shape[0] * qkv_ref.shape[2]
    rows = qkv_ref.shape[2]
    q_all = qkv_ref[block, 0, :, :span] * BF(HEAD ** (-0.5))
    k_all = qkv_ref[:, 0, :, span : 2 * span].reshape(total, span)
    v_all = qkv_ref[:, 0, :, 2 * span :].reshape(total, span)
    valid = lax.broadcasted_iota(jnp.int32, (rows, total), 1) < length
    pieces = []
    for j in range(per):
        part = slice(j * HEAD, (j + 1) * HEAD)
        scores = jnp.where(valid, dot_right(q_all[:, part], k_all[:, part]), -1e30)
        raised = jnp.exp(scores - jnp.max(scores, axis=-1, keepdims=True))
        share = 1.0 / jnp.sum(raised, axis=-1, keepdims=True)
        probs = (raised * share).astype(BF)
        pieces.append(dot_plain(probs, v_all[:, part]))
    out_ref[0, 0] = jnp.concatenate(pieces, axis=-1).astype(BF)


def attention_forward(qkv, lengths, per):
    seqs, rows = qkv.shape[1], qkv.shape[2]
    parts = qkv.shape[0]
    span = per * HEAD
    return pl.pallas_call(
        partial(attention_forward_kernel, per),
        grid_spec=pltpu.PrefetchScalarGridSpec(
            num_scalar_prefetch=1,
            grid=(seqs, parts),
            in_specs=[pl.BlockSpec((parts, 1, rows, 3 * span), lambda m, b, n: (0, m, 0, 0))],
            out_specs=pl.BlockSpec((1, 1, rows, span), lambda m, b, n: (b, m, 0, 0)),
        ),
        out_shape=jax.ShapeDtypeStruct((parts, seqs, rows, span), BF),
        name="attend_forward",
    )(lengths, qkv)


def attention_backward_kernel(per, len_ref, qkv_ref, grad_ref, out_ref, key_acc, value_acc):
    block = pl.program_id(1)
    length = len_ref[pl.program_id(0)]
    span = per * HEAD
    parts, rows = qkv_ref.shape[0], qkv_ref.shape[2]
    total = parts * rows
    scale = HEAD ** (-0.5)

    @pl.when(block == 0)
    def _():
        key_acc[...] = jnp.zeros_like(key_acc)
        value_acc[...] = jnp.zeros_like(value_acc)

    q_all = qkv_ref[block, 0, :, :span] * BF(scale)
    g_all = grad_ref[block, 0]
    k_all = qkv_ref[:, 0, :, span : 2 * span].reshape(total, span)
    v_all = qkv_ref[:, 0, :, 2 * span :].reshape(total, span)
    valid = lax.broadcasted_iota(jnp.int32, (total, rows), 0) < length
    q_pieces, k_pieces, v_pieces = [], [], []
    for j in range(per):
        part = slice(j * HEAD, (j + 1) * HEAD)
        q, g, k, v = q_all[:, part], g_all[:, part], k_all[:, part], v_all[:, part]
        scores = jnp.where(valid, dot_right(k, q), -1e30)
        raised = jnp.exp(scores - jnp.max(scores, axis=0, keepdims=True))
        probs = raised * (1.0 / jnp.sum(raised, axis=0, keepdims=True))
        d_probs = dot_right(v, g)
        delta = jnp.sum(d_probs * probs, axis=0, keepdims=True)
        d_scores = (probs * (d_probs - delta)).astype(BF)
        q_pieces.append(dot_left(d_scores, k) * scale)
        k_pieces.append(dot_plain(d_scores, q))
        v_pieces.append(dot_plain(probs.astype(BF), g))
    out_ref[block, 0, :, :span] = jnp.concatenate(q_pieces, axis=-1).astype(BF)
    key_acc[...] += jnp.concatenate(k_pieces, axis=-1)
    value_acc[...] += jnp.concatenate(v_pieces, axis=-1)

    @pl.when(block == parts - 1)
    def _():
        out_ref[:, 0, :, span : 2 * span] = key_acc[...].astype(BF).reshape(parts, rows, span)
        out_ref[:, 0, :, 2 * span :] = value_acc[...].astype(BF).reshape(parts, rows, span)


def attention_backward(qkv, grads, lengths, per):
    parts, seqs, rows, _ = qkv.shape
    span = per * HEAD
    return pl.pallas_call(
        partial(attention_backward_kernel, per),
        grid_spec=pltpu.PrefetchScalarGridSpec(
            num_scalar_prefetch=1,
            grid=(seqs, parts),
            in_specs=[
                pl.BlockSpec((parts, 1, rows, 3 * span), lambda m, b, n: (0, m, 0, 0)),
                pl.BlockSpec((parts, 1, rows, span), lambda m, b, n: (0, m, 0, 0)),
            ],
            out_specs=pl.BlockSpec((parts, 1, rows, 3 * span), lambda m, b, n: (0, m, 0, 0)),
            scratch_shapes=[
                pltpu.VMEM((parts * rows, span), F32),
                pltpu.VMEM((parts * rows, span), F32),
            ],
        ),
        out_shape=jax.ShapeDtypeStruct(qkv.shape, BF),
        name="attend_backward",
    )(lengths, qkv, grads)


def exchange(blocks):
    return lax.all_to_all(blocks, "seq", split_axis=0, concat_axis=0)


def relocate_begin(pair, step):
    count = lax.axis_size("dp")
    levels = count.bit_length() - 1
    bits = (step, step if step == 0 else levels - step)
    others = []
    for value, bit in zip(pair, bits):
        apart = 1 << bit
        pairs = [(source, source ^ apart) for source in range(count)]
        others.append(lax.ppermute(value, "dp", pairs))
    return bits, tuple(others)


def relocate_end(masks, pair, begun):
    done = []
    for value, bit, other in zip(pair, *begun):
        moving = (jnp.bitwise_and(masks, 1 << bit) != 0)[:, None, None]
        done.append(jnp.where(moving, other, value))
    return tuple(done)


def relocate_one(masks, pair, step, tie):
    bits, others = relocate_begin(pair, step)
    others, pair, tie = lax.optimization_barrier((others, pair, tie))
    return relocate_end(masks, pair, (bits, others)), tie


def relocate_last(masks, pair, first, tie):
    levels = lax.axis_size("dp").bit_length() - 1
    for step in range(first, levels):
        bits, others = relocate_begin(pair, step)
        if step == levels - 1:
            others, pair, _ = lax.optimization_barrier((others, pair, tie))
        pair = relocate_end(masks, pair, (bits, others))
    return pair


def edges(block):
    count = lax.axis_size("seq")
    forward = [(i, i + 1) for i in range(count - 1)]
    backward = [(target, source) for source, target in forward]
    low = lax.ppermute(block[:, -1:], "seq", forward)
    high = lax.ppermute(block[:, :1], "seq", backward)
    return low, high


LINE = ([(0, 1), (3, 2)], [(1, 2), (2, 1)])


def line_sum(value, step):
    if lax.axis_size("seq") != 4:
        return lax.psum(value, "seq") if step == 0 else value
    other = lax.ppermute(value, "seq", LINE[step])
    return value + other


def line_back(value):
    if lax.axis_size("seq") != 4:
        return value
    other = lax.ppermute(value, "seq", [(1, 0), (2, 3)])
    return jnp.where((lax.axis_index("seq") % 3) == 0, other, value)


def shifted(block, low, high):
    before = jnp.concatenate([low, block[:, :-1]], axis=1)
    after = jnp.concatenate([block[:, 1:], high], axis=1)
    flat = (-1, block.shape[-1])
    return before.reshape(flat), block.reshape(flat), after.reshape(flat)


def sum_plan(shapes, high):
    spans, start = [], 0
    for rows, columns in shapes:
        tall = rows // high
        count = tall * (columns // WIDE)
        spans.append((start, start + count, tall))
        start += count
    return spans, start


def sum_kernel(spans, pre_spans, late, pre, high, lag, slots, *refs):
    whole = len(spans)
    count = whole + len(pre_spans)
    total = late + pre
    ins, outs = refs[:count], refs[count : 2 * count]
    own, rc, sc, s1a, s1b, r1a, r1b, r2a, r2b, s2, rz, sz, rm, tot, ready = refs[
        2 * count : 2 * count + 15
    ]
    sems = refs[2 * count + 15]
    credits = refs[2 * count + 16]
    half = WIDE // 2
    dp, z = lax.axis_index("dp"), lax.axis_index("seq")
    core, x, y = dp % 2, (dp // 2) % 2, dp // 4
    at_core = {"dp": dp + 1 - 2 * core}
    at_x = {"dp": dp + 2 - 4 * x}
    at_y = {"dp": dp + 4 - 8 * y}
    outer = (z % 3) == 0
    inner = (z % 3) != 0
    at_inner = {"seq": 1 + z // 3}
    at_middle = {"seq": (3 - z) % 4}
    at_outer = {"seq": (z // 2) * 3}

    barrier = pltpu.get_barrier_semaphore()

    def greet(where):
        pl.semaphore_signal(barrier, inc=1, device_id=where, device_id_type=pl.DeviceIdType.MESH)

    greet(at_core)
    greet(at_x)
    greet(at_y)

    @pl.when(outer)
    def _():
        greet(at_inner)
        pl.semaphore_wait(barrier, 4)

    @pl.when(inner)
    def _():
        greet(at_middle)
        greet(at_outer)
        pl.semaphore_wait(barrier, 5)

    def remote(source, target, name, slot, where):
        return pltpu.make_async_remote_copy(
            src_ref=source,
            dst_ref=target,
            send_sem=sems.at[2 * name, slot],
            recv_sem=sems.at[2 * name + 1, slot],
            device_id=where,
            device_id_type=pl.DeviceIdType.MESH,
        )

    CORE, X1, Y1, X2, Y2, OUTER, MIDDLE, FINAL, LOCAL, READY = range(10)

    def give_credit(name, k, where):
        @pl.when(k + slots < total)
        def _():
            pl.semaphore_signal(
                credits.at[name], inc=1, device_id=where, device_id_type=pl.DeviceIdType.MESH
            )

    def take_credit(name, k):
        @pl.when(k >= slots)
        def _():
            pl.semaphore_wait(credits.at[name], 1)

    def send_core(slot, source):
        return remote(source, rc.at[slot], CORE, slot, at_core)

    def send_x1(slot):
        return remote(sc.at[slot, :, 1 - x, :, :half], r1a.at[slot], X1, slot, at_x)

    def send_y1(slot):
        return remote(sc.at[slot, 1 - y, :, :, half:], r1b.at[slot], Y1, slot, at_y)

    def send_y2(slot):
        return remote(s1a.at[slot, 1 - y], r2a.at[slot], Y2, slot, at_y)

    def send_x2(slot):
        return remote(s1b.at[slot, 1 - x], r2b.at[slot], X2, slot, at_x)

    def send_outer(slot):
        return remote(s2.at[slot], rz.at[slot], OUTER, slot, at_inner)

    def send_middle(slot):
        return remote(sz.at[slot], rm.at[slot], MIDDLE, slot, at_middle)

    def send_final(slot, target):
        return remote(tot.at[slot], target, FINAL, slot, at_outer)

    def load(slot, source):
        return pltpu.make_async_copy(source, own.at[slot], sems.at[2 * LOCAL, slot])

    def load_ready(slot, source):
        return pltpu.make_async_copy(source, ready.at[slot], sems.at[2 * READY, slot])

    def save(slot, target):
        return pltpu.make_async_copy(tot.at[slot], target, sems.at[2 * LOCAL + 1, slot])

    def window(ref, j, tall):
        return pl.ds((j % tall) * high, high), pl.ds((j // tall) * WIDE, WIDE)

    def is_pre(k):
        return (k < 3 * pre) & (k % 3 == 2)

    def late_index(k):
        return jnp.where(k < 3 * pre, (k // 3) * 2 + k % 3, k - pre)

    def each(k, plan, parts, index, run):
        for (start, stop, tall), ref in zip(plan, parts):

            @pl.when((index >= start) & (index < stop))
            def _():
                run(ref, *window(ref, index - start, tall))

    def on_late(k, run):
        pl.when(jnp.logical_not(is_pre(k)))(run)

    def on_pre(k, run):
        pl.when(is_pre(k))(run)

    def add(left, right):
        return (left.astype(F32) + right.astype(F32)).astype(BF)

    def stage(k, run):
        @pl.when((k >= 0) & (k < total))
        def _():
            run(k, lax.rem(jnp.maximum(k, 0), slots))

    first = ins[0].at[:, core, pl.ds(0, high), pl.ds(0, WIDE)]
    final = outs[0].at[pl.ds(0, high), pl.ds(0, WIDE)]
    early = ins[whole].at[pl.ds(0, high), pl.ds(0, WIDE)]

    @pl.loop(0, total + 6 * lag)
    def _(t):
        def begin(k, slot):
            take_credit(CORE, k)

            def go():
                def run(ref, rows, columns):
                    send_core(slot, ref.at[:, 1 - core, rows, columns]).start()
                    load(slot, ref.at[:, core, rows, columns]).start()

                each(k, spans, ins[:whole], late_index(k), run)

            on_late(k, go)

        def add_core(k, slot):
            def go():
                load(slot, first).wait()
                send_core(slot, first).wait()
                both = add(own[slot], rc[slot])
                sc[slot] = both.reshape(2, 2, high, WIDE)

            on_late(k, go)
            give_credit(CORE, k, at_core)

        def add_one(k, slot):
            def go():
                send_x1(slot).wait()
                send_y1(slot).wait()
                s1a[slot] = add(sc[slot, :, x, :, :half], r1a[slot])
                s1b[slot] = add(sc[slot, y, :, :, half:], r1b[slot])

            on_late(k, go)
            give_credit(X1, k, at_x)
            give_credit(Y1, k, at_y)

        def add_two(k, slot):
            def go():
                send_y2(slot).wait()
                send_x2(slot).wait()
                s2[slot, :, :half] = add(s1a[slot, y], r2a[slot])
                s2[slot, :, half:] = add(s1b[slot, x], r2b[slot])

            def take():
                load_ready(slot, early).wait()
                s2[slot] = ready[slot]

            on_late(k, go)
            on_pre(k, take)
            give_credit(Y2, k, at_y)
            give_credit(X2, k, at_x)

        def add_outer(k, slot):
            @pl.when(outer)
            def _():
                send_outer(slot).wait_send()

            @pl.when(inner)
            def _():
                send_outer(slot).wait_recv()
                sz[slot] = add(s2[slot], rz[slot])
                give_credit(OUTER, k, at_outer)

        def add_middle(k, slot):
            @pl.when(inner)
            def _():
                send_middle(slot).wait()
                tot[slot] = add(sz[slot], rm[slot])
                give_credit(MIDDLE, k, at_middle)

        def finish(k, slot):
            @pl.when(inner)
            def _():
                save(slot, final).wait()
                send_final(slot, final).wait_send()

            @pl.when(outer)
            def _():
                send_final(slot, final).wait_recv()
                give_credit(FINAL, k, at_inner)

        def go_one(k, slot):
            take_credit(X1, k)
            take_credit(Y1, k)

            def go():
                send_x1(slot).start()
                send_y1(slot).start()

            on_late(k, go)

        def go_two(k, slot):
            take_credit(Y2, k)
            take_credit(X2, k)

            def go():
                send_y2(slot).start()
                send_x2(slot).start()

            def fetch():
                def run(ref, rows, columns):
                    load_ready(slot, ref.at[rows, columns]).start()

                each(k, pre_spans, ins[whole:], k // 3, run)

            on_late(k, go)
            on_pre(k, fetch)

        def go_outer(k, slot):
            @pl.when(outer)
            def _():
                take_credit(OUTER, k)
                send_outer(slot).start()

        def go_middle(k, slot):
            @pl.when(inner)
            def _():
                take_credit(MIDDLE, k)
                send_middle(slot).start()

        def go_final(k, slot):
            @pl.when(inner)
            def _():
                take_credit(FINAL, k)

                def run(ref, rows, columns):
                    save(slot, ref.at[rows, columns]).start()
                    send_final(slot, ref.at[rows, columns]).start()

                on_late(k, lambda: each(k, spans, outs[:whole], late_index(k), run))
                on_pre(k, lambda: each(k, pre_spans, outs[whole:], k // 3, run))

        stage(t, begin)
        stage(t - lag, add_core)
        stage(t - 2 * lag, add_one)
        stage(t - 3 * lag, add_two)
        stage(t - 4 * lag, add_outer)
        stage(t - 5 * lag, add_middle)
        stage(t - lag, go_one)
        stage(t - 2 * lag, go_two)
        stage(t - 3 * lag, go_outer)
        stage(t - 4 * lag, go_middle)
        stage(t - 5 * lag, go_final)
        stage(t - 6 * lag, finish)


def sum_grads(grads, pres, high=48, lag=3, slots=6):
    shapes = [(grad.shape[0] // 8, grad.shape[1]) for grad in grads]
    pre_shapes = [grad.shape for grad in pres]
    spans, late = sum_plan(shapes, high)
    pre_spans, pre = sum_plan(pre_shapes, high)
    half = WIDE // 2
    anywhere = pl.BlockSpec(memory_space=pl.ANY)
    blocks = [grad.reshape(4, 2, grad.shape[0] // 8, grad.shape[1]) for grad in grads]
    shapes = shapes + pre_shapes
    return pl.pallas_call(
        partial(sum_kernel, spans, pre_spans, late, pre, high, lag, slots),
        in_specs=[anywhere] * len(shapes),
        out_specs=[anywhere] * len(shapes),
        out_shape=[jax.ShapeDtypeStruct(shape, BF) for shape in shapes],
        scratch_shapes=[
            pltpu.VMEM((slots, 4, high, WIDE), BF),
            pltpu.VMEM((slots, 4, high, WIDE), BF),
            pltpu.VMEM((slots, 2, 2, high, WIDE), BF),
            pltpu.VMEM((slots, 2, high, half), BF),
            pltpu.VMEM((slots, 2, high, half), BF),
            pltpu.VMEM((slots, 2, high, half), BF),
            pltpu.VMEM((slots, 2, high, half), BF),
            pltpu.VMEM((slots, high, half), BF),
            pltpu.VMEM((slots, high, half), BF),
            pltpu.VMEM((slots, high, WIDE), BF),
            pltpu.VMEM((slots, high, WIDE), BF),
            pltpu.VMEM((slots, high, WIDE), BF),
            pltpu.VMEM((slots, high, WIDE), BF),
            pltpu.VMEM((slots, high, WIDE), BF),
            pltpu.VMEM((slots, high, WIDE), BF),
            pltpu.SemaphoreType.DMA((20, slots)),
            pltpu.SemaphoreType.REGULAR((8,)),
        ],
        compiler_params=pltpu.CompilerParams(collective_id=1, has_side_effects=True),
        name="sum_grads",
    )(*blocks, *pres)


def heads_first(weight, parts):
    rows = weight.shape[0]
    split = weight.reshape(rows, 3, parts, WIDE // parts)
    return split.transpose(0, 2, 1, 3).reshape(rows, 3 * WIDE)


def heads_last(weight, parts):
    rows = weight.shape[0]
    split = weight.reshape(rows, parts, 3, WIDE // parts)
    return split.transpose(0, 2, 1, 3).reshape(rows, 3 * WIDE)


def flat_small(small):
    return jnp.concatenate([piece.T.reshape(-1) for piece in small])


def pack(weights, small, wide):
    pieces = []
    for weight in weights:
        low = weight.astype(BF)
        pieces += [low[:, start : start + wide] for start in range(0, low.shape[1], wide)]
    flat = flat_small(small).astype(BF)
    high = -(-flat.size // wide)
    high = -(-high // 8) * 8
    pieces.append(jnp.pad(flat, (0, high * wide - flat.size)).reshape(high, wide))
    return lax.all_gather(jnp.concatenate(pieces, axis=0), "dp", axis=0)


def unpack(full, weights, small, wide):
    groups = full.shape[0]
    outs, at = [], 0
    for weight in weights:
        rows, columns = weight.shape
        blocks = columns // wide
        part = full[:, at : at + blocks * rows].reshape(groups, blocks, rows, wide)
        outs.append(part.transpose(0, 2, 1, 3).reshape(groups * rows, columns))
        at += blocks * rows
    used = -(-sum(piece.size for piece in small) // wide)
    table = full[:, at : at + used].astype(F32).reshape(groups, -1)
    vectors, at = [], 0
    for piece in small:
        part = table[:, at : at + piece.size]
        if piece.ndim == 2:
            rows, columns = piece.shape
            part = part.reshape(groups, columns, rows).transpose(1, 0, 2)
            vectors.append(part.reshape(columns, groups * rows))
        else:
            vectors.append(part.reshape(-1))
        at += piece.size
    return outs, vectors


def pack_small(small, groups, multiple):
    pieces = []
    for piece in small:
        columns = piece if isinstance(piece, list) else [piece]
        pieces += [column.reshape(groups, -1) for column in columns]
    flat = jnp.concatenate(pieces, axis=1)
    high = -(-flat.shape[1] // WIDE)
    high = -(-high // multiple) * multiple
    flat = jnp.pad(flat.astype(BF), ((0, 0), (0, high * WIDE - flat.shape[1])))
    return flat.reshape(groups * high, WIDE)


def sum_grads_plain(grads, pres):
    outs = [lax.psum_scatter(grad, "dp", scatter_dimension=0, tiled=True) for grad in grads]
    return [lax.psum(part, "seq") for part in outs + list(pres)]


def reduce_grads(big, pres, small):
    groups = lax.axis_size("dp")
    ours = groups == 8 and lax.axis_size("seq") == 4
    grads = [grad.astype(BF) for grad in big] + [pack_small(small, groups, 48)]
    outs = sum_grads(grads, pres) if ours else sum_grads_plain(grads, pres)
    tail = outs[len(big)]
    sizes = []
    for piece in small:
        columns = piece if isinstance(piece, list) else [piece]
        sizes.append((len(columns), columns[0].size // groups, isinstance(piece, list)))
    used = -(-sum(many * size for many, size, _ in sizes) // WIDE)
    tail = tail[:used].astype(F32).reshape(-1)
    vectors, at = [], 0
    for many, size, matrix in sizes:
        part = tail[at : at + many * size]
        vectors.append(part.reshape(many, size).T if matrix else part)
        at += many * size
    bigs = [piece.astype(F32) for piece in outs[: len(big)]]
    early = [piece.astype(F32) for piece in outs[len(big) + 1 :]]
    return bigs, early, vectors


def scatter_sum(grad):
    return lax.psum_scatter(grad.astype(BF), "dp", scatter_dimension=0, tiled=True)


def body(
    tokens,
    chars,
    char_counts,
    lengths,
    perm,
    token_cot,
    char_cot,
    w_qkv,
    b_qv,
    w_out,
    w_in,
    b_in,
    w_back,
    gru_x,
    gru_h,
    gru_bias,
    blend_w,
    conv_w,
    conv_b,
    norm_gain,
    norm_bias,
    row_bias,
):
    parts = lax.axis_size("seq")
    seqs, local, width = tokens.shape
    rows = seqs * local
    per = width // HEAD // parts
    three = 3 * H
    masks = perm[:, 0]
    place = lax.axis_index("dp")
    own_lengths = lax.dynamic_slice(lengths, (place * seqs,), (seqs,))
    first = (heads_first(w_qkv, parts), gru_x, gru_h)
    first_small = (b_qv, gru_bias)
    first_packed = pack(first, first_small, 3 * width)
    (w_qkv, _, _), (b_qv, _) = unpack(first_packed, first, first_small, 3 * width)
    middle = (w_out, w_in, w_back, blend_w)
    small = (b_in, conv_b, norm_gain, norm_bias, row_bias)
    packed = pack(middle, small, width)
    conv_w = lax.all_gather(conv_w.astype(BF), "dp", axis=0, tiled=True)

    flat_tokens = tokens.reshape(rows, width)
    counts = char_counts.reshape(rows, 1)
    row_chars = chars.transpose(2, 0, 1, 3).reshape(NCHAR, rows, width)
    flat_chars = row_chars.reshape(NCHAR * rows, width)
    bias = jnp.concatenate([b_qv[:width], jnp.zeros((width,), F32), b_qv[width:]])
    bias = heads_first(bias[None], parts)[0]
    project = (dot_plain(flat_tokens, w_qkv) + bias).astype(BF)
    cots = (token_cot, char_cot)
    cots, project = relocate_one(masks, cots, 0, project)
    project, row_chars, first_packed = lax.optimization_barrier((project, row_chars, first_packed))
    (_, gru_x, gru_h), (_, gru_bias) = unpack(first_packed, first, first_small, 3 * width)
    span = 3 * per * HEAD
    qkv = project.reshape(seqs, local, parts, span).transpose(2, 0, 1, 3)
    qkv = exchange(qkv)
    char_state = gru_forward(counts, row_chars, gru_x, gru_h, gru_bias)
    qkv, char_state = lax.optimization_barrier((qkv, char_state))
    context = attention_forward(qkv, own_lengths, per)
    context, packed = lax.optimization_barrier((context, packed))
    middle, small = unpack(packed, middle, small, width)
    w_out, w_in, w_back, blend_w = middle
    b_in, conv_b, norm_gain, norm_bias, row_bias = small
    context = exchange(context)
    context = context.transpose(1, 2, 0, 3).reshape(rows, width)

    cots, context = relocate_one(masks, cots, 1, context)
    summed_first = flat_tokens.astype(F32) + dot_plain(context, w_out) + row_bias[0]
    hidden1 = norm_rows(summed_first, norm_gain[0], norm_bias[0])
    hidden1_low = hidden1.astype(BF)
    inner = dot_plain(hidden1_low, w_in) + b_in
    activated, inner_slope = gelu_both(inner)
    activated, inner_slope = lax.optimization_barrier((activated.astype(BF), inner_slope))
    summed_second = hidden1 + dot_plain(activated, w_back) + row_bias[1]
    hidden2 = norm_rows(summed_second, norm_gain[1], norm_bias[1])
    hidden2_low = hidden2.astype(BF)
    char_low = char_state.astype(BF)
    token_side = dot_plain(hidden2_low, blend_w[:, :width]) + row_bias[2]
    char_side = dot_plain(char_low, blend_w[:, width:]) + row_bias[3]
    joined = jnp.concatenate([token_side, char_side], axis=-1).astype(BF)
    joined = joined.reshape(seqs, local, 2 * width)
    cots, joined = lax.optimization_barrier((cots, joined))
    taps = shifted(joined, *edges(joined))
    stacked = jnp.concatenate(taps, axis=-1)
    mixed = dot_plain(stacked, conv_w) + conv_b
    lifted, mixed_slope = lax.optimization_barrier(gelu_both(mixed))
    token_pre = hidden2 + lifted[:, :width]
    char_pre = char_state + lifted[:, width:]
    token_out = norm_rows(token_pre, norm_gain[2], norm_bias[2]).astype(BF)
    char_out = norm_rows(char_pre, norm_gain[3], norm_bias[3]).astype(BF)
    outs = (token_out.reshape(seqs, local, width), char_out.reshape(seqs, local, width))
    cots = relocate_last(masks, cots, 2, (token_out, char_out))

    token_cots, char_cots = (part.reshape(rows, width).astype(F32) for part in cots)
    d_token_pre, gain_token, shift_token = norm_back(
        token_pre, norm_gain[2], token_cots
    )
    d_char_pre, gain_char, shift_char = norm_back(char_pre, norm_gain[3], char_cots)
    d_mixed = jnp.concatenate([d_token_pre, d_char_pre], axis=-1) * mixed_slope
    d_mixed = d_mixed.astype(BF)
    grad_conv = dot_left(stacked, d_mixed).astype(BF)
    grad_conv, d_mixed = lax.optimization_barrier((grad_conv, d_mixed))
    sum_conv = scatter_sum(grad_conv)
    outs, d_mixed = relocate_one(masks, outs, 0, d_mixed)
    beside = d_mixed.reshape(seqs, local, 2 * width)
    before, same, after = shifted(beside, *edges(beside))
    taps_w = conv_w.reshape(3, 2 * width, 2 * width)
    d_joined = dot_right(after, taps_w[0]) + dot_right(same, taps_w[1])
    d_joined = (d_joined + dot_right(before, taps_w[2])).astype(BF)
    d_token_side = d_joined[:, :width]
    d_char_side = d_joined[:, width:]
    grad_blend = jnp.concatenate(
        [dot_left(hidden2_low, d_token_side), dot_left(char_low, d_char_side)], axis=-1
    )
    grad_blend, d_token_side, d_char_side = lax.optimization_barrier(
        (grad_blend.astype(BF), d_token_side, d_char_side)
    )
    sum_blend = scatter_sum(grad_blend)
    d_hidden2 = d_token_pre + dot_right(d_token_side, blend_w[:, :width])
    d_char_state = d_char_pre + dot_right(d_char_side, blend_w[:, width:])

    d_second, gain_second, shift_second = norm_back(summed_second, norm_gain[1], d_hidden2)
    d_branch = d_second.astype(BF)
    grad_back = dot_left(activated, d_branch).astype(BF)
    grad_back, d_branch = lax.optimization_barrier((grad_back, d_branch))
    sum_back = scatter_sum(grad_back)
    d_inner = (dot_right(d_branch, w_back) * inner_slope).astype(BF)
    grad_in = dot_left(hidden1_low, d_inner)
    d_hidden1 = d_second + dot_right(d_inner, w_in)
    d_first, gain_first, shift_first = norm_back(summed_first, norm_gain[0], d_hidden1)
    d_attend = d_first.astype(BF)
    outs, d_attend = relocate_one(masks, outs, 1, d_attend)
    grad_out = dot_left(context, d_attend)
    d_context = dot_right(d_attend, w_out).astype(BF)
    d_context = d_context.reshape(seqs, local, parts, per * HEAD).transpose(2, 0, 1, 3)
    d_project = attention_backward(qkv, exchange(d_context), own_lengths, per)
    sum_conv, d_char_state, d_project = lax.optimization_barrier((sum_conv, d_char_state, d_project))
    sum_conv = line_sum(sum_conv, 0)
    d_project = exchange(d_project)

    d_gates, grad_gru_h, grad_gru_bias = gru_backward(
        counts, row_chars, gru_x, gru_h, gru_bias, d_char_state
    )
    sum_conv, d_gates = lax.optimization_barrier((sum_conv, d_gates))
    sum_conv = line_sum(sum_conv, 1)
    d_gates = d_gates.reshape(NCHAR * rows, 2 * three)
    grad_gru_x = dot_left(flat_chars, d_gates)
    chars_back = dot_right(d_gates, gru_x).astype(BF)
    chars_back, d_project = lax.optimization_barrier((chars_back, d_project))
    chars_back = chars_back.reshape(NCHAR, seqs, local, width).transpose(1, 2, 0, 3)
    d_project = d_project.transpose(1, 2, 0, 3).reshape(rows, 3 * width)

    grad_qkv = dot_left(flat_tokens, d_project)
    sums = heads_last(column_sum(d_project)[None], parts)[0]
    grad_b_qv = jnp.concatenate([sums[:width], sums[2 * width :]])
    tokens_back = (d_first + dot_right(d_project, w_qkv)).astype(BF)
    big = (grad_in, grad_qkv, grad_gru_x, grad_gru_h, grad_out)
    small = (
        grad_b_qv,
        column_sum(d_inner),
        [grad_gru_bias[0], grad_gru_bias[1]],
        column_sum(d_mixed),
        [gain_first, gain_second, gain_token, gain_char],
        [shift_first, shift_second, shift_token, shift_char],
        [
            column_sum(d_attend),
            column_sum(d_branch),
            column_sum(d_token_side),
            column_sum(d_char_side),
        ],
    )
    big, early, small = reduce_grads(big, (sum_back, sum_blend), small)
    outs, big[-1] = lax.optimization_barrier((outs, big[-1]))
    outs = relocate_last(masks, outs, 2, big[-1])
    g_in, g_qkv, g_gru_x, g_gru_h, g_out = big
    g_back, g_blend = early
    g_conv = line_back(sum_conv).astype(F32)
    g_b_qv, g_b_in, g_gru_bias, g_conv_b, g_gain, g_shift, g_rows = small
    return (
        outs[0],
        outs[1],
        tokens_back.reshape(seqs, local, width),
        chars_back,
        heads_last(g_qkv, parts),
        g_b_qv,
        g_out,
        g_in,
        g_b_in,
        g_back,
        g_gru_x,
        g_gru_h,
        g_gru_bias,
        g_blend,
        g_conv,
        g_conv_b,
        g_gain,
        g_shift,
        g_rows,
    )


def solution(mesh):
    rows, vector, seq = P("dp", None), P("dp"), P("dp", "seq", None)
    weights = (
        rows,
        vector,
        rows,
        rows,
        vector,
        rows,
        rows,
        rows,
        rows,
        rows,
        rows,
        vector,
        rows,
        rows,
        rows,
    )
    return jax.shard_map(
        body,
        mesh=mesh,
        in_specs=(seq, P("dp", "seq", None, None), P("dp", "seq"), P(), P(), seq, seq) + weights,
        out_specs=(seq, seq, seq, P("dp", "seq", None, None)) + weights,
        check_vma=False,
    )
```
